128 devices in a mesh: req: 32 (over y, z, core), mp: 4 (over x).
Axes of the slice: x: 4, y: 4, z: 4, core: 2. Of those that a mesh axis runs over, the one named last changes fastest.
Arguments:
- hidden_in: bfloat16 [16384, 2048], P(('req', 'mp')), may hold values from -48 to 48
- segment_ids: int32 [32, 512], replicated, may hold values from 0 to 2, never falling along the last dimension, each value on 1 to 256 neighbouring positions
- request_prompt: int32 [1024], P('req'), may hold values from 0 to 95, as said below
- page_table: int32 [1024, 16], P('req'), may hold values from 0 to 511, as said below
- ln_attn: bfloat16 [2048], replicated, may hold values from 0.5 to 1.5
- w_query: bfloat16 [2048, 2048], P(None, 'mp'), may hold values from -0.125 to 0.125
- w_key: bfloat16 [2048, 1024], P(None, 'mp'), may hold values from -0.125 to 0.125
- w_value: bfloat16 [2048, 1024], P(None, 'mp'), may hold values from -0.125 to 0.125
- q_gain: bfloat16 [128], replicated, may hold values from 0.5 to 1.5
- k_gain: bfloat16 [128], replicated, may hold values from 0.5 to 1.5
- w_out: bfloat16 [2048, 2048], P('mp'), may hold values from -0.125 to 0.125
- ln_mlp: bfloat16 [2048], replicated, may hold values from 0.5 to 1.5
- w_gate: bfloat16 [2048, 3072], P(None, 'mp'), may hold values from -0.125 to 0.125
- w_up: bfloat16 [2048, 3072], P(None, 'mp'), may hold values from -0.125 to 0.125
- w_down: bfloat16 [3072, 2048], P('mp'), may hold values from -0.109375 to 0.109375
Outputs:
- layer_out: bfloat16 [16384, 2048], P(('req', 'mp'))
- kv_pages: bfloat16 [16384, 16, 8, 256], P('req', None, 'mp')
The draws below stay inside these ranges and needn't reach their ends.
Inputs may be any that keep to these rules, and one draw needn't show every extreme that they name: `request_prompt`: every prompt is continued by 8 to 16 requests, and some prompt by exactly 16. `page_table`: the 32 rows of one index of req name each of the 512 pages once.
All inputs are finite; a program needn't handle non-finite values.
Results may differ from the reference program's by a relative error of at most 0.0075.
Values may be sent and summed in bfloat16 or wider, within the bound.
A program may use at most 128 MiB of HBM per device.

```python
import math
import jax
import jax.numpy as jnp
import numpy as np
from jax import lax

D = 2048
H = 16
KVH = 8
HD = 128
FF = 3072
SEQ_ROWS = 512
PROMPTS_DEV = 3
REQ_DEV = 32
PAGE = 16
PROMPT_MAX = 256
MAXP = 16
PAGES_DEV = 512
TOKENS = 16384
PROMPTS = 96
REQS = 1024
N_REQ = 32


def draw_hidden_in(key, part):
    base_key, row_key, column_key = jax.random.split(key, 3)
    row_scale = jnp.exp(jax.random.uniform(row_key, (TOKENS, 1), jnp.float32, jnp.log(0.4), jnp.log(4.0)))
    column_scale = jnp.exp(jax.random.uniform(column_key, (1, D), jnp.float32, jnp.log(0.3), jnp.log(3.0)))
    base = jax.random.normal(base_key, (TOKENS, D), jnp.float32)
    base = jnp.clip(base, -4.0, 4.0)
    return (base * row_scale * column_scale).astype(jnp.bfloat16)


def draw_request_prompt(key, part):
    spread_key, label_key, order_key = jax.random.split(key, 3)
    base = jnp.repeat(jnp.arange(PROMPTS, dtype=jnp.int32), 8)
    others = jax.random.permutation(spread_key, jnp.repeat(jnp.arange(1, PROMPTS, dtype=jnp.int32), 8))
    extra = jnp.concatenate([jnp.zeros((8,), jnp.int32), others])[:REQS - 8 * PROMPTS]
    relabel = jax.random.permutation(label_key, PROMPTS).astype(jnp.int32)
    every = relabel[jnp.concatenate([base, extra])]
    return jax.random.permutation(order_key, every).astype(jnp.int32)


def draw_page_table(key, part):
    keys = jax.random.split(key, REQS // REQ_DEV)
    tables = jax.vmap(lambda single: jax.random.permutation(single, PAGES_DEV))(keys)
    return tables.astype(jnp.int32).reshape(REQS, MAXP)


def levels(key, shape, shards, low, top_value):
    def one(dim, parts):
        steps = jax.random.uniform(jax.random.fold_in(jax.random.fold_in(key, 6), dim), (parts,), jnp.float32, low / len(shards), top_value / len(shards))
        return jnp.repeat(jnp.exp(steps), shape[dim] // parts).reshape((-1,) + (1,) * (len(shape) - dim - 1))

    level = one(*shards[0])
    for cut in shards[1:]:
        level = level * one(*cut)
    return level


def length_profile(number_of, total, limit, skew):
    loads = [(1 << 20) // math.isqrt(rank ** skew) + 1 for rank in range(2, number_of + 1)]
    rest, given = total - limit - (number_of - 1), [1] * (number_of - 1)
    while rest > 0:
        candidates = [i for i in range(number_of - 1) if given[i] < limit]
        whole, remaining = sum([loads[i] for i in candidates]), rest
        for i in candidates:
            more = min(limit - given[i], max(1, remaining * loads[i] // whole), rest)
            given[i] = given[i] + more
            rest = rest - more
    return np.array([limit] + given)


def ragged_sizes(rng, amount, total, most, lean):
    if amount == 2:
        one = jax.random.randint(rng, (), max(1, total - most), min(most, total - 1) + 1)
        return jnp.stack([one, total - one])
    sizes = jnp.asarray(length_profile(amount, total, most, lean), jnp.int32)
    pairs = (amount - 1) // 2
    giver, taker = sizes[1:1 + 2 * pairs:2], sizes[2:2 + 2 * pairs:2]
    slack = jnp.minimum(giver - 1, most - taker)
    shifted = jax.random.randint(jax.random.fold_in(rng, 1), (pairs,), 0, 1 << 20) % (slack + 1)
    sizes = sizes.at[1:1 + 2 * pairs:2].set(giver - shifted).at[2:2 + 2 * pairs:2].set(taker + shifted)
    return sizes[jax.random.permutation(jax.random.fold_in(rng, 2), amount)]


def normal_values(key, shape, deviation, reach, pieces=(), held_as=jnp.bfloat16):
    entries = deviation * jax.random.normal(key, shape, jnp.float32)
    if pieces:
        entries = entries * levels(key, shape, pieces, -0.22, 0.18)
    return jnp.clip(entries, -reach, reach).astype(held_as)


def setup_inputs(seed: int = 0) -> dict:
    key_list = jax.random.split(jax.random.key(seed), 16)
    return {
        "hidden_in": draw_hidden_in(jax.random.fold_in(key_list[15], 71), 0),
        "segment_ids": jax.vmap(lambda own: jnp.searchsorted(jnp.cumsum(ragged_sizes(own, PROMPTS_DEV, SEQ_ROWS, PROMPT_MAX, 1)), jnp.arange(SEQ_ROWS), side="right"))(jax.random.split(key_list[1], N_REQ)).reshape((N_REQ, SEQ_ROWS)).astype(jnp.int32),
        "request_prompt": draw_request_prompt(jax.random.fold_in(key_list[15], 71), 0),
        "page_table": draw_page_table(jax.random.fold_in(key_list[15], 71), 0),
        "ln_attn": jnp.clip(1.0 + 0.1 * jax.random.normal(key_list[4], (D,), jnp.float32), 0.5, 1.5).astype(jnp.bfloat16),
        "w_query": normal_values(key_list[5], (D, H * HD), D ** -0.5, 0.125, ((1, 4),)),
        "w_key": normal_values(key_list[6], (D, KVH * HD), D ** -0.5, 0.125, ((1, 4),)),
        "w_value": normal_values(key_list[7], (D, KVH * HD), D ** -0.5, 0.125, ((1, 4),)),
        "q_gain": jnp.clip(1.0 + 0.1 * jax.random.normal(key_list[8], (HD,), jnp.float32), 0.5, 1.5).astype(jnp.bfloat16),
        "k_gain": jnp.clip(1.0 + 0.1 * jax.random.normal(key_list[9], (HD,), jnp.float32), 0.5, 1.5).astype(jnp.bfloat16),
        "w_out": normal_values(key_list[10], (H * HD, D), (H * HD) ** -0.5, 0.125, ((0, 4),)),
        "ln_mlp": jnp.clip(1.0 + 0.1 * jax.random.normal(key_list[11], (D,), jnp.float32), 0.5, 1.5).astype(jnp.bfloat16),
        "w_gate": normal_values(key_list[12], (D, FF), D ** -0.5, 0.125, ((1, 4),)),
        "w_up": normal_values(key_list[13], (D, FF), D ** -0.5, 0.125, ((1, 4),)),
        "w_down": normal_values(key_list[14], (FF, D), FF ** -0.5, 0.109375, ((0, 4),)),
    }


EPS = 1e-06
THETA = 1000000.0

def rms_scale(values, gain):
    wide = values.astype(jnp.float32)
    return wide * lax.rsqrt(lax.optimization_barrier(jnp.mean(wide * wide, axis=-1, keepdims=True)) + EPS) * gain.astype(jnp.float32)

def segment_table(segment_row):
    member = (segment_row[:, None] == jnp.arange(PROMPTS_DEV, dtype=jnp.int32)[None, :]).astype(jnp.int32)
    lengths = lax.optimization_barrier(jnp.sum(member, axis=0)).astype(jnp.int32)
    starts = (jnp.cumsum(lengths) - lengths).astype(jnp.int32)
    index = jnp.arange(segment_row.shape[0], dtype=jnp.int32)
    position = (index - lax.optimization_barrier(jnp.sum(member * starts[None, :], axis=1))).astype(jnp.int32)
    return (starts, lengths, position)

def rotate(values, position):
    half = HD // 2
    freq = THETA ** (-(jnp.arange(half, dtype=jnp.float32) * 2.0) / HD)
    angle = position.astype(jnp.float32)[:, None] * freq[None, :]
    cosine = jnp.cos(angle)[:, None, :]
    sine = jnp.sin(angle)[:, None, :]
    first = values[..., :half]
    second = values[..., half:]
    return jnp.concatenate([first * cosine - second * sine, second * cosine + first * sine], axis=-1)

def reference(hidden_in, segment_ids, request_prompt, page_table, ln_attn, w_query, w_key, w_value, q_gain, k_gain, w_out, ln_mlp, w_gate, w_up, w_down):
    group = H // KVH

    def layer_group(inputs):
        rows, segment_row = inputs
        count = rows.shape[0]
        unused_starts, unused_lengths, position = segment_table(segment_row)
        normed = rms_scale(rows, ln_attn).astype(jnp.bfloat16)
        query = jnp.dot(normed, w_query, preferred_element_type=jnp.float32).reshape(count, H, HD)
        key = jnp.dot(normed, w_key, preferred_element_type=jnp.float32).reshape(count, KVH, HD)
        value = jnp.dot(normed, w_value, preferred_element_type=jnp.float32).astype(jnp.bfloat16).reshape(count, KVH, HD)
        query = rotate(rms_scale(query, q_gain), position).astype(jnp.bfloat16)
        key = rotate(rms_scale(key, k_gain), position).astype(jnp.bfloat16)
        grouped = query.reshape(count, KVH, group, HD).astype(jnp.float32)
        scores = jnp.einsum('qcgd,kcd->cgqk', grouped, key.astype(jnp.float32)) / math.sqrt(HD)
        index = jnp.arange(count, dtype=jnp.int32)
        allowed = (segment_row[:, None] == segment_row[None, :]) & (index[None, :] <= index[:, None])
        raised = jnp.where(allowed[None, None], jnp.exp(scores), 0.0)
        weights = (raised / lax.optimization_barrier(jnp.sum(raised, axis=-1, keepdims=True))).astype(jnp.bfloat16)
        mixed = jnp.einsum('cgqk,kcd->qcgd', weights.astype(jnp.float32), value.astype(jnp.float32))
        attended = mixed.reshape(count, H * HD).astype(jnp.bfloat16)
        after = (rows.astype(jnp.float32) + jnp.dot(attended, w_out, preferred_element_type=jnp.float32)).astype(jnp.bfloat16)
        normed_mlp = rms_scale(after, ln_mlp).astype(jnp.bfloat16)
        gate = jnp.dot(normed_mlp, w_gate, preferred_element_type=jnp.float32)
        upper = jnp.dot(normed_mlp, w_up, preferred_element_type=jnp.float32)
        hidden = (jax.nn.silu(gate) * upper).astype(jnp.bfloat16)
        result = (after.astype(jnp.float32) + jnp.dot(hidden, w_down, preferred_element_type=jnp.float32)).astype(jnp.bfloat16)
        pairs = jnp.concatenate([key, value], axis=-1)
        return (result, pairs)
    blocks = hidden_in.reshape(N_REQ, SEQ_ROWS, D)
    results, pairs = lax.map(layer_group, (blocks, segment_ids))
    pairs_flat = pairs.reshape(N_REQ * SEQ_ROWS, KVH, 2 * HD)
    all_starts, all_lengths, unused = jax.vmap(segment_table)(segment_ids)
    flat_starts = all_starts.reshape(-1)
    flat_lengths = all_lengths.reshape(-1)

    def fill_pool(inputs):
        table_block, prompt_block = inputs
        owner = jnp.zeros((PAGES_DEV,), jnp.int32).at[table_block.reshape(-1)].set(jnp.arange(PAGES_DEV, dtype=jnp.int32))
        request = owner // MAXP
        page = owner % MAXP
        prompt = prompt_block[request]
        begin = prompt // PROMPTS_DEV * SEQ_ROWS + flat_starts[prompt]
        length = flat_lengths[prompt]
        offset = page[:, None] * PAGE + jnp.arange(PAGE, dtype=jnp.int32)[None, :]
        valid = offset < length[:, None]
        source = jnp.where(valid, begin[:, None] + offset, 0).astype(jnp.int32)
        taken = pairs_flat[source]
        return jnp.where(valid[:, :, None, None], taken, jnp.zeros((), jnp.bfloat16))
    pools = lax.map(fill_pool, (page_table.reshape(N_REQ, REQ_DEV, MAXP), request_prompt.reshape(N_REQ, REQ_DEV)))
    return (results.reshape(TOKENS, D), pools.reshape(N_REQ * PAGES_DEV, PAGE, KVH, 2 * HD))
```

```python
import math

import jax
import jax.numpy as jnp
from jax import lax
from jax.experimental import pallas as pl
from jax.experimental.pallas import tpu as pltpu
from jax.sharding import PartitionSpec as P

HD = 128
PROMPTS_DEV = 3
PAGE = 16


EPS = 1e-06
THETA = 1000000.0


def rms_scale(values, gain):
    wide = values.astype(jnp.float32)
    return (
        wide
        * lax.rsqrt(jnp.mean(wide * wide, axis=-1, keepdims=True) + EPS)
        * gain.astype(jnp.float32)
    )


def segment_table(segment_row):
    member = (segment_row[:, None] == jnp.arange(PROMPTS_DEV, dtype=jnp.int32)[None, :]).astype(
        jnp.int32
    )
    lengths = jnp.sum(member, axis=0)
    starts = jnp.cumsum(lengths) - lengths
    index = jnp.arange(segment_row.shape[0], dtype=jnp.int32)
    position = index - jnp.sum(member * starts[None, :], axis=1)
    return (starts, lengths, position)


def rotate(values, position):
    half = HD // 2
    freq = THETA ** (-(jnp.arange(half, dtype=jnp.float32) * 2.0) / HD)
    angle = position.astype(jnp.float32)[:, None] * freq[None, :]
    cosine = jnp.cos(angle)[:, None, :]
    sine = jnp.sin(angle)[:, None, :]
    first = values[..., :half]
    second = values[..., half:]
    return jnp.concatenate(
        [first * cosine - second * sine, second * cosine + first * sine], axis=-1
    )


def request_rows(segment_ids, request_prompt, seq_rows):
    bound = jnp.arange(PROMPTS_DEV + 1, dtype=jnp.int32)
    below = jnp.sum((segment_ids[:, None, :] < bound[None, :, None]).astype(jnp.int32), axis=2)
    groups = segment_ids.shape[0]
    first = below[:, :PROMPTS_DEV] + jnp.arange(groups, dtype=jnp.int32)[:, None] * seq_rows
    counts = below[:, 1:] - below[:, :-1]
    picks = request_prompt[:, None] == jnp.arange(groups * PROMPTS_DEV, dtype=jnp.int32)[None, :]
    begin = jnp.sum(jnp.where(picks, first.reshape(-1)[None, :], 0), axis=1)
    length = jnp.sum(jnp.where(picks, counts.reshape(-1)[None, :], 0), axis=1)
    return begin, length


SLOTS = 8


def fill_kernel(begin_ref, length_ref, table_ref, rows_ref, out_ref, slots, zeros, in_sem, out_sem):
    requests, most = table_ref.shape
    span = most * PAGE
    last = rows_ref.shape[0] - span
    zeros[...] = jnp.zeros_like(zeros)

    def fetch(r, slot):
        at = jnp.minimum(begin_ref[r], last)
        return pltpu.make_async_copy(
            rows_ref.at[pl.ds(at, span)], slots.at[slot, pl.ds(0, span)], in_sem.at[slot]
        )

    def drain(slot):
        pltpu.make_async_copy(
            out_ref.at[pl.ds(0, most)], out_ref.at[pl.ds(0, most)], out_sem.at[slot]
        ).wait()

    ahead = SLOTS // 2
    for r in range(ahead):
        fetch(r, r).start()

    @pl.loop(0, requests)
    def _(r):
        slot = lax.rem(r, SLOTS)
        fetch(r, slot).wait()
        begin, length = begin_ref[r], length_ref[r]
        shift = begin - jnp.minimum(begin, last)
        full = length // PAGE
        rest = length - full * PAGE

        @pl.when(rest > 0)
        def _():
            at = shift + full * PAGE
            tail = slots[slot, pl.ds(at, PAGE)]
            row = lax.broadcasted_iota(jnp.int32, tail.shape, 0)
            slots[slot, pl.ds(at, PAGE)] = jnp.where(row < rest, tail, jnp.zeros_like(tail))

        for e in range(most):
            page = table_ref[r, e]

            @pl.when(e * PAGE < length)
            def _():
                pltpu.make_async_copy(
                    slots.at[slot, pl.ds(shift + e * PAGE, PAGE)], out_ref.at[page], out_sem.at[slot]
                ).start()

            @pl.when(e * PAGE >= length)
            def _():
                pltpu.make_async_copy(zeros, out_ref.at[page], out_sem.at[slot]).start()

        @pl.when(r + ahead < requests)
        def _():
            other = lax.rem(r + ahead, SLOTS)

            @pl.when(r + ahead >= SLOTS)
            def _():
                drain(other)

            fetch(r + ahead, other).start()

    for r in range(max(0, requests - SLOTS), requests):
        drain(r % SLOTS)


def fill_pages(begin, length, page_table, rows):
    requests, most = page_table.shape
    unit = rows.shape[1:]
    smem = pl.BlockSpec(memory_space=pltpu.SMEM)
    return pl.pallas_call(
        fill_kernel,
        out_shape=jax.ShapeDtypeStruct((requests * most, PAGE) + unit, rows.dtype),
        in_specs=[smem, smem, smem, pl.BlockSpec(memory_space=pl.ANY)],
        out_specs=pl.BlockSpec(memory_space=pl.ANY),
        scratch_shapes=[
            pltpu.VMEM((SLOTS, (most + 1) * PAGE) + unit, rows.dtype),
            pltpu.VMEM((PAGE,) + unit, rows.dtype),
            pltpu.SemaphoreType.DMA((SLOTS,)),
            pltpu.SemaphoreType.DMA((SLOTS,)),
        ],
        name="fill_pages",
    )(begin, length, page_table, rows)


def body(
    hidden_in,
    segment_ids,
    request_prompt,
    page_table,
    ln_attn,
    w_query,
    w_key,
    w_value,
    q_gain,
    k_gain,
    w_out,
    ln_mlp,
    w_gate,
    w_up,
    w_down,
):
    parts = lax.axis_size("mp")
    owner_rows = hidden_in.shape[0]
    seq_rows = owner_rows * parts
    heads_here = w_query.shape[1] // HD
    kv_here = w_key.shape[1] // HD
    group = heads_here // kv_here
    group_index = lax.axis_index("req")
    segment_row = lax.dynamic_index_in_dim(segment_ids, group_index, 0, keepdims=False)
    unused_starts, unused_lengths, position = segment_table(segment_row)
    piece = lax.all_gather(hidden_in, "mp", axis=0, tiled=True)
    count = piece.shape[0]
    normed = rms_scale(piece, ln_attn).astype(jnp.bfloat16)
    query = jnp.dot(normed, w_query, preferred_element_type=jnp.float32).reshape(
        count, heads_here, HD
    )
    project_key = jnp.dot(normed, w_key, preferred_element_type=jnp.float32).reshape(
        count, kv_here, HD
    )
    project_value = jnp.dot(normed, w_value, preferred_element_type=jnp.float32).astype(
        jnp.bfloat16
    )
    query = (
        rotate(rms_scale(query, q_gain), position)
        .astype(jnp.bfloat16)
        .reshape(count, heads_here * HD)
    )
    project_key = (
        rotate(rms_scale(project_key, k_gain), position)
        .astype(jnp.bfloat16)
        .reshape(count, kv_here * HD)
    )
    joined = [query, project_key, project_value]
    projected = jnp.concatenate(joined, axis=1)
    query_width = heads_here * HD
    key_width = kv_here * HD
    query = projected[:, :query_width].reshape(seq_rows, kv_here, group, HD)
    key = projected[:, query_width : query_width + key_width].reshape(seq_rows, kv_here, HD)
    value = projected[:, query_width + key_width : query_width + 2 * key_width].reshape(
        seq_rows, kv_here, HD
    )
    block = min(512, seq_rows)
    blocks = seq_rows // block
    key_index = jnp.arange(seq_rows, dtype=jnp.int32)

    def attend_block(inputs):
        query_block, first = inputs
        scores = jnp.einsum(
            "qcgd,kcd->cgqk", query_block, key, preferred_element_type=jnp.float32
        ) / math.sqrt(HD)
        row_index = first + jnp.arange(block, dtype=jnp.int32)
        allowed = (segment_row[:, None] == segment_row[None, :]) & (
            key_index[None, :] <= row_index[:, None]
        )
        raised = jnp.where(allowed[None, None], jnp.exp(scores), 0.0)
        weights = (raised / jnp.sum(raised, axis=-1, keepdims=True)).astype(jnp.bfloat16)
        mixed = jnp.einsum("cgqk,kcd->qcgd", weights, value, preferred_element_type=jnp.float32)
        return mixed.astype(jnp.bfloat16).reshape(block, query_width)

    attended = lax.map(
        attend_block,
        (
            query.reshape(blocks, block, kv_here, group, HD),
            jnp.arange(blocks, dtype=jnp.int32) * block,
        ),
    )
    attended = attended.reshape(seq_rows, query_width)
    own_sum = lax.psum_scatter(
        jnp.dot(attended, w_out, preferred_element_type=jnp.float32).astype(jnp.bfloat16),
        "mp",
        scatter_dimension=0,
        tiled=True,
    ).astype(jnp.float32)
    after = (hidden_in.astype(jnp.float32) + own_sum).astype(jnp.bfloat16)
    normed_mlp = rms_scale(lax.all_gather(after, "mp", axis=0, tiled=True), ln_mlp).astype(
        jnp.bfloat16
    )
    gate = jnp.dot(normed_mlp, w_gate, preferred_element_type=jnp.float32)
    upper = jnp.dot(normed_mlp, w_up, preferred_element_type=jnp.float32)
    hidden = (jax.nn.silu(gate) * upper).astype(jnp.bfloat16)
    result = (
        after.astype(jnp.float32)
        + lax.psum_scatter(
            jnp.dot(hidden, w_down, preferred_element_type=jnp.float32).astype(jnp.bfloat16),
            "mp",
            scatter_dimension=0,
            tiled=True,
        ).astype(jnp.float32)
    ).astype(jnp.bfloat16)
    pairs = jnp.concatenate([key, value], axis=-1)
    begin, length = request_rows(segment_ids, request_prompt, seq_rows)
    everything = lax.all_gather(pairs, "req", axis=0, tiled=True)
    cache = fill_pages(begin, length, page_table, everything)
    return (result, cache)


def solution(mesh):
    return jax.shard_map(
        body,
        mesh=mesh,
        in_specs=(
            P(("req", "mp"), None),
            P(),
            P("req"),
            P("req", None),
            P(),
            P(None, "mp"),
            P(None, "mp"),
            P(None, "mp"),
            P(),
            P(),
            P("mp", None),
            P(),
            P(None, "mp"),
            P(None, "mp"),
            P("mp", None),
        ),
        out_specs=(P(("req", "mp"), None), P("req", None, "mp", None)),
        check_vma=False,
    )
```

```python
import math

import jax
import jax.numpy as jnp
from jax import lax
from jax.experimental import pallas as pl
from jax.experimental.pallas import tpu as pltpu
from jax.sharding import PartitionSpec as P

HD = 128
PROMPTS_DEV = 3
PAGE = 16


EPS = 1e-06
THETA = 1000000.0


def request_rows(segment_ids, request_prompt, seq_rows):
    bound = jnp.arange(PROMPTS_DEV + 1, dtype=jnp.int32)
    below = jnp.sum((segment_ids[:, None, :] < bound[None, :, None]).astype(jnp.int32), axis=2)
    groups = segment_ids.shape[0]
    first = below[:, :PROMPTS_DEV] + jnp.arange(groups, dtype=jnp.int32)[:, None] * seq_rows
    counts = below[:, 1:] - below[:, :-1]
    picks = request_prompt[:, None] == jnp.arange(groups * PROMPTS_DEV, dtype=jnp.int32)[None, :]
    begin = jnp.sum(jnp.where(picks, first.reshape(-1)[None, :], 0), axis=1)
    length = jnp.sum(jnp.where(picks, counts.reshape(-1)[None, :], 0), axis=1)
    return begin, length


SLOTS = 8


def fill_kernel(begin_ref, length_ref, table_ref, rows_ref, out_ref, slots, zeros, in_sem, out_sem):
    requests, most = table_ref.shape
    span = most * PAGE
    last = rows_ref.shape[0] - span
    zeros[...] = jnp.zeros_like(zeros)

    def fetch(r, slot):
        at = jnp.minimum(begin_ref[r], last)
        return pltpu.make_async_copy(
            rows_ref.at[pl.ds(at, span)], slots.at[slot, pl.ds(0, span)], in_sem.at[slot]
        )

    def drain(slot):
        pltpu.make_async_copy(
            out_ref.at[pl.ds(0, most)], out_ref.at[pl.ds(0, most)], out_sem.at[slot]
        ).wait()

    ahead = SLOTS // 2
    for r in range(ahead):
        fetch(r, r).start()

    @pl.loop(0, requests)
    def _(r):
        slot = lax.rem(r, SLOTS)
        fetch(r, slot).wait()
        begin, length = begin_ref[r], length_ref[r]
        shift = begin - jnp.minimum(begin, last)
        full = length // PAGE
        rest = length - full * PAGE

        @pl.when(rest > 0)
        def _():
            at = shift + full * PAGE
            tail = slots[slot, pl.ds(at, PAGE)]
            row = lax.broadcasted_iota(jnp.int32, tail.shape, 0)
            slots[slot, pl.ds(at, PAGE)] = jnp.where(row < rest, tail, jnp.zeros_like(tail))

        for e in range(most):
            page = table_ref[r, e]

            @pl.when(e * PAGE < length)
            def _():
                pltpu.make_async_copy(
                    slots.at[slot, pl.ds(shift + e * PAGE, PAGE)], out_ref.at[page], out_sem.at[slot]
                ).start()

            @pl.when(e * PAGE >= length)
            def _():
                pltpu.make_async_copy(zeros, out_ref.at[page], out_sem.at[slot]).start()

        @pl.when(r + ahead < requests)
        def _():
            other = lax.rem(r + ahead, SLOTS)

            @pl.when(r + ahead >= SLOTS)
            def _():
                drain(other)

            fetch(r + ahead, other).start()

    for r in range(max(0, requests - SLOTS), requests):
        drain(r % SLOTS)


def fill_pages(begin, length, page_table, rows):
    requests, most = page_table.shape
    unit = rows.shape[1:]
    smem = pl.BlockSpec(memory_space=pltpu.SMEM)
    return pl.pallas_call(
        fill_kernel,
        out_shape=jax.ShapeDtypeStruct((requests * most, PAGE) + unit, rows.dtype),
        in_specs=[smem, smem, smem, pl.BlockSpec(memory_space=pl.ANY)],
        out_specs=pl.BlockSpec(memory_space=pl.ANY),
        scratch_shapes=[
            pltpu.VMEM((SLOTS, (most + 1) * PAGE) + unit, rows.dtype),
            pltpu.VMEM((PAGE,) + unit, rows.dtype),
            pltpu.SemaphoreType.DMA((SLOTS,)),
            pltpu.SemaphoreType.DMA((SLOTS,)),
        ],
        name="fill_pages",
    )(begin, length, page_table, rows)


MESH = pl.DeviceIdType.MESH
HALF = 64
SUBS = 2
SIDE = 4
UNIT = 128
PUMPS = SIDE * SIDE


def rms(wide, gain):
    return wide * lax.rsqrt(jnp.mean(wide * wide, axis=-1, keepdims=True) + EPS) * gain


def layer_kernel(
    hidden,
    seg,
    ln_attn,
    w_query,
    w_key,
    w_value,
    q_gain,
    k_gain,
    w_out,
    ln_mlp,
    w_gate,
    w_up,
    w_down,
    out,
    kv,
    hbuf,
    abuf,
    wq,
    wk,
    wv,
    wo,
    wg,
    wu,
    wd,
    qbuf,
    kbuf,
    vbuf,
    kvbuf,
    attbuf,
    actbuf,
    ownbuf,
    send2f,
    send1,
    recv1,
    send2,
    recv2,
    local_sem,
    ag1_send,
    ag1_recv,
    rs1_send,
    rs1_recv,
    ag2_send,
    ag2_recv,
    rs2_send,
    rs2_recv,
    kv_send,
    kv1_recv,
    kv2_recv,
    kv_pair_recv,
):
    x = lax.axis_index("mp")
    c = lax.axis_index("req")
    core = lax.rem(c, 2)
    z = lax.rem(c // 2, SIDE)
    y = c // (2 * SIDE)
    width = hidden.shape[1]
    rows = hidden.shape[0]
    sub = HALF // SUBS

    def turn(value):
        return lax.rem(value + 2 * SIDE, SIDE)

    def req_of(yy, zz, cc):
        return (yy * SIDE + zz) * 2 + cc

    x_near = ((c, turn(x + 1)), (c, turn(x - 1)))
    pair = (req_of(y, z, 1 - core), x)
    y_near = ((req_of(turn(y + 1), z, core), x), (req_of(turn(y - 1), z, core), x))
    z_near = ((req_of(y, turn(z + 1), core), x), (req_of(y, turn(z - 1), core), x))

    moves = []
    weights = ((w_query, wq), (w_key, wk), (w_value, wv), (w_out, wo), (w_gate, wg), (w_up, wu), (w_down, wd))
    for d in range(2):
        for p in range(SUBS):
            moves.append(
                pltpu.make_async_copy(
                    hidden.at[pl.ds(d * HALF + p * sub, sub)], hbuf.at[x, d, p], local_sem.at[d * SUBS + p]
                )
            )
    for n, (src, dst) in enumerate(weights):
        moves.append(pltpu.make_async_copy(src, dst, local_sem.at[2 * SUBS + n]))
    for move in moves:
        move.start()

    barrier = pltpu.get_barrier_semaphore()
    for near in x_near + y_near + z_near + (pair,):
        pl.semaphore_signal(barrier, inc=1, device_id=near, device_id_type=MESH)
    pl.semaphore_wait(barrier, 7)

    def remote(src, dst, send, recv, near):
        return pltpu.make_async_remote_copy(
            src_ref=src, dst_ref=dst, send_sem=send, recv_sem=recv, device_id=near, device_id_type=MESH
        )

    def gather_step(buf, send, recv, j, d, p):
        block = buf.at[turn(x - j) if d == 0 else turn(x + j), d, p]
        return remote(block, block, send.at[j, d, p], recv.at[j, d, p], x_near[d])

    def gather_advance(buf, send, recv, j):
        for p in range(SUBS):
            for d in range(2):
                gather_step(buf, send, recv, j - 1, d, p).wait_recv()

                @pl.when(j < SIDE - 1)
                def _():
                    gather_step(buf, send, recv, j, d, p).start()

    def ring_rows(buf, j):
        a, b = turn(x - j), turn(x + j)
        upper = buf[a, 0].reshape(HALF, width)
        lower = buf[b, 1].reshape(HALF, width)
        return jnp.concatenate([upper, lower], axis=0).astype(jnp.float32)

    for p in range(SUBS):
        for d in range(2):
            own = hidden.at[pl.ds(d * HALF + p * sub, sub)]
            remote(own, hbuf.at[x, d, p], ag1_send.at[0, d, p], ag1_recv.at[0, d, p], x_near[d]).start()

    seg_row = seg[pl.ds(c, 1), :]
    first1 = jnp.sum((seg_row < 1).astype(jnp.int32), axis=1, keepdims=True)
    first2 = jnp.sum((seg_row < 2).astype(jnp.int32), axis=1, keepdims=True)

    def begin_of(token):
        return jnp.where(token >= first2, first2, jnp.where(token >= first1, first1, 0))

    lane = lax.broadcasted_iota(jnp.int32, (1, HD), 1)
    freq = jnp.exp2(lax.rem(lane, HD // 2).astype(jnp.float32) * (-2.0 * math.log2(THETA) / HD))
    sign = jnp.where(lane < HD // 2, -1.0, 1.0)
    gain_attn = ln_attn[...].astype(jnp.float32)
    gain_mlp = ln_mlp[...].astype(jnp.float32)
    gain_q = q_gain[...].astype(jnp.float32)
    gain_k = k_gain[...].astype(jnp.float32)
    heads = wq.shape[1] // HD
    kv_heads = wk.shape[1] // HD
    group = heads // kv_heads

    for move in moves[: 2 * SUBS + 3]:
        move.wait()

    @pl.loop(0, SIDE)
    def _(j):
        @pl.when(j > 0)
        def _():
            gather_advance(hbuf, ag1_send, ag1_recv, j)

        a, b = turn(x - j), turn(x + j)
        normed = rms(ring_rows(hbuf, j), gain_attn).astype(jnp.bfloat16)
        row = lax.broadcasted_iota(jnp.int32, (rows, 1), 0)
        token = jnp.where(row < HALF, a, b) * rows + row
        angle = (token - begin_of(token)).astype(jnp.float32) * freq
        cosine = jnp.cos(angle)
        sine = jnp.sin(angle) * sign

        def turned(values, gain):
            scaled = rms(values, gain)
            return (scaled * cosine + pltpu.roll(scaled, HD // 2, 1) * sine).astype(jnp.bfloat16)

        query = jnp.dot(normed, wq[...], preferred_element_type=jnp.float32)
        key = jnp.dot(normed, wk[...], preferred_element_type=jnp.float32)
        value = jnp.dot(normed, wv[...], preferred_element_type=jnp.float32).astype(jnp.bfloat16)
        for h in range(heads):
            part = turned(query[:, h * HD : (h + 1) * HD], gain_q)
            qbuf[a, 0, :, h * HD : (h + 1) * HD] = part[:HALF]
            qbuf[b, 1, :, h * HD : (h + 1) * HD] = part[HALF:]
        for h in range(kv_heads):
            part = turned(key[:, h * HD : (h + 1) * HD], gain_k)
            mine = value[:, h * HD : (h + 1) * HD]
            kbuf[a, 0, :, h * HD : (h + 1) * HD] = part[:HALF]
            kbuf[b, 1, :, h * HD : (h + 1) * HD] = part[HALF:]
            both = jnp.concatenate([part, mine], axis=1)
            kvbuf[pl.ds(a * rows, HALF), h, :] = both[:HALF]
            kvbuf[pl.ds(b * rows + HALF, HALF), h, :] = both[HALF:]
        vbuf[a, 0] = value[:HALF]
        vbuf[b, 1] = value[HALF:]

    seq = SIDE * rows
    kv_own = pltpu.make_async_copy(kvbuf, kv.at[pl.ds(c * seq, seq)], local_sem.at[2 * SUBS + len(weights)])
    kv_own.start()

    flows = ((0, 0), (0, 1), (1, 0), (1, 1))

    def pump(p):
        b, k = lax.rem(p, SIDE), p // SIDE
        for f, (axis, d) in enumerate(flows):
            sign_d = 1 if d == 0 else -1
            first = y_near[d] if axis == 0 else z_near[d]
            second = z_near[d] if axis == 0 else y_near[d]
            if axis == 0:
                oy, oz = turn(y - sign_d * b), turn(z - sign_d * k)
            else:
                oy, oz = turn(y - sign_d * k), turn(z - sign_d * b)
            at = req_of(oy, oz, core) * seq + f * UNIT
            block = kv.at[pl.ds(pl.multiple_of(at, UNIT), UNIT)]

            @pl.when((p >= 1) & (p < SIDE))
            def _():
                remote(block, block, kv_send.at[0], kv1_recv.at[f, p - 1], first).wait_recv()

            @pl.when(p >= SIDE)
            def _():
                remote(block, block, kv_send.at[0], kv2_recv.at[f, p - SIDE], second).wait_recv()

            @pl.when(p < SIDE - 1)
            def _():
                remote(block, block, kv_send.at[0], kv1_recv.at[f, p], first).start()

            @pl.when(p < PUMPS - SIDE)
            def _():
                remote(block, block, kv_send.at[0], kv2_recv.at[f, p], second).start()

            remote(block, block, kv_send.at[0], kv_pair_recv.at[0], pair).start()

    kv_own.wait()
    pump(jnp.int32(0))

    keys = kbuf[...].reshape(seq, kv_heads * HD)
    values = vbuf[...].reshape(seq, kv_heads * HD)
    for i in range(SIDE):
        extent = (i + 1) * rows
        token = lax.broadcasted_iota(jnp.int32, (rows, extent), 0) + i * rows
        other = lax.broadcasted_iota(jnp.int32, (rows, extent), 1)
        allowed = (other <= token) & (other >= begin_of(token[:, :1]))
        allowed = jnp.concatenate([allowed.astype(jnp.float32)] * group, axis=0) > 0.5
        block = qbuf[i].reshape(rows, heads * HD)
        for n in range(kv_heads):
            stacked = jnp.concatenate(
                [block[:, (n * group + h) * HD : (n * group + h + 1) * HD] for h in range(group)], axis=0
            )
            scores = lax.dot_general(
                stacked,
                keys[:extent, n * HD : (n + 1) * HD],
                (((1,), (1,)), ((), ())),
                preferred_element_type=jnp.float32,
            )
            raised = jnp.where(allowed, jnp.exp(scores * (1.0 / math.sqrt(HD))), 0.0)
            share = (raised * (1.0 / jnp.sum(raised, axis=-1, keepdims=True))).astype(jnp.bfloat16)
            mixed = jnp.dot(
                share, values[:extent, n * HD : (n + 1) * HD], preferred_element_type=jnp.float32
            ).astype(jnp.bfloat16)
            for h in range(group):
                at = (n * group + h) * HD
                attbuf[i, 0, :, at : at + HD] = mixed[h * rows : h * rows + HALF]
                attbuf[i, 1, :, at : at + HD] = mixed[h * rows + HALF : (h + 1) * rows]
    pump(jnp.int32(1))

    piece = width // SUBS

    def sum_step(send_buf, recv_buf, send, recv, j, d, n):
        return remote(send_buf.at[j, d, n], recv_buf.at[j, d, n], send.at[j, d, n], recv.at[j, d, n], x_near[d])

    def add_arrived(part, send_buf, recv_buf, send, recv, j, n):
        for d in range(2):
            sum_step(send_buf, recv_buf, send, recv, j, d, n).wait_recv()
        return part + jnp.concatenate([recv_buf[j, 0, n], recv_buf[j, 1, n]], axis=0).astype(jnp.float32)

    def send_on(part, send_buf, recv_buf, send, recv, j, n):
        rounded = part.astype(jnp.bfloat16)
        for d in range(2):
            send_buf[j, d, n] = rounded[d * HALF : (d + 1) * HALF]
            sum_step(send_buf, recv_buf, send, recv, j, d, n).start()

    ring1 = (send1, recv1, rs1_send, rs1_recv)
    ring2 = (send2, recv2, rs2_send, rs2_recv)

    moves[2 * SUBS + 3].wait()

    def out_rows(j):
        return jnp.concatenate([attbuf[turn(x - 1 - j), 0], attbuf[turn(x + 1 + j), 1]], axis=0)

    def out_part(mixed, n):
        return jnp.dot(mixed, wo[:, n * piece : (n + 1) * piece], preferred_element_type=jnp.float32)

    mixed = out_rows(0)
    for n in range(SUBS):
        send_on(out_part(mixed, n), *ring1, 0, n)

    @pl.loop(1, SIDE - 1)
    def _(j):
        mixed = out_rows(j)
        for n in range(SUBS):
            part = out_part(mixed, n)
            part = add_arrived(part, *ring1, j - 1, n)
            send_on(part, *ring1, j, n)
        pump(j + 1)

    mixed = out_rows(SIDE - 1)
    for n in range(SUBS):
        part = add_arrived(out_part(mixed, n), *ring1, SIDE - 2, n)
        for d in range(2):
            before = hbuf[x, d, :, :, n * piece : (n + 1) * piece].astype(jnp.float32)
            total = before + part[d * HALF : (d + 1) * HALF].reshape(SUBS, sub, piece)
            abuf[x, d, :, :, n * piece : (n + 1) * piece] = total.astype(jnp.bfloat16)
    for p in range(SUBS):
        for d in range(2):
            gather_step(abuf, ag2_send, ag2_recv, 0, d, p).start()
    pump(jnp.int32(SIDE))

    for move in moves[2 * SUBS + 4 :]:
        move.wait()

    def activation(j):
        normed = rms(ring_rows(abuf, j), gain_mlp).astype(jnp.bfloat16)
        gate = jnp.dot(normed, wg[...], preferred_element_type=jnp.float32)
        upper = jnp.dot(normed, wu[...], preferred_element_type=jnp.float32)
        return (gate * jax.nn.sigmoid(gate) * upper).astype(jnp.bfloat16)

    def down_part(act, n):
        return jnp.dot(act, wd[:, n * piece : (n + 1) * piece], preferred_element_type=jnp.float32)

    @pl.loop(0, SIDE)
    def _(j):
        @pl.when(j > 0)
        def _():
            gather_advance(abuf, ag2_send, ag2_recv, j)

        actbuf[...] = activation(j)
        pump(2 * j + SIDE + 1)

        @pl.when(j > 0)
        def _():
            act = actbuf[...]
            for n in range(SUBS):
                part = down_part(act, n)
                send2f[n] = part

                @pl.when(j > 1)
                def _():
                    send2f[n] = add_arrived(send2f[n], *ring2, j - 2, n)

                send_on(send2f[n], *ring2, j - 1, n)

        @pl.when(j == 0)
        def _():
            ownbuf[...] = actbuf[...]

        pump(2 * j + SIDE + 2)

    act = ownbuf[...]
    for p in range(3 * SIDE + 1, PUMPS):
        pump(jnp.int32(p))
    for n in range(SUBS):
        part = add_arrived(down_part(act, n), *ring2, SIDE - 2, n)
        for d in range(2):
            before = abuf[x, d, :, :, n * piece : (n + 1) * piece].reshape(HALF, piece).astype(jnp.float32)
            total = before + part[d * HALF : (d + 1) * HALF]
            out[d * HALF : (d + 1) * HALF, n * piece : (n + 1) * piece] = total.astype(jnp.bfloat16)

    @pl.loop(0, SIDE - 1)
    def _(j):
        for d in range(2):
            for p in range(SUBS):
                gather_step(hbuf, ag1_send, ag1_recv, j, d, p).wait_send()
                gather_step(abuf, ag2_send, ag2_recv, j, d, p).wait_send()
                sum_step(*ring1, j, d, p).wait_send()
                sum_step(*ring2, j, d, p).wait_send()

    sent = UNIT * len(flows) * (SIDE - 1 + PUMPS - SIDE + PUMPS)
    whole = kv.at[pl.ds(0, sent)]
    remote(whole, whole, kv_send.at[0], kv_pair_recv.at[0], pair).wait_send()
    got = kv.at[pl.ds(0, UNIT * len(flows) * PUMPS)]
    remote(got, got, kv_send.at[0], kv_pair_recv.at[0], pair).wait_recv()


def run_layer(hidden, seg, ln_attn, w_query, w_key, w_value, q_gain, k_gain, w_out, ln_mlp, w_gate, w_up, w_down):
    rows, width = hidden.shape
    seq = rows * SIDE
    units = w_gate.shape[1]
    kvw = w_key.shape[1]
    heads_w = w_query.shape[1]
    bf16, f32 = jnp.bfloat16, jnp.float32
    sub = HALF // SUBS
    vmem = pl.BlockSpec(memory_space=pltpu.VMEM)
    hbm = pl.BlockSpec(memory_space=pl.ANY)
    ring = (SIDE - 1, 2, SUBS)
    dma = pltpu.SemaphoreType.DMA
    blocks = pltpu.VMEM(ring + (HALF, width // SUBS), bf16)
    return pl.pallas_call(
        layer_kernel,
        out_shape=(
            jax.ShapeDtypeStruct((rows, width), bf16),
            jax.ShapeDtypeStruct((seg.shape[0] * seq, kvw // HD, 2 * HD), bf16),
        ),
        in_specs=[hbm, vmem, vmem, hbm, hbm, hbm, vmem, vmem, hbm, vmem, hbm, hbm, hbm],
        out_specs=(vmem, hbm),
        scratch_shapes=[
            pltpu.VMEM((SIDE, 2, SUBS, sub, width), bf16),
            pltpu.VMEM((SIDE, 2, SUBS, sub, width), bf16),
            pltpu.VMEM(w_query.shape, bf16),
            pltpu.VMEM(w_key.shape, bf16),
            pltpu.VMEM(w_value.shape, bf16),
            pltpu.VMEM(w_out.shape, bf16),
            pltpu.VMEM(w_gate.shape, bf16),
            pltpu.VMEM(w_up.shape, bf16),
            pltpu.VMEM(w_down.shape, bf16),
            pltpu.VMEM((SIDE, 2, HALF, heads_w), bf16),
            pltpu.VMEM((SIDE, 2, HALF, kvw), bf16),
            pltpu.VMEM((SIDE, 2, HALF, kvw), bf16),
            pltpu.VMEM((seq, kvw // HD, 2 * HD), bf16),
            pltpu.VMEM((SIDE, 2, HALF, heads_w), bf16),
            pltpu.VMEM((rows, units), bf16),
            pltpu.VMEM((rows, units), bf16),
            pltpu.VMEM((SUBS, rows, width // SUBS), f32),
            blocks,
            blocks,
            blocks,
            blocks,
            dma((2 * SUBS + 8,)),
        ]
        + [dma(ring)] * 8
        + [dma((1,)), dma((4, SIDE - 1)), dma((4, PUMPS - SIDE)), dma((1,))],
        compiler_params=pltpu.CompilerParams(
            collective_id=0, has_side_effects=True, vmem_limit_bytes=60 * 1024 * 1024
        ),
        name="layer",
    )(hidden, seg, ln_attn, w_query, w_key, w_value, q_gain, k_gain, w_out, ln_mlp, w_gate, w_up, w_down)


def body(
    hidden_in,
    segment_ids,
    request_prompt,
    page_table,
    ln_attn,
    w_query,
    w_key,
    w_value,
    q_gain,
    k_gain,
    w_out,
    ln_mlp,
    w_gate,
    w_up,
    w_down,
):
    begin, length = request_rows(segment_ids, request_prompt, segment_ids.shape[1])
    result, everything = run_layer(
        hidden_in,
        segment_ids,
        ln_attn[None, :],
        w_query,
        w_key,
        w_value,
        q_gain[None, :],
        k_gain[None, :],
        w_out,
        ln_mlp[None, :],
        w_gate,
        w_up,
        w_down,
    )
    return (result, fill_pages(begin, length, page_table, everything))


def solution(mesh):
    return jax.shard_map(
        body,
        mesh=mesh,
        in_specs=(
            P(("req", "mp"), None),
            P(),
            P("req"),
            P("req", None),
            P(),
            P(None, "mp"),
            P(None, "mp"),
            P(None, "mp"),
            P(),
            P(),
            P("mp", None),
            P(),
            P(None, "mp"),
            P(None, "mp"),
            P("mp", None),
        ),
        out_specs=(P(("req", "mp"), None), P("req", None, "mp", None)),
        check_vma=False,
    )
```

```python
import math

import jax
import jax.numpy as jnp
from jax import lax
from jax.experimental import pallas as pl
from jax.experimental.pallas import tpu as pltpu
from jax.sharding import PartitionSpec as P

HD = 128
PROMPTS_DEV = 3
PAGE = 16


EPS = 1e-06
THETA = 1000000.0


SLOTS = 16
AHEAD = 12


def fill_kernel(
    table_hbm, prompt_hbm, bounds_hbm, layer_hbm, rows_ref, out_ref, layer_out, table, prompt, bounds, held, slots,
    zeros, small_sem, in_sem, out_sem,
):
    most, requests = table.shape
    span = most * PAGE
    last = rows_ref.shape[0] - span
    seq = rows_ref.shape[0] // bounds.shape[0]
    smalls = [
        pltpu.make_async_copy(src, dst, small_sem.at[n])
        for n, (src, dst) in enumerate(
            ((table_hbm, table), (prompt_hbm, prompt), (bounds_hbm, bounds), (layer_hbm, held))
        )
    ]
    layer_copy = pltpu.make_async_copy(held, layer_out, small_sem.at[4])
    for small in smalls:
        small.start()
    zeros[...] = jnp.zeros_like(zeros)
    for small in smalls:
        small.wait()
    layer_copy.start()

    def place(r):
        p = prompt[r]
        g = p // PROMPTS_DEV
        s = p - g * PROMPTS_DEV
        low = jnp.where(s == 0, 0, jnp.where(s == 1, bounds[g, 0], bounds[g, 1]))
        high = jnp.where(s == 0, bounds[g, 0], jnp.where(s == 1, bounds[g, 1], seq))
        begin = g * seq + low
        return begin, high - low, jnp.minimum(begin, last)

    def fetch(r, slot):
        at = place(r)[2]
        return pltpu.make_async_copy(
            rows_ref.at[pl.ds(at, span)], slots.at[slot, pl.ds(0, span)], in_sem.at[slot]
        )

    def drain(slot):
        pltpu.make_async_copy(
            out_ref.at[pl.ds(0, most)], out_ref.at[pl.ds(0, most)], out_sem.at[slot]
        ).wait()

    for r in range(min(AHEAD, requests)):
        fetch(r, r).start()

    @pl.loop(0, requests)
    def _(r):
        slot = lax.rem(r, SLOTS)
        fetch(r, slot).wait()
        begin, length, at = place(r)
        shift = begin - at
        full = length // PAGE
        rest = length - full * PAGE

        @pl.when(rest > 0)
        def _():
            edge = shift + full * PAGE
            tail = slots[slot, pl.ds(edge, PAGE)]
            row = lax.broadcasted_iota(jnp.int32, tail.shape, 0)
            slots[slot, pl.ds(edge, PAGE)] = jnp.where(row < rest, tail, jnp.zeros_like(tail))

        for e in range(most):
            page = table[e, r]

            @pl.when(e * PAGE < length)
            def _():
                pltpu.make_async_copy(
                    slots.at[slot, pl.ds(shift + e * PAGE, PAGE)], out_ref.at[page], out_sem.at[slot]
                ).start()

            @pl.when(e * PAGE >= length)
            def _():
                pltpu.make_async_copy(zeros, out_ref.at[page], out_sem.at[slot]).start()

        @pl.when(r + AHEAD < requests)
        def _():
            other = lax.rem(r + AHEAD, SLOTS)

            @pl.when(r + AHEAD >= SLOTS)
            def _():
                drain(other)

            fetch(r + AHEAD, other).start()

    for r in range(max(0, requests - SLOTS), requests):
        drain(r % SLOTS)
    layer_copy.wait()


def fill_pages(page_table, request_prompt, bounds, layer, rows):
    requests, most = page_table.shape
    unit = rows.shape[1:]
    hbm = pl.BlockSpec(memory_space=pl.ANY)
    return pl.pallas_call(
        fill_kernel,
        out_shape=(
            jax.ShapeDtypeStruct((requests * most, PAGE) + unit, rows.dtype),
            jax.ShapeDtypeStruct(layer.shape, layer.dtype),
        ),
        in_specs=[hbm] * 5,
        out_specs=(hbm, hbm),
        scratch_shapes=[
            pltpu.SMEM((most, requests), jnp.int32),
            pltpu.SMEM((requests,), jnp.int32),
            pltpu.SMEM(bounds.shape, jnp.int32),
            pltpu.VMEM(layer.shape, layer.dtype),
            pltpu.VMEM((SLOTS, (most + 1) * PAGE) + unit, rows.dtype),
            pltpu.VMEM((PAGE,) + unit, rows.dtype),
            pltpu.SemaphoreType.DMA((5,)),
            pltpu.SemaphoreType.DMA((SLOTS,)),
            pltpu.SemaphoreType.DMA((SLOTS,)),
        ],
        name="fill_pages",
    )(page_table.T, request_prompt, bounds, layer, rows)


MESH = pl.DeviceIdType.MESH
HALF = 64
SUBS = 2
SIDE = 4
UNIT = 128
PUMPS = SIDE * SIDE


def rms(wide, gain):
    return wide * lax.rsqrt(jnp.mean(wide * wide, axis=-1, keepdims=True) + EPS) * gain


def layer_kernel(
    hidden,
    seg,
    ln_attn,
    w_query,
    w_key,
    w_value,
    q_gain,
    k_gain,
    w_out,
    ln_mlp,
    w_gate,
    w_up,
    w_down,
    out,
    kv,
    bounds,
    hbuf,
    abuf,
    wq,
    wk,
    wv,
    wo,
    wg,
    wu,
    wd,
    qbuf,
    kbuf,
    vbuf,
    kvbuf,
    attbuf,
    actbuf,
    ownbuf,
    send2f,
    send1,
    recv1,
    send2,
    recv2,
    local_sem,
    ag1_send,
    ag1_recv,
    rs1_send,
    rs1_recv,
    ag2_send,
    ag2_recv,
    rs2_send,
    rs2_recv,
    kv_send,
    kv1_recv,
    kv2_recv,
    kv_pair_recv,
):
    x = lax.axis_index("mp")
    c = lax.axis_index("req")
    core = lax.rem(c, 2)
    z = lax.rem(c // 2, SIDE)
    y = c // (2 * SIDE)
    width = hidden.shape[1]
    rows = hidden.shape[0]
    sub = HALF // SUBS

    def turn(value):
        return lax.rem(value + 2 * SIDE, SIDE)

    def req_of(yy, zz, cc):
        return (yy * SIDE + zz) * 2 + cc

    x_near = ((c, turn(x + 1)), (c, turn(x - 1)))
    pair = (req_of(y, z, 1 - core), x)
    y_near = ((req_of(turn(y + 1), z, core), x), (req_of(turn(y - 1), z, core), x))
    z_near = ((req_of(y, turn(z + 1), core), x), (req_of(y, turn(z - 1), core), x))

    moves = []
    weights = ((w_query, wq), (w_key, wk), (w_value, wv), (w_out, wo), (w_gate, wg), (w_up, wu), (w_down, wd))
    for d in range(2):
        for p in range(SUBS):
            moves.append(
                pltpu.make_async_copy(
                    hidden.at[pl.ds(d * HALF + p * sub, sub)], hbuf.at[x, d, p], local_sem.at[d * SUBS + p]
                )
            )
    for n, (src, dst) in enumerate(weights):
        moves.append(pltpu.make_async_copy(src, dst, local_sem.at[2 * SUBS + n]))
    for move in moves:
        move.start()

    barrier = pltpu.get_barrier_semaphore()
    for near in x_near + y_near + z_near + (pair,):
        pl.semaphore_signal(barrier, inc=1, device_id=near, device_id_type=MESH)
    pl.semaphore_wait(barrier, 7)

    def remote(src, dst, send, recv, near):
        return pltpu.make_async_remote_copy(
            src_ref=src, dst_ref=dst, send_sem=send, recv_sem=recv, device_id=near, device_id_type=MESH
        )

    def gather_step(buf, send, recv, j, d, p):
        block = buf.at[turn(x - j) if d == 0 else turn(x + j), d, p]
        return remote(block, block, send.at[j, d, p], recv.at[j, d, p], x_near[d])

    def gather_advance(buf, send, recv, j):
        for p in range(SUBS):
            for d in range(2):
                gather_step(buf, send, recv, j - 1, d, p).wait_recv()

                @pl.when(j < SIDE - 1)
                def _():
                    gather_step(buf, send, recv, j, d, p).start()

    def ring_rows(buf, j):
        a, b = turn(x - j), turn(x + j)
        upper = buf[a, 0].reshape(HALF, width)
        lower = buf[b, 1].reshape(HALF, width)
        return jnp.concatenate([upper, lower], axis=0).astype(jnp.float32)

    for p in range(SUBS):
        for d in range(2):
            own = hidden.at[pl.ds(d * HALF + p * sub, sub)]
            remote(own, hbuf.at[x, d, p], ag1_send.at[0, d, p], ag1_recv.at[0, d, p], x_near[d]).start()

    def below(table, bound):
        return jnp.sum((table < bound).astype(jnp.int32), axis=1, keepdims=True)

    seg_row = seg[pl.ds(c, 1), :]
    first1, first2 = below(seg_row, 1), below(seg_row, 2)
    place = lax.broadcasted_iota(jnp.int32, bounds.shape, 1)
    bounds[...] = jnp.where(place == 0, below(seg[...], 1), below(seg[...], 2))

    def begin_of(token):
        return jnp.where(token >= first2, first2, jnp.where(token >= first1, first1, 0))

    lane = lax.broadcasted_iota(jnp.int32, (1, HD), 1)
    freq = jnp.exp2(lax.rem(lane, HD // 2).astype(jnp.float32) * (-2.0 * math.log2(THETA) / HD))
    sign = jnp.where(lane < HD // 2, -1.0, 1.0)
    gain_attn, gain_mlp, gain_q, gain_k = (
        gain[...].astype(jnp.float32).reshape(1, -1) for gain in (ln_attn, ln_mlp, q_gain, k_gain)
    )
    heads = wq.shape[1] // HD
    kv_heads = wk.shape[1] // HD
    group = heads // kv_heads

    for move in moves[: 2 * SUBS + 3]:
        move.wait()

    @pl.loop(0, SIDE)
    def _(j):
        @pl.when(j > 0)
        def _():
            gather_advance(hbuf, ag1_send, ag1_recv, j)

        a, b = turn(x - j), turn(x + j)
        normed = rms(ring_rows(hbuf, j), gain_attn).astype(jnp.bfloat16)
        row = lax.broadcasted_iota(jnp.int32, (rows, 1), 0)
        token = jnp.where(row < HALF, a, b) * rows + row
        angle = (token - begin_of(token)).astype(jnp.float32) * freq
        cosine = jnp.cos(angle)
        sine = jnp.sin(angle) * sign

        def turned(values, gain):
            scaled = rms(values, gain)
            return (scaled * cosine + pltpu.roll(scaled, HD // 2, 1) * sine).astype(jnp.bfloat16)

        query = jnp.dot(normed, wq[...], preferred_element_type=jnp.float32)
        key = jnp.dot(normed, wk[...], preferred_element_type=jnp.float32)
        value = jnp.dot(normed, wv[...], preferred_element_type=jnp.float32).astype(jnp.bfloat16)
        for h in range(heads):
            part = turned(query[:, h * HD : (h + 1) * HD], gain_q)
            qbuf[a, 0, :, h * HD : (h + 1) * HD] = part[:HALF]
            qbuf[b, 1, :, h * HD : (h + 1) * HD] = part[HALF:]
        for h in range(kv_heads):
            part = turned(key[:, h * HD : (h + 1) * HD], gain_k)
            mine = value[:, h * HD : (h + 1) * HD]
            kbuf[a, 0, :, h * HD : (h + 1) * HD] = part[:HALF]
            kbuf[b, 1, :, h * HD : (h + 1) * HD] = part[HALF:]
            both = jnp.concatenate([part, mine], axis=1)
            kvbuf[pl.ds(a * rows, HALF), h, :] = both[:HALF]
            kvbuf[pl.ds(b * rows + HALF, HALF), h, :] = both[HALF:]
        vbuf[a, 0] = value[:HALF]
        vbuf[b, 1] = value[HALF:]

    seq = SIDE * rows
    kv_own = pltpu.make_async_copy(kvbuf, kv.at[pl.ds(c * seq, seq)], local_sem.at[2 * SUBS + len(weights)])
    kv_own.start()

    flows = ((0, 0), (0, 1), (1, 0), (1, 1))

    def pump(p):
        b, k = lax.rem(p, SIDE), p // SIDE
        for f, (axis, d) in enumerate(flows):
            sign_d = 1 if d == 0 else -1
            first = y_near[d] if axis == 0 else z_near[d]
            second = z_near[d] if axis == 0 else y_near[d]
            if axis == 0:
                oy, oz = turn(y - sign_d * b), turn(z - sign_d * k)
            else:
                oy, oz = turn(y - sign_d * k), turn(z - sign_d * b)
            at = req_of(oy, oz, core) * seq + f * UNIT
            block = kv.at[pl.ds(pl.multiple_of(at, UNIT), UNIT)]

            @pl.when((p >= 1) & (p < SIDE))
            def _():
                remote(block, block, kv_send.at[0], kv1_recv.at[f, p - 1], first).wait_recv()

            @pl.when(p >= SIDE)
            def _():
                remote(block, block, kv_send.at[0], kv2_recv.at[f, p - SIDE], second).wait_recv()

            @pl.when(p < SIDE - 1)
            def _():
                remote(block, block, kv_send.at[0], kv1_recv.at[f, p], first).start()

            @pl.when(p < PUMPS - SIDE)
            def _():
                remote(block, block, kv_send.at[0], kv2_recv.at[f, p], second).start()

            remote(block, block, kv_send.at[0], kv_pair_recv.at[0], pair).start()

    kv_own.wait()
    pump(jnp.int32(0))

    keys = kbuf[...].reshape(seq, kv_heads * HD)
    values = vbuf[...].reshape(seq, kv_heads * HD)
    for i in range(SIDE):
        extent = (i + 1) * rows
        token = lax.broadcasted_iota(jnp.int32, (rows, extent), 0) + i * rows
        other = lax.broadcasted_iota(jnp.int32, (rows, extent), 1)
        allowed = (other <= token) & (other >= begin_of(token[:, :1]))
        allowed = jnp.concatenate([allowed.astype(jnp.float32)] * group, axis=0) > 0.5
        block = qbuf[i].reshape(rows, heads * HD)
        for n in range(kv_heads):
            stacked = jnp.concatenate(
                [block[:, (n * group + h) * HD : (n * group + h + 1) * HD] for h in range(group)], axis=0
            )
            scores = lax.dot_general(
                stacked,
                keys[:extent, n * HD : (n + 1) * HD],
                (((1,), (1,)), ((), ())),
                preferred_element_type=jnp.float32,
            )
            raised = jnp.where(allowed, jnp.exp(scores * (1.0 / math.sqrt(HD))), 0.0)
            share = (raised * (1.0 / jnp.sum(raised, axis=-1, keepdims=True))).astype(jnp.bfloat16)
            mixed = jnp.dot(
                share, values[:extent, n * HD : (n + 1) * HD], preferred_element_type=jnp.float32
            ).astype(jnp.bfloat16)
            for h in range(group):
                at = (n * group + h) * HD
                attbuf[i, 0, :, at : at + HD] = mixed[h * rows : h * rows + HALF]
                attbuf[i, 1, :, at : at + HD] = mixed[h * rows + HALF : (h + 1) * rows]
    piece = width // SUBS

    def sum_step(send_buf, recv_buf, send, recv, j, d, n):
        return remote(send_buf.at[j, d, n], recv_buf.at[j, d, n], send.at[j, d, n], recv.at[j, d, n], x_near[d])

    def add_arrived(part, send_buf, recv_buf, send, recv, j, n):
        for d in range(2):
            sum_step(send_buf, recv_buf, send, recv, j, d, n).wait_recv()
        return part + jnp.concatenate([recv_buf[j, 0, n], recv_buf[j, 1, n]], axis=0).astype(jnp.float32)

    def send_on(part, send_buf, recv_buf, send, recv, j, n):
        rounded = part.astype(jnp.bfloat16)
        for d in range(2):
            send_buf[j, d, n] = rounded[d * HALF : (d + 1) * HALF]
            sum_step(send_buf, recv_buf, send, recv, j, d, n).start()

    ring1 = (send1, recv1, rs1_send, rs1_recv)
    ring2 = (send2, recv2, rs2_send, rs2_recv)

    moves[2 * SUBS + 3].wait()

    def out_rows(j):
        return jnp.concatenate([attbuf[turn(x - 1 - j), 0], attbuf[turn(x + 1 + j), 1]], axis=0)

    def out_part(mixed, n):
        return jnp.dot(mixed, wo[:, n * piece : (n + 1) * piece], preferred_element_type=jnp.float32)

    mixed = out_rows(0)
    for n in range(SUBS):
        send_on(out_part(mixed, n), *ring1, 0, n)
    pump(jnp.int32(1))

    @pl.loop(1, SIDE - 1)
    def _(j):
        mixed = out_rows(j)
        for n in range(SUBS):
            part = out_part(mixed, n)
            part = add_arrived(part, *ring1, j - 1, n)
            send_on(part, *ring1, j, n)
        pump(j + 1)

    pump(jnp.int32(SIDE))
    pump(jnp.int32(SIDE + 1))
    mixed = out_rows(SIDE - 1)
    for n in range(SUBS):
        part = add_arrived(out_part(mixed, n), *ring1, SIDE - 2, n)
        for d in range(2):
            before = hbuf[x, d, :, :, n * piece : (n + 1) * piece].astype(jnp.float32)
            total = before + part[d * HALF : (d + 1) * HALF].reshape(SUBS, sub, piece)
            abuf[x, d, :, :, n * piece : (n + 1) * piece] = total.astype(jnp.bfloat16)
    for p in range(SUBS):
        for d in range(2):
            gather_step(abuf, ag2_send, ag2_recv, 0, d, p).start()
    pump(jnp.int32(SIDE + 2))
    pump(jnp.int32(SIDE + 3))

    for move in moves[2 * SUBS + 4 :]:
        move.wait()

    def activation(j):
        normed = rms(ring_rows(abuf, j), gain_mlp).astype(jnp.bfloat16)
        gate = jnp.dot(normed, wg[...], preferred_element_type=jnp.float32)
        upper = jnp.dot(normed, wu[...], preferred_element_type=jnp.float32)
        return (gate * jax.nn.sigmoid(gate) * upper).astype(jnp.bfloat16)

    def down_part(act, n):
        return jnp.dot(act, wd[:, n * piece : (n + 1) * piece], preferred_element_type=jnp.float32)

    @pl.loop(0, SIDE)
    def _(j):
        @pl.when(j > 0)
        def _():
            gather_advance(abuf, ag2_send, ag2_recv, j)

        actbuf[...] = activation(j)
        pump(2 * j + 2 * SIDE)

        @pl.when(j > 0)
        def _():
            act = actbuf[...]
            for n in range(SUBS):
                part = down_part(act, n)
                send2f[n] = part

                @pl.when(j > 1)
                def _():
                    send2f[n] = add_arrived(send2f[n], *ring2, j - 2, n)

                send_on(send2f[n], *ring2, j - 1, n)

        @pl.when(j == 0)
        def _():
            ownbuf[...] = actbuf[...]

        pump(2 * j + 2 * SIDE + 1)

    act = ownbuf[...]
    for n in range(SUBS):
        part = add_arrived(down_part(act, n), *ring2, SIDE - 2, n)
        for d in range(2):
            before = abuf[x, d, :, :, n * piece : (n + 1) * piece].reshape(HALF, piece).astype(jnp.float32)
            total = before + part[d * HALF : (d + 1) * HALF]
            out[d * HALF : (d + 1) * HALF, n * piece : (n + 1) * piece] = total.astype(jnp.bfloat16)

    @pl.loop(0, SIDE - 1)
    def _(j):
        for d in range(2):
            for p in range(SUBS):
                gather_step(hbuf, ag1_send, ag1_recv, j, d, p).wait_send()
                gather_step(abuf, ag2_send, ag2_recv, j, d, p).wait_send()
                sum_step(*ring1, j, d, p).wait_send()
                sum_step(*ring2, j, d, p).wait_send()

    sent = UNIT * len(flows) * (SIDE - 1 + PUMPS - SIDE + PUMPS)
    whole = kv.at[pl.ds(0, sent)]
    remote(whole, whole, kv_send.at[0], kv_pair_recv.at[0], pair).wait_send()
    got = kv.at[pl.ds(0, UNIT * len(flows) * PUMPS)]
    remote(got, got, kv_send.at[0], kv_pair_recv.at[0], pair).wait_recv()


def run_layer(hidden, seg, ln_attn, w_query, w_key, w_value, q_gain, k_gain, w_out, ln_mlp, w_gate, w_up, w_down):
    rows, width = hidden.shape
    seq = rows * SIDE
    units = w_gate.shape[1]
    kvw = w_key.shape[1]
    heads_w = w_query.shape[1]
    bf16, f32 = jnp.bfloat16, jnp.float32
    sub = HALF // SUBS
    vmem = pl.BlockSpec(memory_space=pltpu.VMEM)
    hbm = pl.BlockSpec(memory_space=pl.ANY)
    ring = (SIDE - 1, 2, SUBS)
    dma = pltpu.SemaphoreType.DMA
    blocks = pltpu.VMEM(ring + (HALF, width // SUBS), bf16)
    return pl.pallas_call(
        layer_kernel,
        out_shape=(
            jax.ShapeDtypeStruct((rows, width), bf16),
            jax.ShapeDtypeStruct((seg.shape[0] * seq, kvw // HD, 2 * HD), bf16),
            jax.ShapeDtypeStruct((seg.shape[0], HD), jnp.int32),
        ),
        in_specs=[hbm, vmem, vmem, hbm, hbm, hbm, vmem, vmem, hbm, vmem, hbm, hbm, hbm],
        out_specs=(vmem, hbm, vmem),
        scratch_shapes=[
            pltpu.VMEM((SIDE, 2, SUBS, sub, width), bf16),
            pltpu.VMEM((SIDE, 2, SUBS, sub, width), bf16),
            pltpu.VMEM(w_query.shape, bf16),
            pltpu.VMEM(w_key.shape, bf16),
            pltpu.VMEM(w_value.shape, bf16),
            pltpu.VMEM(w_out.shape, bf16),
            pltpu.VMEM(w_gate.shape, bf16),
            pltpu.VMEM(w_up.shape, bf16),
            pltpu.VMEM(w_down.shape, bf16),
            pltpu.VMEM((SIDE, 2, HALF, heads_w), bf16),
            pltpu.VMEM((SIDE, 2, HALF, kvw), bf16),
            pltpu.VMEM((SIDE, 2, HALF, kvw), bf16),
            pltpu.VMEM((seq, kvw // HD, 2 * HD), bf16),
            pltpu.VMEM((SIDE, 2, HALF, heads_w), bf16),
            pltpu.VMEM((rows, units), bf16),
            pltpu.VMEM((rows, units), bf16),
            pltpu.VMEM((SUBS, rows, width // SUBS), f32),
            blocks,
            blocks,
            blocks,
            blocks,
            dma((2 * SUBS + 8,)),
        ]
        + [dma(ring)] * 8
        + [dma((1,)), dma((4, SIDE - 1)), dma((4, PUMPS - SIDE)), dma((1,))],
        compiler_params=pltpu.CompilerParams(
            collective_id=0, has_side_effects=True, vmem_limit_bytes=60 * 1024 * 1024
        ),
        name="layer",
    )(hidden, seg, ln_attn, w_query, w_key, w_value, q_gain, k_gain, w_out, ln_mlp, w_gate, w_up, w_down)


def body(
    hidden_in,
    segment_ids,
    request_prompt,
    page_table,
    ln_attn,
    w_query,
    w_key,
    w_value,
    q_gain,
    k_gain,
    w_out,
    ln_mlp,
    w_gate,
    w_up,
    w_down,
):
    result, everything, bounds = run_layer(
        hidden_in,
        segment_ids,
        ln_attn,
        w_query,
        w_key,
        w_value,
        q_gain,
        k_gain,
        w_out,
        ln_mlp,
        w_gate,
        w_up,
        w_down,
    )
    cache, result = fill_pages(page_table, request_prompt, bounds, result, everything)
    return (result, cache)


def solution(mesh):
    return jax.shard_map(
        body,
        mesh=mesh,
        in_specs=(
            P(("req", "mp"), None),
            P(),
            P("req"),
            P("req", None),
            P(),
            P(None, "mp"),
            P(None, "mp"),
            P(None, "mp"),
            P(),
            P(),
            P("mp", None),
            P(),
            P(None, "mp"),
            P(None, "mp"),
            P("mp", None),
        ),
        out_specs=(P(("req", "mp"), None), P("req", None, "mp", None)),
        check_vma=False,
    )
```

```python
import math

import jax
import jax.numpy as jnp
from jax import lax
from jax.experimental import pallas as pl
from jax.experimental.pallas import tpu as pltpu
from jax.sharding import PartitionSpec as P

HD = 128
PROMPTS_DEV = 3
PAGE = 16


EPS = 1e-06
THETA = 1000000.0


SLOTS = 16
AHEAD = 12


def fill_kernel(
    table_hbm, prompt_hbm, bounds_hbm, layer_hbm, rows_ref, out_ref, layer_out, table, prompt, bounds, held, slots,
    zeros, small_sem, in_sem, out_sem,
):
    most, requests = table.shape
    span = most * PAGE
    last = rows_ref.shape[0] - span
    seq = rows_ref.shape[0] // bounds.shape[0]
    smalls = [
        pltpu.make_async_copy(src, dst, small_sem.at[n])
        for n, (src, dst) in enumerate(
            ((table_hbm, table), (prompt_hbm, prompt), (bounds_hbm, bounds), (layer_hbm, held))
        )
    ]
    layer_copy = pltpu.make_async_copy(held, layer_out, small_sem.at[4])
    for small in smalls:
        small.start()
    zeros[...] = jnp.zeros_like(zeros)
    for small in smalls:
        small.wait()
    layer_copy.start()

    def place(r):
        p = prompt[r]
        g = p // PROMPTS_DEV
        s = p - g * PROMPTS_DEV
        low = jnp.where(s == 0, 0, jnp.where(s == 1, bounds[g, 0], bounds[g, 1]))
        high = jnp.where(s == 0, bounds[g, 0], jnp.where(s == 1, bounds[g, 1], seq))
        begin = g * seq + low
        return begin, high - low, jnp.minimum(begin, last)

    def fetch(r, slot):
        at = place(r)[2]
        return pltpu.make_async_copy(
            rows_ref.at[pl.ds(at, span)], slots.at[slot, pl.ds(0, span)], in_sem.at[slot]
        )

    def drain(slot):
        pltpu.make_async_copy(
            out_ref.at[pl.ds(0, most)], out_ref.at[pl.ds(0, most)], out_sem.at[slot]
        ).wait()

    for r in range(min(AHEAD, requests)):
        fetch(r, r).start()

    @pl.loop(0, requests)
    def _(r):
        slot = lax.rem(r, SLOTS)
        fetch(r, slot).wait()
        begin, length, at = place(r)
        shift = begin - at
        full = length // PAGE
        rest = length - full * PAGE

        @pl.when(rest > 0)
        def _():
            edge = shift + full * PAGE
            tail = slots[slot, pl.ds(edge, PAGE)]
            row = lax.broadcasted_iota(jnp.int32, tail.shape, 0)
            slots[slot, pl.ds(edge, PAGE)] = jnp.where(row < rest, tail, jnp.zeros_like(tail))

        for e in range(most):
            page = table[e, r]

            @pl.when(e * PAGE < length)
            def _():
                pltpu.make_async_copy(
                    slots.at[slot, pl.ds(shift + e * PAGE, PAGE)], out_ref.at[page], out_sem.at[slot]
                ).start()

            @pl.when(e * PAGE >= length)
            def _():
                pltpu.make_async_copy(zeros, out_ref.at[page], out_sem.at[slot]).start()

        @pl.when(r + AHEAD < requests)
        def _():
            other = lax.rem(r + AHEAD, SLOTS)

            @pl.when(r + AHEAD >= SLOTS)
            def _():
                drain(other)

            fetch(r + AHEAD, other).start()

    for r in range(max(0, requests - SLOTS), requests):
        drain(r % SLOTS)
    layer_copy.wait()


def fill_pages(page_table, request_prompt, bounds, layer, rows):
    requests, most = page_table.shape
    unit = rows.shape[1:]
    hbm = pl.BlockSpec(memory_space=pl.ANY)
    return pl.pallas_call(
        fill_kernel,
        out_shape=(
            jax.ShapeDtypeStruct((requests * most, PAGE) + unit, rows.dtype),
            jax.ShapeDtypeStruct(layer.shape, layer.dtype),
        ),
        in_specs=[hbm] * 5,
        out_specs=(hbm, hbm),
        scratch_shapes=[
            pltpu.SMEM((most, requests), jnp.int32),
            pltpu.SMEM((requests,), jnp.int32),
            pltpu.SMEM(bounds.shape, jnp.int32),
            pltpu.VMEM(layer.shape, layer.dtype),
            pltpu.VMEM((SLOTS, (most + 1) * PAGE) + unit, rows.dtype),
            pltpu.VMEM((PAGE,) + unit, rows.dtype),
            pltpu.SemaphoreType.DMA((5,)),
            pltpu.SemaphoreType.DMA((SLOTS,)),
            pltpu.SemaphoreType.DMA((SLOTS,)),
        ],
        name="fill_pages",
    )(page_table.T, request_prompt, bounds, layer, rows)


MESH = pl.DeviceIdType.MESH
HALF = 64
SUBS = 2
SIDE = 4
UNIT = 128
PUMPS = SIDE * SIDE


def rms(wide, gain):
    return wide * lax.rsqrt(jnp.mean(wide * wide, axis=-1, keepdims=True) + EPS) * gain


def layer_kernel(
    hidden,
    seg,
    ln_attn,
    w_query,
    w_key,
    w_value,
    q_gain,
    k_gain,
    w_out,
    ln_mlp,
    w_gate,
    w_up,
    w_down,
    out,
    kv,
    bounds,
    hbuf,
    abuf,
    wq,
    wk,
    wv,
    wo,
    wg,
    wu,
    wd,
    qbuf,
    kbuf,
    vbuf,
    kvbuf,
    attbuf,
    actbuf,
    ownbuf,
    send2f,
    wfull,
    att_in,
    relay,
    send2,
    recv2,
    local_sem,
    ag1_send,
    ag1_recv,
    wx_send,
    wx_recv,
    a_send,
    a_recv,
    w_send,
    w1_recv,
    w2_recv,
    w_pair_recv,
    ag2_send,
    ag2_recv,
    rs2_send,
    rs2_recv,
    kv_send,
    kv1_recv,
    kv2_recv,
    kv_pair_recv,
):
    x = lax.axis_index("mp")
    c = lax.axis_index("req")
    core = lax.rem(c, 2)
    z = lax.rem(c // 2, SIDE)
    y = c // (2 * SIDE)
    width = hidden.shape[1]
    rows = hidden.shape[0]
    sub = HALF // SUBS

    def turn(value):
        return lax.rem(value + 2 * SIDE, SIDE)

    def req_of(yy, zz, cc):
        return (yy * SIDE + zz) * 2 + cc

    x_near = ((c, turn(x + 1)), (c, turn(x - 1)))
    pair = (req_of(y, z, 1 - core), x)
    y_near = ((req_of(turn(y + 1), z, core), x), (req_of(turn(y - 1), z, core), x))
    z_near = ((req_of(y, turn(z + 1), core), x), (req_of(y, turn(z - 1), core), x))

    moves = []
    weights = ((w_query, wq), (w_key, wk), (w_value, wv), (w_out, wo), (w_gate, wg), (w_up, wu), (w_down, wd))
    for d in range(2):
        for p in range(SUBS):
            moves.append(
                pltpu.make_async_copy(
                    hidden.at[pl.ds(d * HALF + p * sub, sub)], hbuf.at[x, d, p], local_sem.at[d * SUBS + p]
                )
            )
    for n, (src, dst) in enumerate(weights):
        moves.append(pltpu.make_async_copy(src, dst, local_sem.at[2 * SUBS + n]))
    for move in moves:
        move.start()

    barrier = pltpu.get_barrier_semaphore()
    peers = x_near + y_near + z_near + (pair, (c, turn(x + 2)))
    for near in peers:
        pl.semaphore_signal(barrier, inc=1, device_id=near, device_id_type=MESH)
    pl.semaphore_wait(barrier, len(peers))

    def remote(src, dst, send, recv, near):
        return pltpu.make_async_remote_copy(
            src_ref=src, dst_ref=dst, send_sem=send, recv_sem=recv, device_id=near, device_id_type=MESH
        )

    def gather_step(buf, send, recv, j, d, p):
        block = buf.at[turn(x - j) if d == 0 else turn(x + j), d, p]
        return remote(block, block, send.at[j, d, p], recv.at[j, d, p], x_near[d])

    def gather_advance(buf, send, recv, j, p):
        for d in range(2):
            gather_step(buf, send, recv, j - 1, d, p).wait_recv()

            @pl.when(j < SIDE - 1)
            def _():
                gather_step(buf, send, recv, j, d, p).start()

    def ring_rows(buf, j):
        a, b = turn(x - j), turn(x + j)
        upper = buf[a, 0].reshape(HALF, width)
        lower = buf[b, 1].reshape(HALF, width)
        return jnp.concatenate([upper, lower], axis=0).astype(jnp.float32)

    deep = wfull.shape[4]

    def out_exchange(k):
        return remote(
            w_out.at[pl.ds(c * deep, deep)],
            wfull.at[k - 1, y, z, core],
            wx_send.at[k - 1],
            wx_recv.at[k - 1],
            (c, turn(x - k)),
        )

    for k in (2, 1, 3):
        out_exchange(k).start()
    for p in range(SUBS):
        for d in range(2):
            own = hidden.at[pl.ds(d * HALF + p * sub, sub)]
            remote(own, hbuf.at[x, d, p], ag1_send.at[0, d, p], ag1_recv.at[0, d, p], x_near[d]).start()

    def below(table, bound):
        return jnp.sum((table < bound).astype(jnp.int32), axis=1, keepdims=True)

    seg_row = seg[pl.ds(c, 1), :]
    first1, first2 = below(seg_row, 1), below(seg_row, 2)
    place = lax.broadcasted_iota(jnp.int32, bounds.shape, 1)
    bounds[...] = jnp.where(place == 0, below(seg[...], 1), below(seg[...], 2))

    def begin_of(token):
        return jnp.where(token >= first2, first2, jnp.where(token >= first1, first1, 0))

    lane = lax.broadcasted_iota(jnp.int32, (1, HD), 1)
    freq = jnp.exp2(lax.rem(lane, HD // 2).astype(jnp.float32) * (-2.0 * math.log2(THETA) / HD))
    sign = jnp.where(lane < HD // 2, -1.0, 1.0)
    gain_attn, gain_mlp, gain_q, gain_k = (
        gain[...].astype(jnp.float32).reshape(1, -1) for gain in (ln_attn, ln_mlp, q_gain, k_gain)
    )
    heads = wq.shape[1] // HD
    kv_heads = wk.shape[1] // HD
    group = heads // kv_heads

    flows = ((0, 0), (0, 1), (1, 0), (1, 1))

    def make_pump(block_of, send, recv1, recv2, pair_recv):
        def pump(p):
            b, k = lax.rem(p, SIDE), p // SIDE
            for f, (axis, d) in enumerate(flows):
                step = 1 if d == 0 else -1
                first = y_near[d] if axis == 0 else z_near[d]
                second = z_near[d] if axis == 0 else y_near[d]
                if axis == 0:
                    block = block_of(f, turn(y - step * b), turn(z - step * k))
                else:
                    block = block_of(f, turn(y - step * k), turn(z - step * b))

                @pl.when((p >= 1) & (p < SIDE))
                def _():
                    remote(block, block, send.at[0], recv1.at[f, p - 1], first).wait_recv()

                @pl.when(p >= SIDE)
                def _():
                    remote(block, block, send.at[1], recv2.at[f, p - SIDE], second).wait_recv()

                @pl.when(p < SIDE - 1)
                def _():
                    remote(block, block, send.at[0], recv1.at[f, p], first).start()

                @pl.when(p < PUMPS - SIDE)
                def _():
                    remote(block, block, send.at[1], recv2.at[f, p], second).start()

                remote(block, block, send.at[2], pair_recv.at[0], pair).start()

        return pump

    seq = SIDE * rows
    strip = width // len(flows)

    def kv_block(f, oy, oz):
        return kv.at[pl.ds(pl.multiple_of(req_of(oy, oz, core) * seq + f * UNIT, UNIT), UNIT)]

    def w_block(f, oy, oz):
        return wfull.at[:, oy, oz, core, :, pl.ds(f * strip, strip)]

    pump = make_pump(kv_block, kv_send, kv1_recv, kv2_recv, kv_pair_recv)
    w_pump = make_pump(w_block, w_send, w1_recv, w2_recv, w_pair_recv)

    def settle(send, pair_recv, first, second, last):
        remote(first, first, send.at[0], pair_recv.at[0], pair).wait_send()
        remote(second, second, send.at[1], pair_recv.at[0], pair).wait_send()
        remote(last, last, send.at[2], pair_recv.at[0], pair).wait_send()

    for move in moves[: 2 * SUBS + 3]:
        move.wait()

    @pl.loop(0, SIDE)
    def _(j):
        @pl.when(j > 0)
        def _():
            for p in range(SUBS):
                gather_advance(hbuf, ag1_send, ag1_recv, j, p)
                w_pump(3 * j - 2 + p)

        a, b = turn(x - j), turn(x + j)
        normed = rms(ring_rows(hbuf, j), gain_attn).astype(jnp.bfloat16)
        row = lax.broadcasted_iota(jnp.int32, (rows, 1), 0)
        token = jnp.where(row < HALF, a, b) * rows + row
        angle = (token - begin_of(token)).astype(jnp.float32) * freq
        cosine = jnp.cos(angle)
        sine = jnp.sin(angle) * sign

        def turned(values, gain):
            scaled = rms(values, gain)
            return (scaled * cosine + pltpu.roll(scaled, HD // 2, 1) * sine).astype(jnp.bfloat16)

        query = jnp.dot(normed, wq[...], preferred_element_type=jnp.float32)
        key = jnp.dot(normed, wk[...], preferred_element_type=jnp.float32)
        value = jnp.dot(normed, wv[...], preferred_element_type=jnp.float32).astype(jnp.bfloat16)
        for h in range(heads):
            part = turned(query[:, h * HD : (h + 1) * HD], gain_q)
            qbuf[a, 0, :, h * HD : (h + 1) * HD] = part[:HALF]
            qbuf[b, 1, :, h * HD : (h + 1) * HD] = part[HALF:]
        for h in range(kv_heads):
            part = turned(key[:, h * HD : (h + 1) * HD], gain_k)
            mine = value[:, h * HD : (h + 1) * HD]
            kbuf[a, 0, :, h * HD : (h + 1) * HD] = part[:HALF]
            kbuf[b, 1, :, h * HD : (h + 1) * HD] = part[HALF:]
            both = jnp.concatenate([part, mine], axis=1)
            kvbuf[pl.ds(a * rows, HALF), h, :] = both[:HALF]
            kvbuf[pl.ds(b * rows + HALF, HALF), h, :] = both[HALF:]
        vbuf[a, 0] = value[:HALF]
        vbuf[b, 1] = value[HALF:]

        @pl.when(j == 0)
        def _():
            for k in (1, 3, 2):
                out_exchange(k).wait_recv()

        w_pump(3 * j)

    kv_own = pltpu.make_async_copy(kvbuf, kv.at[pl.ds(c * seq, seq)], local_sem.at[2 * SUBS + len(weights)])
    kv_own.start()

    w_pump(jnp.int32(3 * SIDE - 2))
    w_pump(jnp.int32(3 * SIDE - 1))
    kv_own.wait()
    pump(jnp.int32(0))

    def a_copy(n, src, dst, near):
        return remote(src, dst, a_send.at[n], a_recv.at[n], near)

    def head_copy(n, i=0):
        if n < 2:
            return a_copy(n, attbuf.at[i], att_in.at[2 - 2 * n], x_near[n])
        return a_copy(n, attbuf.at[i, n - 2], relay.at[n - 2], x_near[n - 2])

    relays = (
        a_copy(4, relay.at[0], att_in.at[1, 0], x_near[0]),
        a_copy(5, relay.at[1], att_in.at[1, 1], x_near[1]),
    )

    keys = kbuf[...].reshape(seq, kv_heads * HD)
    values = vbuf[...].reshape(seq, kv_heads * HD)
    for i in range(SIDE):
        extent = (i + 1) * rows
        token = lax.broadcasted_iota(jnp.int32, (rows, extent), 0) + i * rows
        other = lax.broadcasted_iota(jnp.int32, (rows, extent), 1)
        allowed = (other <= token) & (other >= begin_of(token[:, :1]))
        allowed = jnp.concatenate([allowed.astype(jnp.float32)] * group, axis=0) > 0.5
        block = qbuf[i].reshape(rows, heads * HD)
        for n in range(kv_heads):
            stacked = jnp.concatenate(
                [block[:, (n * group + h) * HD : (n * group + h + 1) * HD] for h in range(group)], axis=0
            )
            scores = lax.dot_general(
                stacked,
                keys[:extent, n * HD : (n + 1) * HD],
                (((1,), (1,)), ((), ())),
                preferred_element_type=jnp.float32,
            )
            raised = jnp.where(allowed, jnp.exp(scores * (1.0 / math.sqrt(HD))), 0.0)
            share = (raised * (1.0 / jnp.sum(raised, axis=-1, keepdims=True))).astype(jnp.bfloat16)
            mixed = jnp.dot(
                share, values[:extent, n * HD : (n + 1) * HD], preferred_element_type=jnp.float32
            ).astype(jnp.bfloat16)
            for h in range(group):
                at = (n * group + h) * HD
                attbuf[i, 0, :, at : at + HD] = mixed[h * rows : h * rows + HALF]
                attbuf[i, 1, :, at : at + HD] = mixed[h * rows + HALF : (h + 1) * rows]
        ahead = turn(i - x)

        @pl.when(ahead == 1)
        def _():
            head_copy(0, i).start()

        @pl.when(ahead == SIDE - 1)
        def _():
            head_copy(1, i).start()

        @pl.when(ahead == 2)
        def _():
            head_copy(2, i).start()
            head_copy(3, i).start()

        w_pump(jnp.int32(3 * SIDE + i))
    piece = width // SUBS

    def sum_step(send_buf, recv_buf, send, recv, j, d, n):
        return remote(send_buf.at[j, d, n], recv_buf.at[j, d, n], send.at[j, d, n], recv.at[j, d, n], x_near[d])

    def add_arrived(part, send_buf, recv_buf, send, recv, j, n):
        for d in range(2):
            sum_step(send_buf, recv_buf, send, recv, j, d, n).wait_recv()
        return part + jnp.concatenate([recv_buf[j, 0, n], recv_buf[j, 1, n]], axis=0).astype(jnp.float32)

    def send_on(part, send_buf, recv_buf, send, recv, j, n):
        rounded = part.astype(jnp.bfloat16)
        for d in range(2):
            send_buf[j, d, n] = rounded[d * HALF : (d + 1) * HALF]
            sum_step(send_buf, recv_buf, send, recv, j, d, n).start()

    ring2 = (send2, recv2, rs2_send, rs2_recv)

    def add_heads(mixed, weight, n):
        send2f[n] += jnp.dot(mixed, weight, preferred_element_type=jnp.float32)

    def add_source(k):
        mixed = att_in[k - 1].reshape(rows, att_in.shape[3])
        for n in range(SUBS):
            weight = wfull[k - 1, :, :, :, :, n * piece : (n + 1) * piece].reshape(att_in.shape[3], piece)
            add_heads(mixed, weight, n)

    moves[2 * SUBS + 3].wait()
    for n, move in enumerate(relays):
        head_copy(2 + n).wait_recv()
        move.start()
    mixed = attbuf[x].reshape(rows, heads * HD)
    for n in range(SUBS):
        columns = slice(n * piece, (n + 1) * piece)
        before = [hbuf[x, d, :, :, columns].reshape(HALF, piece) for d in range(2)]
        send2f[n] = jnp.concatenate(before, axis=0).astype(jnp.float32)
        add_heads(mixed, wo[:, columns], n)
    half = wfull.at[:, :, :, 0]
    remote(half, half, w_send.at[2], w_pair_recv.at[0], pair).wait_recv()
    head_copy(1).wait_recv()
    add_source(1)
    head_copy(0).wait_recv()
    add_source(3)
    for move in relays:
        move.wait_recv()
    add_source(2)
    for n in range(SUBS):
        total = send2f[n].astype(jnp.bfloat16)
        for d in range(2):
            abuf[x, d, :, :, n * piece : (n + 1) * piece] = total[d * HALF : (d + 1) * HALF].reshape(SUBS, sub, piece)
    for p in range(SUBS):
        for d in range(2):
            gather_step(abuf, ag2_send, ag2_recv, 0, d, p).start()
    pump(jnp.int32(1))

    for move in moves[2 * SUBS + 4 :]:
        move.wait()

    def activation(j):
        normed = rms(ring_rows(abuf, j), gain_mlp).astype(jnp.bfloat16)
        gate = jnp.dot(normed, wg[...], preferred_element_type=jnp.float32)
        upper = jnp.dot(normed, wu[...], preferred_element_type=jnp.float32)
        return (gate * jax.nn.sigmoid(gate) * upper).astype(jnp.bfloat16)

    def down_part(act, n):
        return jnp.dot(act, wd[:, n * piece : (n + 1) * piece], preferred_element_type=jnp.float32)

    @pl.loop(0, SIDE)
    def _(j):
        @pl.when(j > 0)
        def _():
            for p in range(SUBS):
                gather_advance(abuf, ag2_send, ag2_recv, j, p)
                pump(4 * j - 1 + p)

        actbuf[...] = activation(j)

        @pl.when(j > 0)
        def _():
            pump(4 * j + 1)

        @pl.when(j > 0)
        def _():
            act = actbuf[...]
            for n in range(SUBS):
                part = down_part(act, n)
                send2f[n] = part

                @pl.when(j > 1)
                def _():
                    send2f[n] = add_arrived(send2f[n], *ring2, j - 2, n)

                send_on(send2f[n], *ring2, j - 1, n)

        @pl.when(j == 0)
        def _():
            ownbuf[...] = actbuf[...]

        pump(4 * j + 2)

    act = ownbuf[...]
    pump(jnp.int32(PUMPS - 1))
    for n in range(SUBS):
        part = add_arrived(down_part(act, n), *ring2, SIDE - 2, n)
        for d in range(2):
            before = abuf[x, d, :, :, n * piece : (n + 1) * piece].reshape(HALF, piece).astype(jnp.float32)
            total = before + part[d * HALF : (d + 1) * HALF]
            out[d * HALF : (d + 1) * HALF, n * piece : (n + 1) * piece] = total.astype(jnp.bfloat16)

    @pl.loop(0, SIDE - 1)
    def _(j):
        for d in range(2):
            for p in range(SUBS):
                gather_step(hbuf, ag1_send, ag1_recv, j, d, p).wait_send()
                gather_step(abuf, ag2_send, ag2_recv, j, d, p).wait_send()
                sum_step(*ring2, j, d, p).wait_send()

    for k in range(1, SIDE):
        out_exchange(k).wait_send()
    for n in range(4):
        head_copy(n).wait_send()
    for move in relays:
        move.wait_send()
    settle(
        w_send, w_pair_recv, wfull.at[:, 0, pl.ds(0, SIDE - 1), 0], wfull.at[:, pl.ds(0, SIDE - 1), :, 0], half
    )
    settle(
        kv_send,
        kv_pair_recv,
        kv.at[pl.ds(0, UNIT * len(flows) * (SIDE - 1))],
        kv.at[pl.ds(0, UNIT * len(flows) * (PUMPS - SIDE))],
        kv.at[pl.ds(0, UNIT * len(flows) * PUMPS)],
    )
    got = kv.at[pl.ds(0, UNIT * len(flows) * PUMPS)]
    remote(got, got, kv_send.at[2], kv_pair_recv.at[0], pair).wait_recv()


def run_layer(hidden, seg, ln_attn, w_query, w_key, w_value, q_gain, k_gain, w_out, ln_mlp, w_gate, w_up, w_down):
    rows, width = hidden.shape
    seq = rows * SIDE
    units = w_gate.shape[1]
    kvw = w_key.shape[1]
    heads_w = w_query.shape[1]
    bf16, f32 = jnp.bfloat16, jnp.float32
    sub = HALF // SUBS
    vmem = pl.BlockSpec(memory_space=pltpu.VMEM)
    hbm = pl.BlockSpec(memory_space=pl.ANY)
    ring = (SIDE - 1, 2, SUBS)
    dma = pltpu.SemaphoreType.DMA
    gather_sems = [dma((3,)), dma((4, SIDE - 1)), dma((4, PUMPS - SIDE)), dma((1,))]
    blocks = pltpu.VMEM(ring + (HALF, width // SUBS), bf16)
    return pl.pallas_call(
        layer_kernel,
        out_shape=(
            jax.ShapeDtypeStruct((rows, width), bf16),
            jax.ShapeDtypeStruct((seg.shape[0] * seq, kvw // HD, 2 * HD), bf16),
            jax.ShapeDtypeStruct((seg.shape[0], HD), jnp.int32),
        ),
        in_specs=[hbm, vmem, vmem, hbm, hbm, hbm, vmem, vmem, hbm, vmem, hbm, hbm, hbm],
        out_specs=(vmem, hbm, vmem),
        scratch_shapes=[
            pltpu.VMEM((SIDE, 2, SUBS, sub, width), bf16),
            pltpu.VMEM((SIDE, 2, SUBS, sub, width), bf16),
            pltpu.VMEM(w_query.shape, bf16),
            pltpu.VMEM(w_key.shape, bf16),
            pltpu.VMEM(w_value.shape, bf16),
            pltpu.VMEM(w_out.shape, bf16),
            pltpu.VMEM(w_gate.shape, bf16),
            pltpu.VMEM(w_up.shape, bf16),
            pltpu.VMEM(w_down.shape, bf16),
            pltpu.VMEM((SIDE, 2, HALF, heads_w), bf16),
            pltpu.VMEM((SIDE, 2, HALF, kvw), bf16),
            pltpu.VMEM((SIDE, 2, HALF, kvw), bf16),
            pltpu.VMEM((seq, kvw // HD, 2 * HD), bf16),
            pltpu.VMEM((SIDE, 2, HALF, heads_w), bf16),
            pltpu.VMEM((rows, units), bf16),
            pltpu.VMEM((rows, units), bf16),
            pltpu.VMEM((SUBS, rows, width // SUBS), f32),
            pltpu.VMEM((SIDE - 1, SIDE, SIDE, 2, w_out.shape[0] // seg.shape[0], width), bf16),
            pltpu.VMEM((SIDE - 1, 2, HALF, heads_w), bf16),
            pltpu.VMEM((2, HALF, heads_w), bf16),
            blocks,
            blocks,
            dma((2 * SUBS + 8,)),
            dma(ring),
            dma(ring),
            dma((SIDE - 1,)),
            dma((SIDE - 1,)),
            dma((6,)),
            dma((6,)),
        ]
        + gather_sems
        + [dma(ring)] * 4
        + gather_sems,
        compiler_params=pltpu.CompilerParams(
            collective_id=0, has_side_effects=True, vmem_limit_bytes=60 * 1024 * 1024
        ),
        name="layer",
    )(hidden, seg, ln_attn, w_query, w_key, w_value, q_gain, k_gain, w_out, ln_mlp, w_gate, w_up, w_down)


def body(
    hidden_in,
    segment_ids,
    request_prompt,
    page_table,
    ln_attn,
    w_query,
    w_key,
    w_value,
    q_gain,
    k_gain,
    w_out,
    ln_mlp,
    w_gate,
    w_up,
    w_down,
):
    result, everything, bounds = run_layer(
        hidden_in,
        segment_ids,
        ln_attn,
        w_query,
        w_key,
        w_value,
        q_gain,
        k_gain,
        w_out,
        ln_mlp,
        w_gate,
        w_up,
        w_down,
    )
    cache, result = fill_pages(page_table, request_prompt, bounds, result, everything)
    return (result, cache)


def solution(mesh):
    return jax.shard_map(
        body,
        mesh=mesh,
        in_specs=(
            P(("req", "mp"), None),
            P(),
            P("req"),
            P("req", None),
            P(),
            P(None, "mp"),
            P(None, "mp"),
            P(None, "mp"),
            P(),
            P(),
            P("mp", None),
            P(),
            P(None, "mp"),
            P(None, "mp"),
            P("mp", None),
        ),
        out_specs=(P(("req", "mp"), None), P("req", None, "mp", None)),
        check_vma=False,
    )
```

```python
import math

import jax
import jax.numpy as jnp
from jax import lax
from jax.experimental import pallas as pl
from jax.experimental.pallas import tpu as pltpu
from jax.sharding import PartitionSpec as P

HD = 128
PROMPTS_DEV = 3
PAGE = 16


EPS = 1e-06
THETA = 1000000.0


SLOTS = 16
AHEAD = 12


def fill_kernel(
    table_hbm, prompt_hbm, bounds_hbm, layer_hbm, rows_ref, out_ref, layer_out, table, prompt, bounds, held, slots,
    zeros, small_sem, in_sem, out_sem,
):
    most, requests = table.shape
    span = most * PAGE
    last = rows_ref.shape[0] - span
    seq = rows_ref.shape[0] // bounds.shape[0]
    smalls = [
        pltpu.make_async_copy(src, dst, small_sem.at[n])
        for n, (src, dst) in enumerate(
            ((table_hbm, table), (prompt_hbm, prompt), (bounds_hbm, bounds), (layer_hbm, held))
        )
    ]
    layer_copy = pltpu.make_async_copy(held, layer_out, small_sem.at[4])
    for small in smalls:
        small.start()
    zeros[...] = jnp.zeros_like(zeros)
    for small in smalls:
        small.wait()
    layer_copy.start()

    def place(r):
        p = prompt[r]
        g = p // PROMPTS_DEV
        s = p - g * PROMPTS_DEV
        low = jnp.where(s == 0, 0, jnp.where(s == 1, bounds[g, 0], bounds[g, 1]))
        high = jnp.where(s == 0, bounds[g, 0], jnp.where(s == 1, bounds[g, 1], seq))
        begin = g * seq + low
        return begin, high - low, jnp.minimum(begin, last)

    def fetch(r, slot):
        at = place(r)[2]
        return pltpu.make_async_copy(
            rows_ref.at[pl.ds(at, span)], slots.at[slot, pl.ds(0, span)], in_sem.at[slot]
        )

    def drain(slot):
        pltpu.make_async_copy(
            out_ref.at[pl.ds(0, most)], out_ref.at[pl.ds(0, most)], out_sem.at[slot]
        ).wait()

    for r in range(min(AHEAD, requests)):
        fetch(r, r).start()

    @pl.loop(0, requests)
    def _(r):
        slot = lax.rem(r, SLOTS)
        fetch(r, slot).wait()
        begin, length, at = place(r)
        shift = begin - at
        full = length // PAGE
        rest = length - full * PAGE

        @pl.when(rest > 0)
        def _():
            edge = shift + full * PAGE
            tail = slots[slot, pl.ds(edge, PAGE)]
            row = lax.broadcasted_iota(jnp.int32, tail.shape, 0)
            slots[slot, pl.ds(edge, PAGE)] = jnp.where(row < rest, tail, jnp.zeros_like(tail))

        for e in range(most):
            page = table[e, r]

            @pl.when(e * PAGE < length)
            def _():
                pltpu.make_async_copy(
                    slots.at[slot, pl.ds(shift + e * PAGE, PAGE)], out_ref.at[page], out_sem.at[slot]
                ).start()

            @pl.when(e * PAGE >= length)
            def _():
                pltpu.make_async_copy(zeros, out_ref.at[page], out_sem.at[slot]).start()

        @pl.when(r + AHEAD < requests)
        def _():
            other = lax.rem(r + AHEAD, SLOTS)

            @pl.when(r + AHEAD >= SLOTS)
            def _():
                drain(other)

            fetch(r + AHEAD, other).start()

    for r in range(max(0, requests - SLOTS), requests):
        drain(r % SLOTS)
    layer_copy.wait()


def fill_pages(page_table, request_prompt, bounds, layer, rows):
    requests, most = page_table.shape
    unit = rows.shape[1:]
    hbm = pl.BlockSpec(memory_space=pl.ANY)
    return pl.pallas_call(
        fill_kernel,
        out_shape=(
            jax.ShapeDtypeStruct((requests * most, PAGE) + unit, rows.dtype),
            jax.ShapeDtypeStruct(layer.shape, layer.dtype),
        ),
        in_specs=[hbm] * 5,
        out_specs=(hbm, hbm),
        scratch_shapes=[
            pltpu.SMEM((most, requests), jnp.int32),
            pltpu.SMEM((requests,), jnp.int32),
            pltpu.SMEM(bounds.shape, jnp.int32),
            pltpu.VMEM(layer.shape, layer.dtype),
            pltpu.VMEM((SLOTS, (most + 1) * PAGE) + unit, rows.dtype),
            pltpu.VMEM((PAGE,) + unit, rows.dtype),
            pltpu.SemaphoreType.DMA((5,)),
            pltpu.SemaphoreType.DMA((SLOTS,)),
            pltpu.SemaphoreType.DMA((SLOTS,)),
        ],
        name="fill_pages",
    )(page_table.T, request_prompt, bounds, layer, rows)


MESH = pl.DeviceIdType.MESH
HALF = 64
SUBS = 2
SIDE = 4
PUMPS = SIDE * SIDE


def rms(wide, gain):
    return wide * lax.rsqrt(jnp.mean(wide * wide, axis=-1, keepdims=True) + EPS) * gain


def layer_kernel(
    hidden,
    seg,
    ln_attn,
    w_query,
    w_key,
    w_value,
    q_gain,
    k_gain,
    w_out,
    ln_mlp,
    w_gate,
    w_up,
    w_down,
    out,
    kv,
    bounds,
    hbuf,
    abuf,
    wq,
    wk,
    wv,
    wo,
    wg,
    wu,
    wd,
    qbuf,
    kbuf,
    vbuf,
    kvbuf,
    attbuf,
    actbuf,
    ownbuf,
    send2f,
    wfull,
    att_in,
    relay,
    send2,
    recv2,
    local_sem,
    ag1_send,
    ag1_recv,
    wx_send,
    wx_recv,
    a_send,
    a_recv,
    w_send,
    w1_recv,
    w2_recv,
    w_pair_recv,
    ag2_send,
    ag2_recv,
    rs2_send,
    rs2_recv,
    kv_send_a,
    kv1_recv_a,
    kv2_recv_a,
    kv_pair_recv_a,
    kv_send_b,
    kv1_recv_b,
    kv2_recv_b,
    kv_pair_recv_b,
):
    x = lax.axis_index("mp")
    c = lax.axis_index("req")
    core = lax.rem(c, 2)
    z = lax.rem(c // 2, SIDE)
    y = c // (2 * SIDE)
    width = hidden.shape[1]
    rows = hidden.shape[0]
    sub = HALF // SUBS

    def turn(value):
        return lax.rem(value + 2 * SIDE, SIDE)

    def req_of(yy, zz, cc):
        return (yy * SIDE + zz) * 2 + cc

    x_near = ((c, turn(x + 1)), (c, turn(x - 1)))
    pair = (req_of(y, z, 1 - core), x)
    y_near = ((req_of(turn(y + 1), z, core), x), (req_of(turn(y - 1), z, core), x))
    z_near = ((req_of(y, turn(z + 1), core), x), (req_of(y, turn(z - 1), core), x))

    moves = []
    weights = ((w_query, wq), (w_key, wk), (w_value, wv), (w_out, wo), (w_gate, wg), (w_up, wu), (w_down, wd))
    for d in range(2):
        for p in range(SUBS):
            moves.append(
                pltpu.make_async_copy(
                    hidden.at[pl.ds(d * HALF + p * sub, sub)], hbuf.at[x, d, p], local_sem.at[d * SUBS + p]
                )
            )
    for n, (src, dst) in enumerate(weights):
        moves.append(pltpu.make_async_copy(src, dst, local_sem.at[2 * SUBS + n]))
    for move in moves:
        move.start()

    barrier = pltpu.get_barrier_semaphore()
    peers = x_near + y_near + z_near + (pair, (c, turn(x + 2)))
    for near in peers:
        pl.semaphore_signal(barrier, inc=1, device_id=near, device_id_type=MESH)
    pl.semaphore_wait(barrier, len(peers))

    def remote(src, dst, send, recv, near):
        return pltpu.make_async_remote_copy(
            src_ref=src, dst_ref=dst, send_sem=send, recv_sem=recv, device_id=near, device_id_type=MESH
        )

    def gather_step(buf, send, recv, j, d, p):
        block = buf.at[turn(x - j) if d == 0 else turn(x + j), d, p]
        return remote(block, block, send.at[j, d, p], recv.at[j, d, p], x_near[d])

    def gather_advance(buf, send, recv, j, p):
        for d in range(2):
            gather_step(buf, send, recv, j - 1, d, p).wait_recv()

            @pl.when(j < SIDE - 1)
            def _():
                gather_step(buf, send, recv, j, d, p).start()

    def ring_rows(buf, j):
        a, b = turn(x - j), turn(x + j)
        upper = buf[a, 0].reshape(HALF, width)
        lower = buf[b, 1].reshape(HALF, width)
        return jnp.concatenate([upper, lower], axis=0).astype(jnp.float32)

    deep = wfull.shape[4]

    def out_exchange(k):
        return remote(
            w_out.at[pl.ds(c * deep, deep)],
            wfull.at[k - 1, y, z, core],
            wx_send.at[k - 1],
            wx_recv.at[k - 1],
            (c, turn(x - k)),
        )

    for k in (2, 1, 3):
        out_exchange(k).start()
    for p in range(SUBS):
        for d in range(2):
            own = hidden.at[pl.ds(d * HALF + p * sub, sub)]
            remote(own, hbuf.at[x, d, p], ag1_send.at[0, d, p], ag1_recv.at[0, d, p], x_near[d]).start()

    def below(table, bound):
        return jnp.sum((table < bound).astype(jnp.int32), axis=1, keepdims=True)

    seg_row = seg[pl.ds(c, 1), :]
    first1, first2 = below(seg_row, 1), below(seg_row, 2)
    place = lax.broadcasted_iota(jnp.int32, bounds.shape, 1)
    bounds[...] = jnp.where(place == 0, below(seg[...], 1), below(seg[...], 2))

    def begin_of(token):
        return jnp.where(token >= first2, first2, jnp.where(token >= first1, first1, 0))

    lane = lax.broadcasted_iota(jnp.int32, (1, HD), 1)
    freq = jnp.exp2(lax.rem(lane, HD // 2).astype(jnp.float32) * (-2.0 * math.log2(THETA) / HD))
    sign = jnp.where(lane < HD // 2, -1.0, 1.0)
    gain_attn, gain_mlp, gain_q, gain_k = (
        gain[...].astype(jnp.float32).reshape(1, -1) for gain in (ln_attn, ln_mlp, q_gain, k_gain)
    )
    heads = wq.shape[1] // HD
    kv_heads = wk.shape[1] // HD
    group = heads // kv_heads

    flows = ((0, 0), (0, 1), (1, 0), (1, 1))

    def make_pump(block_of, send, recv1, recv2, pair_recv):
        def pump(p, own=None):
            p = jnp.int32(p)
            b, k = lax.rem(p, SIDE), p // SIDE
            for f, (axis, d) in enumerate(flows):
                step = 1 if d == 0 else -1
                first = y_near[d] if axis == 0 else z_near[d]
                second = z_near[d] if axis == 0 else y_near[d]
                if axis == 0:
                    block = block_of(f, turn(y - step * b), turn(z - step * k))
                else:
                    block = block_of(f, turn(y - step * k), turn(z - step * b))
                source = block if own is None else own(f)

                @pl.when((p >= 1) & (p < SIDE))
                def _():
                    remote(block, block, send.at[0], recv1.at[f, p - 1], first).wait_recv()

                @pl.when(p >= SIDE)
                def _():
                    remote(block, block, send.at[1], recv2.at[f, p - SIDE], second).wait_recv()

                @pl.when(p < SIDE - 1)
                def _():
                    remote(source, block, send.at[0], recv1.at[f, p], first).start()

                @pl.when(p < PUMPS - SIDE)
                def _():
                    remote(source, block, send.at[1], recv2.at[f, p], second).start()

                remote(source, block, send.at[2], pair_recv.at[0], pair).start()

        return pump

    seq = SIDE * rows
    strip = width // len(flows)

    def piece_at(j, d):
        chunk = turn(x - j) if d == 0 else turn(x + j)
        return pl.multiple_of(chunk * rows + d * HALF, HALF)

    def kv_block(stage):
        def block_of(f, oy, oz):
            return kv.at[pl.ds(req_of(oy, oz, core) * seq + piece_at(2 * stage + f // 2, f % 2), HALF)]

        return block_of

    def kv_source(stage):
        return lambda f: kvbuf.at[pl.ds(piece_at(2 * stage + f // 2, f % 2), HALF)]

    def w_block(f, oy, oz):
        return wfull.at[:, oy, oz, core, :, pl.ds(f * strip, strip)]

    pump_a = make_pump(kv_block(0), kv_send_a, kv1_recv_a, kv2_recv_a, kv_pair_recv_a)
    pump_b = make_pump(kv_block(1), kv_send_b, kv1_recv_b, kv2_recv_b, kv_pair_recv_b)
    w_pump = make_pump(w_block, w_send, w1_recv, w2_recv, w_pair_recv)

    def settle(send, pair_recv, first, second, last):
        remote(first, first, send.at[0], pair_recv.at[0], pair).wait_send()
        remote(second, second, send.at[1], pair_recv.at[0], pair).wait_send()
        remote(last, last, send.at[2], pair_recv.at[0], pair).wait_send()

    for move in moves[: 2 * SUBS + 3]:
        move.wait()

    @pl.loop(0, SIDE)
    def _(j):
        @pl.when(j > 0)
        def _():
            for p in range(SUBS):
                gather_advance(hbuf, ag1_send, ag1_recv, j, p)
                w_pump(3 * j - 2 + p)

                @pl.when(j > 1)
                def _():
                    pump_a(3 * j - 5 + p)

        a, b = turn(x - j), turn(x + j)
        normed = rms(ring_rows(hbuf, j), gain_attn).astype(jnp.bfloat16)
        row = lax.broadcasted_iota(jnp.int32, (rows, 1), 0)
        token = jnp.where(row < HALF, a, b) * rows + row
        angle = (token - begin_of(token)).astype(jnp.float32) * freq
        cosine = jnp.cos(angle)
        sine = jnp.sin(angle) * sign

        def turned(values, gain):
            scaled = rms(values, gain)
            return (scaled * cosine + pltpu.roll(scaled, HD // 2, 1) * sine).astype(jnp.bfloat16)

        query = jnp.dot(normed, wq[...], preferred_element_type=jnp.float32)
        key = jnp.dot(normed, wk[...], preferred_element_type=jnp.float32)
        value = jnp.dot(normed, wv[...], preferred_element_type=jnp.float32).astype(jnp.bfloat16)
        for h in range(heads):
            part = turned(query[:, h * HD : (h + 1) * HD], gain_q)
            qbuf[a, 0, :, h * HD : (h + 1) * HD] = part[:HALF]
            qbuf[b, 1, :, h * HD : (h + 1) * HD] = part[HALF:]
        for h in range(kv_heads):
            part = turned(key[:, h * HD : (h + 1) * HD], gain_k)
            mine = value[:, h * HD : (h + 1) * HD]
            kbuf[a, 0, :, h * HD : (h + 1) * HD] = part[:HALF]
            kbuf[b, 1, :, h * HD : (h + 1) * HD] = part[HALF:]
            both = jnp.concatenate([part, mine], axis=1)
            kvbuf[pl.ds(a * rows, HALF), h, :] = both[:HALF]
            kvbuf[pl.ds(b * rows + HALF, HALF), h, :] = both[HALF:]
        vbuf[a, 0] = value[:HALF]
        vbuf[b, 1] = value[HALF:]

        @pl.when(j == 0)
        def _():
            for k in (1, 3, 2):
                out_exchange(k).wait_recv()

        w_pump(3 * j)

        @pl.when(j == 1)
        def _():
            pump_a(0, kv_source(0))

        @pl.when(j > 1)
        def _():
            pump_a(3 * j - 3)

    kv_own = pltpu.make_async_copy(kvbuf, kv.at[pl.ds(c * seq, seq)], local_sem.at[2 * SUBS + len(weights)])
    kv_own.start()

    w_pump(3 * SIDE - 2)
    pump_b(0, kv_source(1))
    w_pump(3 * SIDE - 1)
    pump_a(7)

    def a_copy(n, src, dst, near):
        return remote(src, dst, a_send.at[n], a_recv.at[n], near)

    def head_copy(n, i=0):
        if n < 2:
            return a_copy(n, attbuf.at[i], att_in.at[2 - 2 * n], x_near[n])
        return a_copy(n, attbuf.at[i, n - 2], relay.at[n - 2], x_near[n - 2])

    relays = (
        a_copy(4, relay.at[0], att_in.at[1, 0], x_near[0]),
        a_copy(5, relay.at[1], att_in.at[1, 1], x_near[1]),
    )

    keys = kbuf[...].reshape(seq, kv_heads * HD)
    values = vbuf[...].reshape(seq, kv_heads * HD)
    for i in range(SIDE):
        extent = (i + 1) * rows
        token = lax.broadcasted_iota(jnp.int32, (rows, extent), 0) + i * rows
        other = lax.broadcasted_iota(jnp.int32, (rows, extent), 1)
        allowed = (other <= token) & (other >= begin_of(token[:, :1]))
        allowed = jnp.concatenate([allowed.astype(jnp.float32)] * group, axis=0) > 0.5
        block = qbuf[i].reshape(rows, heads * HD)
        for n in range(kv_heads):
            stacked = jnp.concatenate(
                [block[:, (n * group + h) * HD : (n * group + h + 1) * HD] for h in range(group)], axis=0
            )
            scores = lax.dot_general(
                stacked,
                keys[:extent, n * HD : (n + 1) * HD],
                (((1,), (1,)), ((), ())),
                preferred_element_type=jnp.float32,
            )
            raised = jnp.where(allowed, jnp.exp(scores * (1.0 / math.sqrt(HD))), 0.0)
            share = (raised * (1.0 / jnp.sum(raised, axis=-1, keepdims=True))).astype(jnp.bfloat16)
            mixed = jnp.dot(
                share, values[:extent, n * HD : (n + 1) * HD], preferred_element_type=jnp.float32
            ).astype(jnp.bfloat16)
            for h in range(group):
                at = (n * group + h) * HD
                attbuf[i, 0, :, at : at + HD] = mixed[h * rows : h * rows + HALF]
                attbuf[i, 1, :, at : at + HD] = mixed[h * rows + HALF : (h + 1) * rows]
        ahead = turn(i - x)

        @pl.when(ahead == 1)
        def _():
            head_copy(0, i).start()

        @pl.when(ahead == SIDE - 1)
        def _():
            head_copy(1, i).start()

        @pl.when(ahead == 2)
        def _():
            head_copy(2, i).start()
            head_copy(3, i).start()

        w_pump(3 * SIDE + i)
        if i % 2 == 1:
            pump_a(8 + i // 2)
    piece = width // SUBS

    def sum_step(send_buf, recv_buf, send, recv, j, d, n):
        return remote(send_buf.at[j, d, n], recv_buf.at[j, d, n], send.at[j, d, n], recv.at[j, d, n], x_near[d])

    def add_arrived(part, send_buf, recv_buf, send, recv, j, n):
        for d in range(2):
            sum_step(send_buf, recv_buf, send, recv, j, d, n).wait_recv()
        return part + jnp.concatenate([recv_buf[j, 0, n], recv_buf[j, 1, n]], axis=0).astype(jnp.float32)

    def send_on(part, send_buf, recv_buf, send, recv, j, n):
        rounded = part.astype(jnp.bfloat16)
        for d in range(2):
            send_buf[j, d, n] = rounded[d * HALF : (d + 1) * HALF]
            sum_step(send_buf, recv_buf, send, recv, j, d, n).start()

    ring2 = (send2, recv2, rs2_send, rs2_recv)

    def add_heads(mixed, weight, n):
        send2f[n] += jnp.dot(mixed, weight, preferred_element_type=jnp.float32)

    def add_source(k):
        mixed = att_in[k - 1].reshape(rows, att_in.shape[3])
        for n in range(SUBS):
            weight = wfull[k - 1, :, :, :, :, n * piece : (n + 1) * piece].reshape(att_in.shape[3], piece)
            add_heads(mixed, weight, n)

    moves[2 * SUBS + 3].wait()
    for n, move in enumerate(relays):
        head_copy(2 + n).wait_recv()
        move.start()
    mixed = attbuf[x].reshape(rows, heads * HD)
    for n in range(SUBS):
        columns = slice(n * piece, (n + 1) * piece)
        before = [hbuf[x, d, :, :, columns].reshape(HALF, piece) for d in range(2)]
        send2f[n] = jnp.concatenate(before, axis=0).astype(jnp.float32)
        add_heads(mixed, wo[:, columns], n)
    pump_b(1)
    pump_a(10)
    half = wfull.at[:, :, :, 0]
    remote(half, half, w_send.at[2], w_pair_recv.at[0], pair).wait_recv()
    head_copy(1).wait_recv()
    add_source(1)
    head_copy(0).wait_recv()
    add_source(3)
    pump_a(11)
    for move in relays:
        move.wait_recv()
    add_source(2)
    for n in range(SUBS):
        total = send2f[n].astype(jnp.bfloat16)
        for d in range(2):
            abuf[x, d, :, :, n * piece : (n + 1) * piece] = total[d * HALF : (d + 1) * HALF].reshape(SUBS, sub, piece)
    for p in range(SUBS):
        for d in range(2):
            gather_step(abuf, ag2_send, ag2_recv, 0, d, p).start()
    pump_b(2)
    pump_a(12)

    for move in moves[2 * SUBS + 4 :]:
        move.wait()

    def activation(j):
        normed = rms(ring_rows(abuf, j), gain_mlp).astype(jnp.bfloat16)
        gate = jnp.dot(normed, wg[...], preferred_element_type=jnp.float32)
        upper = jnp.dot(normed, wu[...], preferred_element_type=jnp.float32)
        return (gate * jax.nn.sigmoid(gate) * upper).astype(jnp.bfloat16)

    def down_part(act, n):
        return jnp.dot(act, wd[:, n * piece : (n + 1) * piece], preferred_element_type=jnp.float32)

    @pl.loop(0, SIDE)
    def _(j):
        @pl.when(j > 0)
        def _():
            for p in range(SUBS):
                gather_advance(abuf, ag2_send, ag2_recv, j, p)
                pump_b(4 * j + p)

                @pl.when(j == 1)
                def _():
                    pump_a(14 + p)

        actbuf[...] = activation(j)

        @pl.when(j > 0)
        def _():
            pump_b(4 * j + 2)

        @pl.when(j > 0)
        def _():
            act = actbuf[...]
            for n in range(SUBS):
                part = down_part(act, n)
                send2f[n] = part

                @pl.when(j > 1)
                def _():
                    send2f[n] = add_arrived(send2f[n], *ring2, j - 2, n)

                send_on(send2f[n], *ring2, j - 1, n)

        @pl.when(j == 0)
        def _():
            ownbuf[...] = actbuf[...]
            pump_a(13)

        pump_b(4 * j + 3)

    act = ownbuf[...]
    for n in range(SUBS):
        part = add_arrived(down_part(act, n), *ring2, SIDE - 2, n)
        for d in range(2):
            before = abuf[x, d, :, :, n * piece : (n + 1) * piece].reshape(HALF, piece).astype(jnp.float32)
            total = before + part[d * HALF : (d + 1) * HALF]
            out[d * HALF : (d + 1) * HALF, n * piece : (n + 1) * piece] = total.astype(jnp.bfloat16)

    @pl.loop(0, SIDE - 1)
    def _(j):
        for d in range(2):
            for p in range(SUBS):
                gather_step(hbuf, ag1_send, ag1_recv, j, d, p).wait_send()
                gather_step(abuf, ag2_send, ag2_recv, j, d, p).wait_send()
                sum_step(*ring2, j, d, p).wait_send()

    for k in range(1, SIDE):
        out_exchange(k).wait_send()
    for n in range(4):
        head_copy(n).wait_send()
    for move in relays:
        move.wait_send()
    settle(
        w_send, w_pair_recv, wfull.at[:, 0, pl.ds(0, SIDE - 1), 0], wfull.at[:, pl.ds(0, SIDE - 1), :, 0], half
    )
    kv_own.wait()
    units = HALF * len(flows)
    got = kv.at[pl.ds(0, units * PUMPS)]
    for send, pair_recv in ((kv_send_a, kv_pair_recv_a), (kv_send_b, kv_pair_recv_b)):
        settle(send, pair_recv, kv.at[pl.ds(0, units * (SIDE - 1))], kv.at[pl.ds(0, units * (PUMPS - SIDE))], got)
        remote(got, got, send.at[2], pair_recv.at[0], pair).wait_recv()


def run_layer(hidden, seg, ln_attn, w_query, w_key, w_value, q_gain, k_gain, w_out, ln_mlp, w_gate, w_up, w_down):
    rows, width = hidden.shape
    seq = rows * SIDE
    units = w_gate.shape[1]
    kvw = w_key.shape[1]
    heads_w = w_query.shape[1]
    bf16, f32 = jnp.bfloat16, jnp.float32
    sub = HALF // SUBS
    vmem = pl.BlockSpec(memory_space=pltpu.VMEM)
    hbm = pl.BlockSpec(memory_space=pl.ANY)
    ring = (SIDE - 1, 2, SUBS)
    dma = pltpu.SemaphoreType.DMA
    gather_sems = [dma((3,)), dma((4, SIDE - 1)), dma((4, PUMPS - SIDE)), dma((1,))]
    blocks = pltpu.VMEM(ring + (HALF, width // SUBS), bf16)
    return pl.pallas_call(
        layer_kernel,
        out_shape=(
            jax.ShapeDtypeStruct((rows, width), bf16),
            jax.ShapeDtypeStruct((seg.shape[0] * seq, kvw // HD, 2 * HD), bf16),
            jax.ShapeDtypeStruct((seg.shape[0], HD), jnp.int32),
        ),
        in_specs=[hbm, vmem, vmem, hbm, hbm, hbm, vmem, vmem, hbm, vmem, hbm, hbm, hbm],
        out_specs=(vmem, hbm, vmem),
        scratch_shapes=[
            pltpu.VMEM((SIDE, 2, SUBS, sub, width), bf16),
            pltpu.VMEM((SIDE, 2, SUBS, sub, width), bf16),
            pltpu.VMEM(w_query.shape, bf16),
            pltpu.VMEM(w_key.shape, bf16),
            pltpu.VMEM(w_value.shape, bf16),
            pltpu.VMEM(w_out.shape, bf16),
            pltpu.VMEM(w_gate.shape, bf16),
            pltpu.VMEM(w_up.shape, bf16),
            pltpu.VMEM(w_down.shape, bf16),
            pltpu.VMEM((SIDE, 2, HALF, heads_w), bf16),
            pltpu.VMEM((SIDE, 2, HALF, kvw), bf16),
            pltpu.VMEM((SIDE, 2, HALF, kvw), bf16),
            pltpu.VMEM((seq, kvw // HD, 2 * HD), bf16),
            pltpu.VMEM((SIDE, 2, HALF, heads_w), bf16),
            pltpu.VMEM((rows, units), bf16),
            pltpu.VMEM((rows, units), bf16),
            pltpu.VMEM((SUBS, rows, width // SUBS), f32),
            pltpu.VMEM((SIDE - 1, SIDE, SIDE, 2, w_out.shape[0] // seg.shape[0], width), bf16),
            pltpu.VMEM((SIDE - 1, 2, HALF, heads_w), bf16),
            pltpu.VMEM((2, HALF, heads_w), bf16),
            blocks,
            blocks,
            dma((2 * SUBS + 8,)),
            dma(ring),
            dma(ring),
            dma((SIDE - 1,)),
            dma((SIDE - 1,)),
            dma((6,)),
            dma((6,)),
        ]
        + gather_sems
        + [dma(ring)] * 4
        + gather_sems * 2,
        compiler_params=pltpu.CompilerParams(
            collective_id=0, has_side_effects=True, vmem_limit_bytes=60 * 1024 * 1024
        ),
        name="layer",
    )(hidden, seg, ln_attn, w_query, w_key, w_value, q_gain, k_gain, w_out, ln_mlp, w_gate, w_up, w_down)


def body(
    hidden_in,
    segment_ids,
    request_prompt,
    page_table,
    ln_attn,
    w_query,
    w_key,
    w_value,
    q_gain,
    k_gain,
    w_out,
    ln_mlp,
    w_gate,
    w_up,
    w_down,
):
    result, everything, bounds = run_layer(
        hidden_in,
        segment_ids,
        ln_attn,
        w_query,
        w_key,
        w_value,
        q_gain,
        k_gain,
        w_out,
        ln_mlp,
        w_gate,
        w_up,
        w_down,
    )
    cache, result = fill_pages(page_table, request_prompt, bounds, result, everything)
    return (result, cache)


def solution(mesh):
    return jax.shard_map(
        body,
        mesh=mesh,
        in_specs=(
            P(("req", "mp"), None),
            P(),
            P("req"),
            P("req", None),
            P(),
            P(None, "mp"),
            P(None, "mp"),
            P(None, "mp"),
            P(),
            P(),
            P("mp", None),
            P(),
            P(None, "mp"),
            P(None, "mp"),
            P("mp", None),
        ),
        out_specs=(P(("req", "mp"), None), P("req", None, "mp", None)),
        check_vma=False,
    )
```

```python
import math

import jax
import jax.numpy as jnp
from jax import lax
from jax.experimental import pallas as pl
from jax.experimental.pallas import tpu as pltpu
from jax.sharding import PartitionSpec as P

HD = 128
PROMPTS_DEV = 3
PAGE = 16


EPS = 1e-06
THETA = 1000000.0


def fill_kernel(
    table_hbm, prompt_hbm, bounds_hbm, layer_hbm, rows_ref, out_ref, layer_out, table, prompt, bounds, held, edges,
    zeros, small_sem, out_sem,
):
    most, requests = table.shape
    seq = rows_ref.shape[0] // bounds.shape[0]
    smalls = [
        pltpu.make_async_copy(src, dst, small_sem.at[n])
        for n, (src, dst) in enumerate(
            ((table_hbm, table), (prompt_hbm, prompt), (bounds_hbm, bounds), (layer_hbm, held))
        )
    ]
    layer_copy = pltpu.make_async_copy(held, layer_out, small_sem.at[4])
    for small in smalls:
        small.start()
    zeros[...] = jnp.zeros_like(zeros)
    for small in smalls:
        small.wait()
    layer_copy.start()

    @pl.loop(0, requests)
    def _(r):
        p = prompt[r]
        g = p // PROMPTS_DEV
        s = p - g * PROMPTS_DEV
        low = jnp.where(s == 0, 0, jnp.where(s == 1, bounds[g, 0], bounds[g, 1]))
        high = jnp.where(s == 0, bounds[g, 0], jnp.where(s == 1, bounds[g, 1], seq))
        begin, length = g * seq + low, high - low
        full = length // PAGE
        rest = length - full * PAGE

        @pl.when(rest > 0)
        def _():
            at = begin + full * PAGE
            for o in range(PAGE):
                line = rows_ref[pl.ds(jnp.minimum(at + o, rows_ref.shape[0] - 1), 1)]
                edges[r, pl.ds(o, 1)] = jnp.where(o < rest, line, jnp.zeros_like(line))

        for e in range(most):
            page = table[e, r]

            @pl.when(e < full)
            def _():
                pltpu.make_async_copy(
                    rows_ref.at[pl.ds(begin + e * PAGE, PAGE)], out_ref.at[page], out_sem.at[0]
                ).start()

            @pl.when(e * PAGE >= length)
            def _():
                pltpu.make_async_copy(zeros, out_ref.at[page], out_sem.at[0]).start()

        @pl.when(rest > 0)
        def _():
            pltpu.make_async_copy(edges.at[r], out_ref.at[table[full, r]], out_sem.at[0]).start()

    pltpu.make_async_copy(out_ref, out_ref, out_sem.at[0]).wait()
    layer_copy.wait()


def fill_pages(page_table, request_prompt, bounds, layer, rows):
    requests, most = page_table.shape
    unit = rows.shape[1:]
    hbm = pl.BlockSpec(memory_space=pl.ANY)
    return pl.pallas_call(
        fill_kernel,
        out_shape=(
            jax.ShapeDtypeStruct((requests * most, PAGE) + unit, rows.dtype),
            jax.ShapeDtypeStruct(layer.shape, layer.dtype),
        ),
        in_specs=[hbm] * 4 + [pl.BlockSpec(memory_space=pltpu.VMEM)],
        out_specs=(hbm, hbm),
        scratch_shapes=[
            pltpu.SMEM((most, requests), jnp.int32),
            pltpu.SMEM((requests,), jnp.int32),
            pltpu.SMEM(bounds.shape, jnp.int32),
            pltpu.VMEM(layer.shape, layer.dtype),
            pltpu.VMEM((requests, PAGE) + unit, rows.dtype),
            pltpu.VMEM((PAGE,) + unit, rows.dtype),
            pltpu.SemaphoreType.DMA((5,)),
            pltpu.SemaphoreType.DMA((1,)),
        ],
        compiler_params=pltpu.CompilerParams(vmem_limit_bytes=46 * 1024 * 1024),
        name="fill_pages",
    )(page_table.T, request_prompt, bounds, layer, rows)


MESH = pl.DeviceIdType.MESH
HALF = 64
SUBS = 2
SIDE = 4
PUMPS = SIDE * SIDE


def rms(wide, gain):
    return wide * lax.rsqrt(jnp.mean(wide * wide, axis=-1, keepdims=True) + EPS) * gain


def layer_kernel(
    hidden,
    seg,
    ln_attn,
    w_query,
    w_key,
    w_value,
    q_gain,
    k_gain,
    w_out,
    ln_mlp,
    w_gate,
    w_up,
    w_down,
    out,
    kv,
    bounds,
    hbuf,
    abuf,
    wq,
    wk,
    wv,
    wo,
    wg,
    wu,
    wd,
    qbuf,
    kbuf,
    vbuf,
    kvbuf,
    attbuf,
    actbuf,
    ownbuf,
    send2f,
    wfull,
    att_in,
    relay,
    send2,
    recv2,
    local_sem,
    ag1_send,
    ag1_recv,
    wx_send,
    wx_recv,
    a_send,
    a_recv,
    w_send,
    w1_recv,
    w2_recv,
    w_pair_recv,
    ag2_send,
    ag2_recv,
    rs2_send,
    rs2_recv,
    kv_send_a,
    kv1_recv_a,
    kv2_recv_a,
    kv_pair_recv_a,
    kv_send_b,
    kv1_recv_b,
    kv2_recv_b,
    kv_pair_recv_b,
):
    x = lax.axis_index("mp")
    c = lax.axis_index("req")
    core = lax.rem(c, 2)
    z = lax.rem(c // 2, SIDE)
    y = c // (2 * SIDE)
    width = hidden.shape[1]
    rows = hidden.shape[0]
    sub = HALF // SUBS

    def turn(value):
        return lax.rem(value + 2 * SIDE, SIDE)

    def req_of(yy, zz, cc):
        return (yy * SIDE + zz) * 2 + cc

    x_near = ((c, turn(x + 1)), (c, turn(x - 1)))
    pair = (req_of(y, z, 1 - core), x)
    y_near = ((req_of(turn(y + 1), z, core), x), (req_of(turn(y - 1), z, core), x))
    z_near = ((req_of(y, turn(z + 1), core), x), (req_of(y, turn(z - 1), core), x))

    moves = []
    weights = ((w_query, wq), (w_key, wk), (w_value, wv), (w_out, wo), (w_gate, wg), (w_up, wu), (w_down, wd))
    for d in range(2):
        for p in range(SUBS):
            moves.append(
                pltpu.make_async_copy(
                    hidden.at[pl.ds(d * HALF + p * sub, sub)], hbuf.at[x, d, p], local_sem.at[d * SUBS + p]
                )
            )
    for n, (src, dst) in enumerate(weights):
        moves.append(pltpu.make_async_copy(src, dst, local_sem.at[2 * SUBS + n]))
    for move in moves:
        move.start()

    barrier = pltpu.get_barrier_semaphore()
    peers = x_near + y_near + z_near + (pair, (c, turn(x + 2)))
    for near in peers:
        pl.semaphore_signal(barrier, inc=1, device_id=near, device_id_type=MESH)
    pl.semaphore_wait(barrier, len(peers))

    def remote(src, dst, send, recv, near):
        return pltpu.make_async_remote_copy(
            src_ref=src, dst_ref=dst, send_sem=send, recv_sem=recv, device_id=near, device_id_type=MESH
        )

    def gather_step(buf, send, recv, j, d, p):
        block = buf.at[turn(x - j) if d == 0 else turn(x + j), d, p]
        return remote(block, block, send.at[j, d, p], recv.at[j, d, p], x_near[d])

    def gather_advance(buf, send, recv, j, p):
        for d in range(2):
            gather_step(buf, send, recv, j - 1, d, p).wait_recv()

            @pl.when(j < SIDE - 1)
            def _():
                gather_step(buf, send, recv, j, d, p).start()

    def ring_rows(buf, j):
        a, b = turn(x - j), turn(x + j)
        upper = buf[a, 0].reshape(HALF, width)
        lower = buf[b, 1].reshape(HALF, width)
        return jnp.concatenate([upper, lower], axis=0).astype(jnp.float32)

    deep = wfull.shape[4]

    def out_exchange(k):
        return remote(
            w_out.at[pl.ds(c * deep, deep)],
            wfull.at[k - 1, y, z, core],
            wx_send.at[k - 1],
            wx_recv.at[k - 1],
            (c, turn(x - k)),
        )

    for k in (2, 1, 3):
        out_exchange(k).start()
    for p in range(SUBS):
        for d in range(2):
            own = hidden.at[pl.ds(d * HALF + p * sub, sub)]
            remote(own, hbuf.at[x, d, p], ag1_send.at[0, d, p], ag1_recv.at[0, d, p], x_near[d]).start()

    def below(table, bound):
        return jnp.sum((table < bound).astype(jnp.int32), axis=1, keepdims=True)

    seg_row = seg[pl.ds(c, 1), :]
    first1, first2 = below(seg_row, 1), below(seg_row, 2)
    place = lax.broadcasted_iota(jnp.int32, bounds.shape, 1)
    bounds[...] = jnp.where(place == 0, below(seg[...], 1), below(seg[...], 2))

    def begin_of(token):
        return jnp.where(token >= first2, first2, jnp.where(token >= first1, first1, 0))

    lane = lax.broadcasted_iota(jnp.int32, (1, HD), 1)
    freq = jnp.exp2(lax.rem(lane, HD // 2).astype(jnp.float32) * (-2.0 * math.log2(THETA) / HD))
    sign = jnp.where(lane < HD // 2, -1.0, 1.0)
    gain_attn, gain_mlp, gain_q, gain_k = (
        gain[...].astype(jnp.float32).reshape(1, -1) for gain in (ln_attn, ln_mlp, q_gain, k_gain)
    )
    heads = wq.shape[1] // HD
    kv_heads = wk.shape[1] // HD
    group = heads // kv_heads

    flows = ((0, 0), (0, 1), (1, 0), (1, 1))

    def make_pump(block_of, send, recv1, recv2, pair_recv):
        def pump(p, own=None):
            p = jnp.int32(p)
            b, k = lax.rem(p, SIDE), p // SIDE
            for f, (axis, d) in enumerate(flows):
                step = 1 if d == 0 else -1
                first = y_near[d] if axis == 0 else z_near[d]
                second = z_near[d] if axis == 0 else y_near[d]
                if axis == 0:
                    block = block_of(f, turn(y - step * b), turn(z - step * k))
                else:
                    block = block_of(f, turn(y - step * k), turn(z - step * b))
                source = block if own is None else own(f)

                @pl.when((p >= 1) & (p < SIDE))
                def _():
                    remote(block, block, send.at[0], recv1.at[f, p - 1], first).wait_recv()

                @pl.when(p >= SIDE)
                def _():
                    remote(block, block, send.at[1], recv2.at[f, p - SIDE], second).wait_recv()

                @pl.when(p < SIDE - 1)
                def _():
                    remote(source, block, send.at[0], recv1.at[f, p], first).start()

                @pl.when(p < PUMPS - SIDE)
                def _():
                    remote(source, block, send.at[1], recv2.at[f, p], second).start()

                remote(source, block, send.at[2], pair_recv.at[0], pair).start()

        return pump

    seq = SIDE * rows
    strip = width // len(flows)

    def piece_at(j, d):
        chunk = turn(x - j) if d == 0 else turn(x + j)
        return pl.multiple_of(chunk * rows + d * HALF, HALF)

    def kv_block(stage):
        def block_of(f, oy, oz):
            return kv.at[pl.ds(req_of(oy, oz, core) * seq + piece_at(2 * stage + f // 2, f % 2), HALF)]

        return block_of

    def kv_source(stage):
        return lambda f: kvbuf.at[pl.ds(piece_at(2 * stage + f // 2, f % 2), HALF)]

    def w_block(f, oy, oz):
        return wfull.at[:, oy, oz, core, :, pl.ds(f * strip, strip)]

    pump_a = make_pump(kv_block(0), kv_send_a, kv1_recv_a, kv2_recv_a, kv_pair_recv_a)
    pump_b = make_pump(kv_block(1), kv_send_b, kv1_recv_b, kv2_recv_b, kv_pair_recv_b)
    w_pump = make_pump(w_block, w_send, w1_recv, w2_recv, w_pair_recv)

    def settle(send, pair_recv, first, second, last):
        remote(first, first, send.at[0], pair_recv.at[0], pair).wait_send()
        remote(second, second, send.at[1], pair_recv.at[0], pair).wait_send()
        remote(last, last, send.at[2], pair_recv.at[0], pair).wait_send()

    for move in moves[: 2 * SUBS + 3]:
        move.wait()

    @pl.loop(0, SIDE)
    def _(j):
        @pl.when(j > 0)
        def _():
            for p in range(SUBS):
                gather_advance(hbuf, ag1_send, ag1_recv, j, p)

                @pl.when(j == 1)
                def _():
                    w_pump(1 + p)

                @pl.when(j > 1)
                def _():
                    w_pump(5 * j - 6 + 2 * p)
                    w_pump(5 * j - 5 + 2 * p)

        a, b = turn(x - j), turn(x + j)
        normed = rms(ring_rows(hbuf, j), gain_attn).astype(jnp.bfloat16)
        row = lax.broadcasted_iota(jnp.int32, (rows, 1), 0)
        token = jnp.where(row < HALF, a, b) * rows + row
        angle = (token - begin_of(token)).astype(jnp.float32) * freq
        cosine = jnp.cos(angle)
        sine = jnp.sin(angle) * sign

        def turned(values, gain):
            scaled = rms(values, gain)
            return (scaled * cosine + pltpu.roll(scaled, HD // 2, 1) * sine).astype(jnp.bfloat16)

        query = jnp.dot(normed, wq[...], preferred_element_type=jnp.float32)
        key = jnp.dot(normed, wk[...], preferred_element_type=jnp.float32)
        value = jnp.dot(normed, wv[...], preferred_element_type=jnp.float32).astype(jnp.bfloat16)
        for h in range(heads):
            part = turned(query[:, h * HD : (h + 1) * HD], gain_q)
            qbuf[a, 0, :, h * HD : (h + 1) * HD] = part[:HALF]
            qbuf[b, 1, :, h * HD : (h + 1) * HD] = part[HALF:]
        for h in range(kv_heads):
            part = turned(key[:, h * HD : (h + 1) * HD], gain_k)
            mine = value[:, h * HD : (h + 1) * HD]
            kbuf[a, 0, :, h * HD : (h + 1) * HD] = part[:HALF]
            kbuf[b, 1, :, h * HD : (h + 1) * HD] = part[HALF:]
            both = jnp.concatenate([part, mine], axis=1)
            kvbuf[pl.ds(a * rows, HALF), h, :] = both[:HALF]
            kvbuf[pl.ds(b * rows + HALF, HALF), h, :] = both[HALF:]
        vbuf[a, 0] = value[:HALF]
        vbuf[b, 1] = value[HALF:]

        @pl.when(j == 0)
        def _():
            for k in (1, 3, 2):
                out_exchange(k).wait_recv()

        w_pump(jnp.maximum(5 * j - 2, 0))

        @pl.when(j == 2)
        def _():
            pump_a(0, kv_source(0))

    kv_own = pltpu.make_async_copy(kvbuf, kv.at[pl.ds(c * seq, seq)], local_sem.at[2 * SUBS + len(weights)])
    kv_own.start()

    pump_a(1)
    pump_b(0, kv_source(1))
    w_pump(14)

    def a_copy(n, src, dst, near):
        return remote(src, dst, a_send.at[n], a_recv.at[n], near)

    def head_copy(n, i=0):
        if n < 2:
            return a_copy(n, attbuf.at[i], att_in.at[2 - 2 * n], x_near[n])
        return a_copy(n, attbuf.at[i, n - 2], relay.at[n - 2], x_near[n - 2])

    relays = (
        a_copy(4, relay.at[0], att_in.at[1, 0], x_near[0]),
        a_copy(5, relay.at[1], att_in.at[1, 1], x_near[1]),
    )

    keys = kbuf[...].reshape(seq, kv_heads * HD)
    values = vbuf[...].reshape(seq, kv_heads * HD)
    for i in range(SIDE):
        extent = (i + 1) * rows
        token = lax.broadcasted_iota(jnp.int32, (rows, extent), 0) + i * rows
        other = lax.broadcasted_iota(jnp.int32, (rows, extent), 1)
        allowed = (other <= token) & (other >= begin_of(token[:, :1]))
        allowed = jnp.concatenate([allowed.astype(jnp.float32)] * group, axis=0) > 0.5
        block = qbuf[i].reshape(rows, heads * HD)
        for n in range(kv_heads):
            stacked = jnp.concatenate(
                [block[:, (n * group + h) * HD : (n * group + h + 1) * HD] for h in range(group)], axis=0
            )
            scores = lax.dot_general(
                stacked,
                keys[:extent, n * HD : (n + 1) * HD],
                (((1,), (1,)), ((), ())),
                preferred_element_type=jnp.float32,
            )
            raised = jnp.where(allowed, jnp.exp(scores * (1.0 / math.sqrt(HD))), 0.0)
            share = (raised * (1.0 / jnp.sum(raised, axis=-1, keepdims=True))).astype(jnp.bfloat16)
            mixed = jnp.dot(
                share, values[:extent, n * HD : (n + 1) * HD], preferred_element_type=jnp.float32
            ).astype(jnp.bfloat16)
            for h in range(group):
                at = (n * group + h) * HD
                attbuf[i, 0, :, at : at + HD] = mixed[h * rows : h * rows + HALF]
                attbuf[i, 1, :, at : at + HD] = mixed[h * rows + HALF : (h + 1) * rows]
        ahead = turn(i - x)

        @pl.when(ahead == 1)
        def _():
            head_copy(0, i).start()

        @pl.when(ahead == SIDE - 1)
        def _():
            head_copy(1, i).start()

        @pl.when(ahead == 2)
        def _():
            head_copy(2, i).start()
            head_copy(3, i).start()

        if i == 2:
            w_pump(15)
    piece = width // SUBS

    def sum_step(send_buf, recv_buf, send, recv, j, d, n):
        return remote(send_buf.at[j, d, n], recv_buf.at[j, d, n], send.at[j, d, n], recv.at[j, d, n], x_near[d])

    def add_arrived(part, send_buf, recv_buf, send, recv, j, n):
        for d in range(2):
            sum_step(send_buf, recv_buf, send, recv, j, d, n).wait_recv()
        return part + jnp.concatenate([recv_buf[j, 0, n], recv_buf[j, 1, n]], axis=0).astype(jnp.float32)

    def send_on(part, send_buf, recv_buf, send, recv, j, n):
        rounded = part.astype(jnp.bfloat16)
        for d in range(2):
            send_buf[j, d, n] = rounded[d * HALF : (d + 1) * HALF]
            sum_step(send_buf, recv_buf, send, recv, j, d, n).start()

    ring2 = (send2, recv2, rs2_send, rs2_recv)

    def add_heads(mixed, weight, n):
        send2f[n] += jnp.dot(mixed, weight, preferred_element_type=jnp.float32)

    def add_source(k):
        mixed = att_in[k - 1].reshape(rows, att_in.shape[3])
        for n in range(SUBS):
            weight = wfull[k - 1, :, :, :, :, n * piece : (n + 1) * piece].reshape(att_in.shape[3], piece)
            add_heads(mixed, weight, n)

    moves[2 * SUBS + 3].wait()
    for n, move in enumerate(relays):
        head_copy(2 + n).wait_recv()
        move.start()
    pump_a(2)
    mixed = attbuf[x].reshape(rows, heads * HD)
    for n in range(SUBS):
        columns = slice(n * piece, (n + 1) * piece)
        before = [hbuf[x, d, :, :, columns].reshape(HALF, piece) for d in range(2)]
        send2f[n] = jnp.concatenate(before, axis=0).astype(jnp.float32)
        add_heads(mixed, wo[:, columns], n)
    pump_b(1)
    half = wfull.at[:, :, :, 0]
    remote(half, half, w_send.at[2], w_pair_recv.at[0], pair).wait_recv()
    head_copy(1).wait_recv()
    add_source(1)
    head_copy(0).wait_recv()
    add_source(3)
    for move in relays:
        move.wait_recv()
    add_source(2)
    for n in range(SUBS):
        total = send2f[n].astype(jnp.bfloat16)
        for d in range(2):
            abuf[x, d, :, :, n * piece : (n + 1) * piece] = total[d * HALF : (d + 1) * HALF].reshape(SUBS, sub, piece)
    for p in range(SUBS):
        for d in range(2):
            gather_step(abuf, ag2_send, ag2_recv, 0, d, p).start()
    for p in range(3, 7):
        pump_a(p)

    for move in moves[2 * SUBS + 4 :]:
        move.wait()

    def activation(j):
        normed = rms(ring_rows(abuf, j), gain_mlp).astype(jnp.bfloat16)
        gate = jnp.dot(normed, wg[...], preferred_element_type=jnp.float32)
        upper = jnp.dot(normed, wu[...], preferred_element_type=jnp.float32)
        return (gate * jax.nn.sigmoid(gate) * upper).astype(jnp.bfloat16)

    def down_part(act, n):
        return jnp.dot(act, wd[:, n * piece : (n + 1) * piece], preferred_element_type=jnp.float32)

    @pl.loop(0, SIDE)
    def _(j):
        @pl.when(j > 0)
        def _():
            for p in range(SUBS):
                gather_advance(abuf, ag2_send, ag2_recv, j, p)

                @pl.when(j > 1)
                def _():
                    pump_b(4 * j - 2 + p)

                if p == 0:

                    @pl.when(j == 1)
                    def _():
                        pump_a(7)

                    pump_a(4 * j + 3 + lax.select(j == 1, 1, 0))
                else:

                    @pl.when(j == 2)
                    def _():
                        pump_a(12)

        actbuf[...] = activation(j)

        @pl.when(j == 0)
        def _():
            pump_b(2)

        @pl.when(j == 1)
        def _():
            pump_b(3)
            pump_b(4)
            pump_b(5)

        @pl.when(j == 2)
        def _():
            pump_a(13)

        @pl.when(j > 1)
        def _():
            pump_b(4 * j)

        @pl.when(j > 0)
        def _():
            act = actbuf[...]
            for n in range(SUBS):
                part = down_part(act, n)
                send2f[n] = part

                @pl.when(j > 1)
                def _():
                    send2f[n] = add_arrived(send2f[n], *ring2, j - 2, n)

                send_on(send2f[n], *ring2, j - 1, n)

        @pl.when(j == 0)
        def _():
            ownbuf[...] = actbuf[...]

        @pl.when(j == 1)
        def _():
            pump_a(9)
            pump_a(10)

        @pl.when(j == 2)
        def _():
            pump_a(14)

        @pl.when(j > 1)
        def _():
            pump_b(4 * j + 1)

    act = ownbuf[...]
    pump_b(14)
    pump_b(15)
    for n in range(SUBS):
        part = add_arrived(down_part(act, n), *ring2, SIDE - 2, n)
        for d in range(2):
            before = abuf[x, d, :, :, n * piece : (n + 1) * piece].reshape(HALF, piece).astype(jnp.float32)
            total = before + part[d * HALF : (d + 1) * HALF]
            out[d * HALF : (d + 1) * HALF, n * piece : (n + 1) * piece] = total.astype(jnp.bfloat16)

    @pl.loop(0, SIDE - 1)
    def _(j):
        for d in range(2):
            for p in range(SUBS):
                gather_step(hbuf, ag1_send, ag1_recv, j, d, p).wait_send()
                gather_step(abuf, ag2_send, ag2_recv, j, d, p).wait_send()
                sum_step(*ring2, j, d, p).wait_send()

    for k in range(1, SIDE):
        out_exchange(k).wait_send()
    for n in range(4):
        head_copy(n).wait_send()
    for move in relays:
        move.wait_send()
    settle(
        w_send, w_pair_recv, wfull.at[:, 0, pl.ds(0, SIDE - 1), 0], wfull.at[:, pl.ds(0, SIDE - 1), :, 0], half
    )
    kv_own.wait()
    units = HALF * len(flows)
    got = kv.at[pl.ds(0, units * PUMPS)]
    for send, pair_recv in ((kv_send_a, kv_pair_recv_a), (kv_send_b, kv_pair_recv_b)):
        settle(send, pair_recv, kv.at[pl.ds(0, units * (SIDE - 1))], kv.at[pl.ds(0, units * (PUMPS - SIDE))], got)
        remote(got, got, send.at[2], pair_recv.at[0], pair).wait_recv()


def run_layer(hidden, seg, ln_attn, w_query, w_key, w_value, q_gain, k_gain, w_out, ln_mlp, w_gate, w_up, w_down):
    rows, width = hidden.shape
    seq = rows * SIDE
    units = w_gate.shape[1]
    kvw = w_key.shape[1]
    heads_w = w_query.shape[1]
    bf16, f32 = jnp.bfloat16, jnp.float32
    sub = HALF // SUBS
    vmem = pl.BlockSpec(memory_space=pltpu.VMEM)
    hbm = pl.BlockSpec(memory_space=pl.ANY)
    ring = (SIDE - 1, 2, SUBS)
    dma = pltpu.SemaphoreType.DMA
    gather_sems = [dma((3,)), dma((4, SIDE - 1)), dma((4, PUMPS - SIDE)), dma((1,))]
    blocks = pltpu.VMEM(ring + (HALF, width // SUBS), bf16)
    return pl.pallas_call(
        layer_kernel,
        out_shape=(
            jax.ShapeDtypeStruct((rows, width), bf16),
            pltpu.VMEM((seg.shape[0] * seq, kvw // HD, 2 * HD), bf16),
            jax.ShapeDtypeStruct((seg.shape[0], HD), jnp.int32),
        ),
        in_specs=[hbm, vmem, vmem, hbm, hbm, hbm, vmem, vmem, hbm, vmem, hbm, hbm, hbm],
        out_specs=(vmem, vmem, vmem),
        scratch_shapes=[
            pltpu.VMEM((SIDE, 2, SUBS, sub, width), bf16),
            pltpu.VMEM((SIDE, 2, SUBS, sub, width), bf16),
            pltpu.VMEM(w_query.shape, bf16),
            pltpu.VMEM(w_key.shape, bf16),
            pltpu.VMEM(w_value.shape, bf16),
            pltpu.VMEM(w_out.shape, bf16),
            pltpu.VMEM(w_gate.shape, bf16),
            pltpu.VMEM(w_up.shape, bf16),
            pltpu.VMEM(w_down.shape, bf16),
            pltpu.VMEM((SIDE, 2, HALF, heads_w), bf16),
            pltpu.VMEM((SIDE, 2, HALF, kvw), bf16),
            pltpu.VMEM((SIDE, 2, HALF, kvw), bf16),
            pltpu.VMEM((seq, kvw // HD, 2 * HD), bf16),
            pltpu.VMEM((SIDE, 2, HALF, heads_w), bf16),
            pltpu.VMEM((rows, units), bf16),
            pltpu.VMEM((rows, units), bf16),
            pltpu.VMEM((SUBS, rows, width // SUBS), f32),
            pltpu.VMEM((SIDE - 1, SIDE, SIDE, 2, w_out.shape[0] // seg.shape[0], width), bf16),
            pltpu.VMEM((SIDE - 1, 2, HALF, heads_w), bf16),
            pltpu.VMEM((2, HALF, heads_w), bf16),
            blocks,
            blocks,
            dma((2 * SUBS + 8,)),
            dma(ring),
            dma(ring),
            dma((SIDE - 1,)),
            dma((SIDE - 1,)),
            dma((6,)),
            dma((6,)),
        ]
        + gather_sems
        + [dma(ring)] * 4
        + gather_sems * 2,
        compiler_params=pltpu.CompilerParams(
            collective_id=0, has_side_effects=True, vmem_limit_bytes=46 * 1024 * 1024
        ),
        name="layer",
    )(hidden, seg, ln_attn, w_query, w_key, w_value, q_gain, k_gain, w_out, ln_mlp, w_gate, w_up, w_down)


def body(
    hidden_in,
    segment_ids,
    request_prompt,
    page_table,
    ln_attn,
    w_query,
    w_key,
    w_value,
    q_gain,
    k_gain,
    w_out,
    ln_mlp,
    w_gate,
    w_up,
    w_down,
):
    result, everything, bounds = run_layer(
        hidden_in,
        segment_ids,
        ln_attn,
        w_query,
        w_key,
        w_value,
        q_gain,
        k_gain,
        w_out,
        ln_mlp,
        w_gate,
        w_up,
        w_down,
    )
    everything = pltpu.with_memory_space_constraint(everything, pltpu.VMEM)
    cache, result = fill_pages(page_table, request_prompt, bounds, result, everything)
    return (result, cache)


def solution(mesh):
    return jax.shard_map(
        body,
        mesh=mesh,
        in_specs=(
            P(("req", "mp"), None),
            P(),
            P("req"),
            P("req", None),
            P(),
            P(None, "mp"),
            P(None, "mp"),
            P(None, "mp"),
            P(),
            P(),
            P("mp", None),
            P(),
            P(None, "mp"),
            P(None, "mp"),
            P("mp", None),
        ),
        out_specs=(P(("req", "mp"), None), P("req", None, "mp", None)),
        check_vma=False,
    )
```

```python
import math

import jax
import jax.numpy as jnp
from jax import lax
from jax.experimental import pallas as pl
from jax.experimental.pallas import tpu as pltpu
from jax.sharding import PartitionSpec as P

HD = 128
PROMPTS_DEV = 3
PAGE = 16


EPS = 1e-06
THETA = 1000000.0


def fill_kernel(
    table_hbm, prompt_hbm, bounds_ref, layer_ref, rows_ref, out_ref, layer_out, table, prompt, bounds, edges, zeros,
    small_sem, out_sem,
):
    most, requests = table.shape
    seq = rows_ref.shape[0] // bounds.shape[0]
    smalls = [
        pltpu.make_async_copy(src, dst, small_sem.at[n])
        for n, (src, dst) in enumerate(
            ((table_hbm, table), (prompt_hbm, prompt), (bounds_ref, bounds))
        )
    ]
    layer_copy = pltpu.make_async_copy(layer_ref, layer_out, small_sem.at[3])
    for small in smalls:
        small.start()
    zeros[...] = jnp.zeros_like(zeros)
    for small in smalls:
        small.wait()
    layer_copy.start()

    @pl.loop(0, requests)
    def _(r):
        p = prompt[r]
        g = p // PROMPTS_DEV
        s = p - g * PROMPTS_DEV
        low = jnp.where(s == 0, 0, jnp.where(s == 1, bounds[g, 0], bounds[g, 1]))
        high = jnp.where(s == 0, bounds[g, 0], jnp.where(s == 1, bounds[g, 1], seq))
        begin, length = g * seq + low, high - low
        full = length // PAGE
        rest = length - full * PAGE

        @pl.when(rest > 0)
        def _():
            at = begin + full * PAGE
            for o in range(PAGE):
                line = rows_ref[pl.ds(jnp.minimum(at + o, rows_ref.shape[0] - 1), 1)]
                edges[r, pl.ds(o, 1)] = jnp.where(o < rest, line, jnp.zeros_like(line))

        for e in range(most):
            page = table[e, r]

            @pl.when(e < full)
            def _():
                pltpu.make_async_copy(
                    rows_ref.at[pl.ds(begin + e * PAGE, PAGE)], out_ref.at[page], out_sem.at[0]
                ).start()

            @pl.when(e * PAGE >= length)
            def _():
                pltpu.make_async_copy(zeros, out_ref.at[page], out_sem.at[0]).start()

        @pl.when(rest > 0)
        def _():
            pltpu.make_async_copy(edges.at[r], out_ref.at[table[full, r]], out_sem.at[0]).start()

    pltpu.make_async_copy(out_ref, out_ref, out_sem.at[0]).wait()
    layer_copy.wait()


def fill_pages(page_table, request_prompt, bounds, layer, rows):
    requests, most = page_table.shape
    unit = rows.shape[1:]
    hbm = pl.BlockSpec(memory_space=pl.ANY)
    return pl.pallas_call(
        fill_kernel,
        out_shape=(
            jax.ShapeDtypeStruct((requests * most, PAGE) + unit, rows.dtype),
            jax.ShapeDtypeStruct(layer.shape, layer.dtype),
        ),
        in_specs=[hbm] * 2 + [pl.BlockSpec(memory_space=pltpu.VMEM)] * 3,
        out_specs=(hbm, hbm),
        scratch_shapes=[
            pltpu.SMEM((most, requests), jnp.int32),
            pltpu.SMEM((requests,), jnp.int32),
            pltpu.SMEM(bounds.shape, jnp.int32),
            pltpu.VMEM((requests, PAGE) + unit, rows.dtype),
            pltpu.VMEM((PAGE,) + unit, rows.dtype),
            pltpu.SemaphoreType.DMA((4,)),
            pltpu.SemaphoreType.DMA((1,)),
        ],
        compiler_params=pltpu.CompilerParams(vmem_limit_bytes=46 * 1024 * 1024),
        name="fill_pages",
    )(page_table.T, request_prompt, bounds, layer, rows)


MESH = pl.DeviceIdType.MESH
HALF = 64
SUBS = 2
SIDE = 4
PUMPS = SIDE * SIDE


def rms(wide, gain):
    return wide * lax.rsqrt(jnp.mean(wide * wide, axis=-1, keepdims=True) + EPS) * gain


def layer_kernel(
    hidden,
    seg_hbm,
    ln_attn_hbm,
    w_query,
    w_key,
    w_value,
    q_gain_hbm,
    k_gain_hbm,
    w_out,
    ln_mlp_hbm,
    w_gate,
    w_up,
    w_down,
    out,
    kv,
    bounds,
    seg,
    ln_attn,
    q_gain,
    k_gain,
    ln_mlp,
    hbuf,
    abuf,
    wq,
    wk,
    wv,
    wo,
    wg,
    wu,
    wd,
    qbuf,
    kbuf,
    vbuf,
    kvbuf,
    attbuf,
    actbuf,
    ownbuf,
    send2f,
    wfull,
    att_in,
    relay,
    send2,
    recv2,
    local_sem,
    ag1_send,
    ag1_recv,
    wx_send,
    wx_recv,
    a_send,
    a_recv,
    w_send,
    w1_recv,
    w2_recv,
    w_pair_recv,
    ag2_send,
    ag2_recv,
    rs2_send,
    rs2_recv,
    kv_send_a,
    kv1_recv_a,
    kv2_recv_a,
    kv_pair_recv_a,
    kv_send_b,
    kv1_recv_b,
    kv2_recv_b,
    kv_pair_recv_b,
):
    x = lax.axis_index("mp")
    c = lax.axis_index("req")
    core = lax.rem(c, 2)
    z = lax.rem(c // 2, SIDE)
    y = c // (2 * SIDE)
    width = hidden.shape[1]
    rows = hidden.shape[0]
    sub = HALF // SUBS

    def turn(value):
        return lax.rem(value + 2 * SIDE, SIDE)

    def req_of(yy, zz, cc):
        return (yy * SIDE + zz) * 2 + cc

    x_near = ((c, turn(x + 1)), (c, turn(x - 1)))
    pair = (req_of(y, z, 1 - core), x)
    y_near = ((req_of(turn(y + 1), z, core), x), (req_of(turn(y - 1), z, core), x))
    z_near = ((req_of(y, turn(z + 1), core), x), (req_of(y, turn(z - 1), core), x))

    moves = []
    weights = ((w_query, wq), (w_key, wk), (w_value, wv), (w_out, wo), (w_gate, wg), (w_up, wu), (w_down, wd))
    for d in range(2):
        for p in range(SUBS):
            moves.append(
                pltpu.make_async_copy(
                    hidden.at[pl.ds(d * HALF + p * sub, sub)], hbuf.at[x, d, p], local_sem.at[d * SUBS + p]
                )
            )
    for n, (src, dst) in enumerate(weights):
        moves.append(pltpu.make_async_copy(src, dst, local_sem.at[2 * SUBS + n]))
    smalls = [
        pltpu.make_async_copy(src, dst, local_sem.at[2 * SUBS + len(weights) + 1 + n])
        for n, (src, dst) in enumerate(
            ((seg_hbm, seg), (ln_attn_hbm, ln_attn), (q_gain_hbm, q_gain), (k_gain_hbm, k_gain), (ln_mlp_hbm, ln_mlp))
        )
    ]
    for move in smalls + moves:
        move.start()

    barrier = pltpu.get_barrier_semaphore()
    peers = x_near + y_near + z_near + (pair, (c, turn(x + 2)))
    for near in peers:
        pl.semaphore_signal(barrier, inc=1, device_id=near, device_id_type=MESH)
    pl.semaphore_wait(barrier, len(peers))

    def remote(src, dst, send, recv, near):
        return pltpu.make_async_remote_copy(
            src_ref=src, dst_ref=dst, send_sem=send, recv_sem=recv, device_id=near, device_id_type=MESH
        )

    def gather_step(buf, send, recv, j, d, p):
        block = buf.at[turn(x - j) if d == 0 else turn(x + j), d, p]
        return remote(block, block, send.at[j, d, p], recv.at[j, d, p], x_near[d])

    def gather_advance(buf, send, recv, j, p):
        for d in range(2):
            gather_step(buf, send, recv, j - 1, d, p).wait_recv()

            @pl.when(j < SIDE - 1)
            def _():
                gather_step(buf, send, recv, j, d, p).start()

    def ring_rows(buf, j):
        a, b = turn(x - j), turn(x + j)
        upper = buf[a, 0].reshape(HALF, width)
        lower = buf[b, 1].reshape(HALF, width)
        return jnp.concatenate([upper, lower], axis=0).astype(jnp.float32)

    deep = wfull.shape[4]

    def out_exchange(k):
        return remote(
            w_out.at[pl.ds(c * deep, deep)],
            wfull.at[k - 1, y, z, core],
            wx_send.at[k - 1],
            wx_recv.at[k - 1],
            (c, turn(x - k)),
        )

    for k in (2, 1, 3):
        out_exchange(k).start()
    for p in range(SUBS):
        for d in range(2):
            own = hidden.at[pl.ds(d * HALF + p * sub, sub)]
            remote(own, hbuf.at[x, d, p], ag1_send.at[0, d, p], ag1_recv.at[0, d, p], x_near[d]).start()

    for move in smalls:
        move.wait()

    def below(table, bound):
        return jnp.sum((table < bound).astype(jnp.int32), axis=1, keepdims=True)

    seg_row = seg[pl.ds(c, 1), :]
    first1, first2 = below(seg_row, 1), below(seg_row, 2)
    place = lax.broadcasted_iota(jnp.int32, bounds.shape, 1)
    bounds[...] = jnp.where(place == 0, below(seg[...], 1), below(seg[...], 2))

    def begin_of(token):
        return jnp.where(token >= first2, first2, jnp.where(token >= first1, first1, 0))

    lane = lax.broadcasted_iota(jnp.int32, (1, HD), 1)
    freq = jnp.exp2(lax.rem(lane, HD // 2).astype(jnp.float32) * (-2.0 * math.log2(THETA) / HD))
    sign = jnp.where(lane < HD // 2, -1.0, 1.0)
    gain_attn, gain_mlp, gain_q, gain_k = (
        gain[...].astype(jnp.float32).reshape(1, -1) for gain in (ln_attn, ln_mlp, q_gain, k_gain)
    )
    heads = wq.shape[1] // HD
    kv_heads = wk.shape[1] // HD
    group = heads // kv_heads

    flows = ((0, 0), (0, 1), (1, 0), (1, 1))

    def make_pump(block_of, send, recv1, recv2, pair_recv):
        def pump(p, own=None):
            p = jnp.int32(p)
            b, k = lax.rem(p, SIDE), p // SIDE
            for f, (axis, d) in enumerate(flows):
                step = 1 if d == 0 else -1
                first = y_near[d] if axis == 0 else z_near[d]
                second = z_near[d] if axis == 0 else y_near[d]
                if axis == 0:
                    block = block_of(f, turn(y - step * b), turn(z - step * k))
                else:
                    block = block_of(f, turn(y - step * k), turn(z - step * b))
                source = block if own is None else own(f)

                @pl.when((p >= 1) & (p < SIDE))
                def _():
                    remote(block, block, send.at[0], recv1.at[f, p - 1], first).wait_recv()

                @pl.when(p >= SIDE)
                def _():
                    remote(block, block, send.at[1], recv2.at[f, p - SIDE], second).wait_recv()

                @pl.when(p < SIDE - 1)
                def _():
                    remote(source, block, send.at[0], recv1.at[f, p], first).start()

                @pl.when(p < PUMPS - SIDE)
                def _():
                    remote(source, block, send.at[1], recv2.at[f, p], second).start()

                remote(source, block, send.at[2], pair_recv.at[0], pair).start()

        return pump

    seq = SIDE * rows
    strip = width // len(flows)

    def piece_at(j, d):
        chunk = turn(x - j) if d == 0 else turn(x + j)
        return pl.multiple_of(chunk * rows + d * HALF, HALF)

    def kv_block(stage):
        def block_of(f, oy, oz):
            return kv.at[pl.ds(req_of(oy, oz, core) * seq + piece_at(2 * stage + f // 2, f % 2), HALF)]

        return block_of

    def kv_source(stage):
        return lambda f: kvbuf.at[pl.ds(piece_at(2 * stage + f // 2, f % 2), HALF)]

    def w_block(f, oy, oz):
        return wfull.at[:, oy, oz, core, :, pl.ds(f * strip, strip)]

    pump_a = make_pump(kv_block(0), kv_send_a, kv1_recv_a, kv2_recv_a, kv_pair_recv_a)
    pump_b = make_pump(kv_block(1), kv_send_b, kv1_recv_b, kv2_recv_b, kv_pair_recv_b)
    w_pump = make_pump(w_block, w_send, w1_recv, w2_recv, w_pair_recv)

    def settle(send, pair_recv, first, second, last):
        remote(first, first, send.at[0], pair_recv.at[0], pair).wait_send()
        remote(second, second, send.at[1], pair_recv.at[0], pair).wait_send()
        remote(last, last, send.at[2], pair_recv.at[0], pair).wait_send()

    for move in moves[: 2 * SUBS + 3]:
        move.wait()

    for k in (1, 3, 2):
        out_exchange(k).wait_recv()
    w_pump(0)

    @pl.loop(0, SIDE)
    def _(j):
        @pl.when(j > 0)
        def _():
            for p in range(SUBS):
                gather_advance(hbuf, ag1_send, ag1_recv, j, p)

                @pl.when(j == 1)
                def _():
                    w_pump(1 + p)

                @pl.when(j == 2)
                def _():
                    w_pump(4 + 2 * p)
                    w_pump(5 + 2 * p)
                    if p == 1:
                        w_pump(8)

                @pl.when(j == 3)
                def _():
                    w_pump(10 + p)

        a, b = turn(x - j), turn(x + j)
        normed = rms(ring_rows(hbuf, j), gain_attn).astype(jnp.bfloat16)
        row = lax.broadcasted_iota(jnp.int32, (rows, 1), 0)
        token = jnp.where(row < HALF, a, b) * rows + row
        angle = (token - begin_of(token)).astype(jnp.float32) * freq
        cosine = jnp.cos(angle)
        sine = jnp.sin(angle) * sign

        def turned(values, gain):
            scaled = rms(values, gain)
            return (scaled * cosine + pltpu.roll(scaled, HD // 2, 1) * sine).astype(jnp.bfloat16)

        query = jnp.dot(normed, wq[...], preferred_element_type=jnp.float32)
        key = jnp.dot(normed, wk[...], preferred_element_type=jnp.float32)
        value = jnp.dot(normed, wv[...], preferred_element_type=jnp.float32).astype(jnp.bfloat16)
        for h in range(heads):
            part = turned(query[:, h * HD : (h + 1) * HD], gain_q)
            qbuf[a, 0, :, h * HD : (h + 1) * HD] = part[:HALF]
            qbuf[b, 1, :, h * HD : (h + 1) * HD] = part[HALF:]
        for h in range(kv_heads):
            part = turned(key[:, h * HD : (h + 1) * HD], gain_k)
            mine = value[:, h * HD : (h + 1) * HD]
            kbuf[a, 0, :, h * HD : (h + 1) * HD] = part[:HALF]
            kbuf[b, 1, :, h * HD : (h + 1) * HD] = part[HALF:]
            both = jnp.concatenate([part, mine], axis=1)
            kvbuf[pl.ds(a * rows, HALF), h, :] = both[:HALF]
            kvbuf[pl.ds(b * rows + HALF, HALF), h, :] = both[HALF:]
        vbuf[a, 0] = value[:HALF]
        vbuf[b, 1] = value[HALF:]

        @pl.when(j > 0)
        def _():
            w_pump(lax.select(j == 1, 3, 3 * j + 3))

        @pl.when(j == 2)
        def _():
            pump_a(0, kv_source(0))

    kv_own = pltpu.make_async_copy(kvbuf, kv.at[pl.ds(c * seq, seq)], local_sem.at[2 * SUBS + len(weights)])
    kv_own.start()

    pump_a(1)
    pump_b(0, kv_source(1))
    w_pump(13)

    def a_copy(n, src, dst, near):
        return remote(src, dst, a_send.at[n], a_recv.at[n], near)

    def head_copy(n, i=0):
        if n < 2:
            return a_copy(n, attbuf.at[i], att_in.at[2 - 2 * n], x_near[n])
        return a_copy(n, attbuf.at[i, n - 2], relay.at[n - 2], x_near[n - 2])

    relays = (
        a_copy(4, relay.at[0], att_in.at[1, 0], x_near[0]),
        a_copy(5, relay.at[1], att_in.at[1, 1], x_near[1]),
    )

    keys = kbuf[...].reshape(seq, kv_heads * HD)
    values = vbuf[...].reshape(seq, kv_heads * HD)
    for i in range(SIDE):
        extent = (i + 1) * rows
        token = lax.broadcasted_iota(jnp.int32, (rows, extent), 0) + i * rows
        other = lax.broadcasted_iota(jnp.int32, (rows, extent), 1)
        allowed = (other <= token) & (other >= begin_of(token[:, :1]))
        allowed = jnp.concatenate([allowed.astype(jnp.float32)] * group, axis=0) > 0.5
        block = qbuf[i].reshape(rows, heads * HD)
        for n in range(kv_heads):
            stacked = jnp.concatenate(
                [block[:, (n * group + h) * HD : (n * group + h + 1) * HD] for h in range(group)], axis=0
            )
            scores = lax.dot_general(
                stacked,
                keys[:extent, n * HD : (n + 1) * HD],
                (((1,), (1,)), ((), ())),
                preferred_element_type=jnp.float32,
            )
            raised = jnp.where(allowed, jnp.exp(scores * (1.0 / math.sqrt(HD))), 0.0)
            share = (raised * (1.0 / jnp.sum(raised, axis=-1, keepdims=True))).astype(jnp.bfloat16)
            mixed = jnp.dot(
                share, values[:extent, n * HD : (n + 1) * HD], preferred_element_type=jnp.float32
            ).astype(jnp.bfloat16)
            for h in range(group):
                at = (n * group + h) * HD
                attbuf[i, 0, :, at : at + HD] = mixed[h * rows : h * rows + HALF]
                attbuf[i, 1, :, at : at + HD] = mixed[h * rows + HALF : (h + 1) * rows]
        ahead = turn(i - x)

        @pl.when(ahead == 1)
        def _():
            head_copy(0, i).start()

        @pl.when(ahead == SIDE - 1)
        def _():
            head_copy(1, i).start()

        @pl.when(ahead == 2)
        def _():
            head_copy(2, i).start()
            head_copy(3, i).start()

        if i < 2:
            w_pump(14 + i)
    piece = width // SUBS

    def sum_step(send_buf, recv_buf, send, recv, j, d, n):
        return remote(send_buf.at[j, d, n], recv_buf.at[j, d, n], send.at[j, d, n], recv.at[j, d, n], x_near[d])

    def add_arrived(part, send_buf, recv_buf, send, recv, j, n):
        for d in range(2):
            sum_step(send_buf, recv_buf, send, recv, j, d, n).wait_recv()
        return part + jnp.concatenate([recv_buf[j, 0, n], recv_buf[j, 1, n]], axis=0).astype(jnp.float32)

    def send_on(part, send_buf, recv_buf, send, recv, j, n):
        rounded = part.astype(jnp.bfloat16)
        for d in range(2):
            send_buf[j, d, n] = rounded[d * HALF : (d + 1) * HALF]
            sum_step(send_buf, recv_buf, send, recv, j, d, n).start()

    ring2 = (send2, recv2, rs2_send, rs2_recv)

    def add_heads(mixed, weight, n):
        send2f[n] += jnp.dot(mixed, weight, preferred_element_type=jnp.float32)

    def add_source(k):
        mixed = att_in[k - 1].reshape(rows, att_in.shape[3])
        for n in range(SUBS):
            weight = wfull[k - 1, :, :, :, :, n * piece : (n + 1) * piece].reshape(att_in.shape[3], piece)
            add_heads(mixed, weight, n)

    moves[2 * SUBS + 3].wait()
    for n, move in enumerate(relays):
        head_copy(2 + n).wait_recv()
        move.start()
    pump_a(2)
    mixed = attbuf[x].reshape(rows, heads * HD)
    for n in range(SUBS):
        columns = slice(n * piece, (n + 1) * piece)
        before = [hbuf[x, d, :, :, columns].reshape(HALF, piece) for d in range(2)]
        send2f[n] = jnp.concatenate(before, axis=0).astype(jnp.float32)
        add_heads(mixed, wo[:, columns], n)
    pump_b(1)
    half = wfull.at[:, :, :, 0]
    remote(half, half, w_send.at[2], w_pair_recv.at[0], pair).wait_recv()
    head_copy(1).wait_recv()
    add_source(1)
    head_copy(0).wait_recv()
    add_source(3)
    for move in relays:
        move.wait_recv()
    add_source(2)
    for n in range(SUBS):
        total = send2f[n].astype(jnp.bfloat16)
        for d in range(2):
            abuf[x, d, :, :, n * piece : (n + 1) * piece] = total[d * HALF : (d + 1) * HALF].reshape(SUBS, sub, piece)
    for p in range(SUBS):
        for d in range(2):
            gather_step(abuf, ag2_send, ag2_recv, 0, d, p).start()
    for p in range(3, 7):
        pump_a(p)

    for move in moves[2 * SUBS + 4 :]:
        move.wait()

    def activation(j):
        normed = rms(ring_rows(abuf, j), gain_mlp).astype(jnp.bfloat16)
        gate = jnp.dot(normed, wg[...], preferred_element_type=jnp.float32)
        upper = jnp.dot(normed, wu[...], preferred_element_type=jnp.float32)
        return (gate * jax.nn.sigmoid(gate) * upper).astype(jnp.bfloat16)

    def down_part(act, n):
        return jnp.dot(act, wd[:, n * piece : (n + 1) * piece], preferred_element_type=jnp.float32)

    @pl.loop(0, SIDE)
    def _(j):
        @pl.when(j > 0)
        def _():
            for p in range(SUBS):
                gather_advance(abuf, ag2_send, ag2_recv, j, p)

                @pl.when(j > 1)
                def _():
                    pump_b(4 * j - 2 + p)

                if p == 0:

                    @pl.when(j == 1)
                    def _():
                        pump_a(7)

                    pump_a(4 * j + 3 + lax.select(j == 1, 1, 0))
                else:

                    @pl.when(j == 2)
                    def _():
                        pump_a(12)

        actbuf[...] = activation(j)

        @pl.when(j == 0)
        def _():
            pump_b(2)

        @pl.when(j == 1)
        def _():
            pump_b(3)
            pump_b(4)
            pump_b(5)

        @pl.when(j == 2)
        def _():
            pump_a(13)

        @pl.when(j > 1)
        def _():
            pump_b(4 * j)

        @pl.when(j > 0)
        def _():
            act = actbuf[...]
            for n in range(SUBS):
                part = down_part(act, n)
                send2f[n] = part

                @pl.when(j > 1)
                def _():
                    send2f[n] = add_arrived(send2f[n], *ring2, j - 2, n)

                send_on(send2f[n], *ring2, j - 1, n)

        @pl.when(j == 0)
        def _():
            ownbuf[...] = actbuf[...]

        @pl.when(j == 1)
        def _():
            pump_a(9)
            pump_a(10)

        @pl.when(j == 2)
        def _():
            pump_a(14)

        @pl.when(j > 1)
        def _():
            pump_b(4 * j + 1)

    act = ownbuf[...]
    pump_b(14)
    pump_b(15)
    for n in range(SUBS):
        part = add_arrived(down_part(act, n), *ring2, SIDE - 2, n)
        for d in range(2):
            before = abuf[x, d, :, :, n * piece : (n + 1) * piece].reshape(HALF, piece).astype(jnp.float32)
            total = before + part[d * HALF : (d + 1) * HALF]
            out[d * HALF : (d + 1) * HALF, n * piece : (n + 1) * piece] = total.astype(jnp.bfloat16)

    @pl.loop(0, SIDE - 1)
    def _(j):
        for d in range(2):
            for p in range(SUBS):
                gather_step(hbuf, ag1_send, ag1_recv, j, d, p).wait_send()
                gather_step(abuf, ag2_send, ag2_recv, j, d, p).wait_send()
                sum_step(*ring2, j, d, p).wait_send()

    for k in range(1, SIDE):
        out_exchange(k).wait_send()
    for n in range(4):
        head_copy(n).wait_send()
    for move in relays:
        move.wait_send()
    settle(
        w_send, w_pair_recv, wfull.at[:, 0, pl.ds(0, SIDE - 1), 0], wfull.at[:, pl.ds(0, SIDE - 1), :, 0], half
    )
    kv_own.wait()
    units = HALF * len(flows)
    got = kv.at[pl.ds(0, units * PUMPS)]
    for send, pair_recv in ((kv_send_a, kv_pair_recv_a), (kv_send_b, kv_pair_recv_b)):
        settle(send, pair_recv, kv.at[pl.ds(0, units * (SIDE - 1))], kv.at[pl.ds(0, units * (PUMPS - SIDE))], got)
        remote(got, got, send.at[2], pair_recv.at[0], pair).wait_recv()


def run_layer(hidden, seg, ln_attn, w_query, w_key, w_value, q_gain, k_gain, w_out, ln_mlp, w_gate, w_up, w_down):
    rows, width = hidden.shape
    seq = rows * SIDE
    units = w_gate.shape[1]
    kvw = w_key.shape[1]
    heads_w = w_query.shape[1]
    bf16, f32 = jnp.bfloat16, jnp.float32
    sub = HALF // SUBS
    vmem = pl.BlockSpec(memory_space=pltpu.VMEM)
    hbm = pl.BlockSpec(memory_space=pl.ANY)
    ring = (SIDE - 1, 2, SUBS)
    dma = pltpu.SemaphoreType.DMA
    gather_sems = [dma((3,)), dma((4, SIDE - 1)), dma((4, PUMPS - SIDE)), dma((1,))]
    blocks = pltpu.VMEM(ring + (HALF, width // SUBS), bf16)
    return pl.pallas_call(
        layer_kernel,
        out_shape=(
            pltpu.VMEM((rows, width), bf16),
            pltpu.VMEM((seg.shape[0] * seq, kvw // HD, 2 * HD), bf16),
            pltpu.VMEM((seg.shape[0], HD), jnp.int32),
        ),
        in_specs=[hbm] * 13,
        out_specs=(vmem, vmem, vmem),
        scratch_shapes=[
            pltpu.VMEM(seg.shape, seg.dtype),
            pltpu.VMEM(ln_attn.shape, bf16),
            pltpu.VMEM(q_gain.shape, bf16),
            pltpu.VMEM(k_gain.shape, bf16),
            pltpu.VMEM(ln_mlp.shape, bf16),
            pltpu.VMEM((SIDE, 2, SUBS, sub, width), bf16),
            pltpu.VMEM((SIDE, 2, SUBS, sub, width), bf16),
            pltpu.VMEM(w_query.shape, bf16),
            pltpu.VMEM(w_key.shape, bf16),
            pltpu.VMEM(w_value.shape, bf16),
            pltpu.VMEM(w_out.shape, bf16),
            pltpu.VMEM(w_gate.shape, bf16),
            pltpu.VMEM(w_up.shape, bf16),
            pltpu.VMEM(w_down.shape, bf16),
            pltpu.VMEM((SIDE, 2, HALF, heads_w), bf16),
            pltpu.VMEM((SIDE, 2, HALF, kvw), bf16),
            pltpu.VMEM((SIDE, 2, HALF, kvw), bf16),
            pltpu.VMEM((seq, kvw // HD, 2 * HD), bf16),
            pltpu.VMEM((SIDE, 2, HALF, heads_w), bf16),
            pltpu.VMEM((rows, units), bf16),
            pltpu.VMEM((rows, units), bf16),
            pltpu.VMEM((SUBS, rows, width // SUBS), f32),
            pltpu.VMEM((SIDE - 1, SIDE, SIDE, 2, w_out.shape[0] // seg.shape[0], width), bf16),
            pltpu.VMEM((SIDE - 1, 2, HALF, heads_w), bf16),
            pltpu.VMEM((2, HALF, heads_w), bf16),
            blocks,
            blocks,
            dma((2 * SUBS + 13,)),
            dma(ring),
            dma(ring),
            dma((SIDE - 1,)),
            dma((SIDE - 1,)),
            dma((6,)),
            dma((6,)),
        ]
        + gather_sems
        + [dma(ring)] * 4
        + gather_sems * 2,
        compiler_params=pltpu.CompilerParams(
            collective_id=0, has_side_effects=True, vmem_limit_bytes=46 * 1024 * 1024
        ),
        name="layer",
    )(hidden, seg, ln_attn, w_query, w_key, w_value, q_gain, k_gain, w_out, ln_mlp, w_gate, w_up, w_down)


def body(
    hidden_in,
    segment_ids,
    request_prompt,
    page_table,
    ln_attn,
    w_query,
    w_key,
    w_value,
    q_gain,
    k_gain,
    w_out,
    ln_mlp,
    w_gate,
    w_up,
    w_down,
):
    result, everything, bounds = run_layer(
        hidden_in,
        segment_ids,
        ln_attn,
        w_query,
        w_key,
        w_value,
        q_gain,
        k_gain,
        w_out,
        ln_mlp,
        w_gate,
        w_up,
        w_down,
    )
    result, everything, bounds = (
        pltpu.with_memory_space_constraint(array, pltpu.VMEM) for array in (result, everything, bounds)
    )
    cache, result = fill_pages(page_table, request_prompt, bounds, result, everything)
    return (result, cache)


def solution(mesh):
    return jax.shard_map(
        body,
        mesh=mesh,
        in_specs=(
            P(("req", "mp"), None),
            P(),
            P("req"),
            P("req", None),
            P(),
            P(None, "mp"),
            P(None, "mp"),
            P(None, "mp"),
            P(),
            P(),
            P("mp", None),
            P(),
            P(None, "mp"),
            P(None, "mp"),
            P("mp", None),
        ),
        out_specs=(P(("req", "mp"), None), P("req", None, "mp", None)),
        check_vma=False,
    )
```

```python
import math

import jax
import jax.numpy as jnp
from jax import lax
from jax.experimental import pallas as pl
from jax.experimental.pallas import tpu as pltpu
from jax.sharding import PartitionSpec as P

HD = 128
PROMPTS_DEV = 3
PAGE = 16


EPS = 1e-06
THETA = 1000000.0


def fill_kernel(
    table_hbm, prompt_hbm, bounds_ref, layer_ref, rows_ref, out_ref, layer_out, table, prompt, bounds, edges, zeros,
    small_sem, out_sem,
):
    most, requests = table.shape
    seq = rows_ref.shape[0] // bounds.shape[0]
    smalls = [
        pltpu.make_async_copy(src, dst, small_sem.at[n])
        for n, (src, dst) in enumerate(
            ((table_hbm, table), (prompt_hbm, prompt), (bounds_ref, bounds))
        )
    ]
    layer_copy = pltpu.make_async_copy(layer_ref, layer_out, small_sem.at[3])
    for small in smalls:
        small.start()
    zeros[...] = jnp.zeros_like(zeros)
    for small in smalls:
        small.wait()
    layer_copy.start()

    @pl.loop(0, requests)
    def _(r):
        p = prompt[r]
        g = p // PROMPTS_DEV
        s = p - g * PROMPTS_DEV
        low = jnp.where(s == 0, 0, jnp.where(s == 1, bounds[g, 0], bounds[g, 1]))
        high = jnp.where(s == 0, bounds[g, 0], jnp.where(s == 1, bounds[g, 1], seq))
        begin, length = g * seq + low, high - low
        full = length // PAGE
        rest = length - full * PAGE

        @pl.when(rest > 0)
        def _():
            at = begin + full * PAGE
            for o in range(PAGE):
                line = rows_ref[pl.ds(jnp.minimum(at + o, rows_ref.shape[0] - 1), 1)]
                edges[r, pl.ds(o, 1)] = jnp.where(o < rest, line, jnp.zeros_like(line))

        for e in range(most):
            page = table[e, r]

            @pl.when(e < full)
            def _():
                pltpu.make_async_copy(
                    rows_ref.at[pl.ds(begin + e * PAGE, PAGE)], out_ref.at[page], out_sem.at[0]
                ).start()

            @pl.when(e * PAGE >= length)
            def _():
                pltpu.make_async_copy(zeros, out_ref.at[page], out_sem.at[0]).start()

        @pl.when(rest > 0)
        def _():
            pltpu.make_async_copy(edges.at[r], out_ref.at[table[full, r]], out_sem.at[0]).start()

    pltpu.make_async_copy(out_ref, out_ref, out_sem.at[0]).wait()
    layer_copy.wait()


def fill_pages(page_table, request_prompt, bounds, layer, rows):
    requests, most = page_table.shape
    unit = rows.shape[1:]
    hbm = pl.BlockSpec(memory_space=pl.ANY)
    return pl.pallas_call(
        fill_kernel,
        out_shape=(
            jax.ShapeDtypeStruct((requests * most, PAGE) + unit, rows.dtype),
            jax.ShapeDtypeStruct(layer.shape, layer.dtype),
        ),
        in_specs=[hbm] * 2 + [pl.BlockSpec(memory_space=pltpu.VMEM)] * 3,
        out_specs=(hbm, hbm),
        scratch_shapes=[
            pltpu.SMEM((most, requests), jnp.int32),
            pltpu.SMEM((requests,), jnp.int32),
            pltpu.SMEM(bounds.shape, jnp.int32),
            pltpu.VMEM((requests, PAGE) + unit, rows.dtype),
            pltpu.VMEM((PAGE,) + unit, rows.dtype),
            pltpu.SemaphoreType.DMA((4,)),
            pltpu.SemaphoreType.DMA((1,)),
        ],
        compiler_params=pltpu.CompilerParams(vmem_limit_bytes=46 * 1024 * 1024),
        name="fill_pages",
    )(page_table.T, request_prompt, bounds, layer, rows)


MESH = pl.DeviceIdType.MESH
HALF = 64
SUBS = 2
SIDE = 4
PUMPS = SIDE * SIDE


def rms(wide, gain):
    return wide * lax.rsqrt(jnp.mean(wide * wide, axis=-1, keepdims=True) + EPS) * gain


def layer_kernel(
    hidden,
    seg_hbm,
    ln_attn_hbm,
    w_query,
    w_key,
    w_value,
    q_gain_hbm,
    k_gain_hbm,
    w_out,
    ln_mlp_hbm,
    w_gate,
    w_up,
    w_down,
    out,
    kv,
    bounds,
    seg,
    ln_attn,
    q_gain,
    k_gain,
    ln_mlp,
    hbuf,
    abuf,
    wq,
    wk,
    wv,
    wo,
    wg,
    wu,
    wd,
    qbuf,
    kbuf,
    vbuf,
    kvbuf,
    attbuf,
    actbuf,
    ownbuf,
    send2f,
    wfull,
    att_in,
    relay,
    send2,
    recv2,
    local_sem,
    ag1_send,
    ag1_recv,
    wx_send,
    wx_recv,
    a_send,
    a_recv,
    w_send,
    w1_recv,
    w2_recv,
    w_pair_recv,
    ag2_send,
    ag2_recv,
    rs2_send,
    rs2_recv,
    kv_send_a,
    kv1_recv_a,
    kv2_recv_a,
    kv_pair_recv_a,
    kv_send_b,
    kv1_recv_b,
    kv2_recv_b,
    kv_pair_recv_b,
):
    x = lax.axis_index("mp")
    c = lax.axis_index("req")
    core = lax.rem(c, 2)
    z = lax.rem(c // 2, SIDE)
    y = c // (2 * SIDE)
    width = hidden.shape[1]
    rows = hidden.shape[0]
    sub = HALF // SUBS

    def turn(value):
        return lax.rem(value + 2 * SIDE, SIDE)

    def req_of(yy, zz, cc):
        return (yy * SIDE + zz) * 2 + cc

    x_near = ((c, turn(x + 1)), (c, turn(x - 1)))
    pair = (req_of(y, z, 1 - core), x)
    y_near = ((req_of(turn(y + 1), z, core), x), (req_of(turn(y - 1), z, core), x))
    z_near = ((req_of(y, turn(z + 1), core), x), (req_of(y, turn(z - 1), core), x))

    moves = []
    weights = ((w_query, wq), (w_key, wk), (w_value, wv), (w_out, wo), (w_gate, wg), (w_up, wu), (w_down, wd))
    for d in range(2):
        for p in range(SUBS):
            moves.append(
                pltpu.make_async_copy(
                    hidden.at[pl.ds(d * HALF + p * sub, sub)], hbuf.at[x, d, p], local_sem.at[d * SUBS + p]
                )
            )
    for n, (src, dst) in enumerate(weights):
        moves.append(pltpu.make_async_copy(src, dst, local_sem.at[2 * SUBS + n]))
    smalls = [
        pltpu.make_async_copy(src, dst, local_sem.at[2 * SUBS + len(weights) + 1 + n])
        for n, (src, dst) in enumerate(
            ((seg_hbm, seg), (ln_attn_hbm, ln_attn), (q_gain_hbm, q_gain), (k_gain_hbm, k_gain), (ln_mlp_hbm, ln_mlp))
        )
    ]
    for move in smalls + moves:
        move.start()

    barrier = pltpu.get_barrier_semaphore()
    peers = x_near + y_near + z_near + (pair, (c, turn(x + 2)))
    for near in peers:
        pl.semaphore_signal(barrier, inc=1, device_id=near, device_id_type=MESH)
    pl.semaphore_wait(barrier, len(peers))

    def remote(src, dst, send, recv, near):
        return pltpu.make_async_remote_copy(
            src_ref=src, dst_ref=dst, send_sem=send, recv_sem=recv, device_id=near, device_id_type=MESH
        )

    def gather_step(buf, send, recv, j, d, p):
        block = buf.at[turn(x - j) if d == 0 else turn(x + j), d, p]
        return remote(block, block, send.at[j, d, p], recv.at[j, d, p], x_near[d])

    def gather_advance(buf, send, recv, j, p):
        for d in range(2):
            gather_step(buf, send, recv, j - 1, d, p).wait_recv()

            @pl.when(j < SIDE - 1)
            def _():
                gather_step(buf, send, recv, j, d, p).start()

    def ring_rows(buf, j):
        a, b = turn(x - j), turn(x + j)
        upper = buf[a, 0].reshape(HALF, width)
        lower = buf[b, 1].reshape(HALF, width)
        return jnp.concatenate([upper, lower], axis=0).astype(jnp.float32)

    deep = wfull.shape[4]

    def out_exchange(k):
        return remote(
            w_out.at[pl.ds(c * deep, deep)],
            wfull.at[k - 1, y, z, core],
            wx_send.at[k - 1],
            wx_recv.at[k - 1],
            (c, turn(x - k)),
        )

    for k in (2, 1, 3):
        out_exchange(k).start()
    for p in range(SUBS):
        for d in range(2):
            own = hidden.at[pl.ds(d * HALF + p * sub, sub)]
            remote(own, hbuf.at[x, d, p], ag1_send.at[0, d, p], ag1_recv.at[0, d, p], x_near[d]).start()

    for move in smalls:
        move.wait()

    def below(table, bound):
        return jnp.sum((table < bound).astype(jnp.int32), axis=1, keepdims=True)

    seg_row = seg[pl.ds(c, 1), :]
    first1, first2 = below(seg_row, 1), below(seg_row, 2)
    place = lax.broadcasted_iota(jnp.int32, bounds.shape, 1)
    bounds[...] = jnp.where(place == 0, below(seg[...], 1), below(seg[...], 2))

    def begin_of(token):
        return jnp.where(token >= first2, first2, jnp.where(token >= first1, first1, 0))

    lane = lax.broadcasted_iota(jnp.int32, (1, HD), 1)
    freq = jnp.exp2(lax.rem(lane, HD // 2).astype(jnp.float32) * (-2.0 * math.log2(THETA) / HD))
    sign = jnp.where(lane < HD // 2, -1.0, 1.0)
    gain_attn, gain_mlp, gain_q, gain_k = (
        gain[...].astype(jnp.float32).reshape(1, -1) for gain in (ln_attn, ln_mlp, q_gain, k_gain)
    )
    heads = wq.shape[1] // HD
    kv_heads = wk.shape[1] // HD
    group = heads // kv_heads

    flows = ((0, 0), (0, 1), (1, 0), (1, 1))

    def make_pump(block_of, send, recv1, recv2, pair_recv):
        def pump(p, own=None):
            p = jnp.int32(p)
            b, k = lax.rem(p, SIDE), p // SIDE
            for f, (axis, d) in enumerate(flows):
                step = 1 if d == 0 else -1
                first = y_near[d] if axis == 0 else z_near[d]
                second = z_near[d] if axis == 0 else y_near[d]
                if axis == 0:
                    block = block_of(f, turn(y - step * b), turn(z - step * k))
                else:
                    block = block_of(f, turn(y - step * k), turn(z - step * b))
                source = block if own is None else own(f)

                @pl.when((p >= 1) & (p < SIDE))
                def _():
                    remote(block, block, send.at[0], recv1.at[f, p - 1], first).wait_recv()

                @pl.when(p >= SIDE)
                def _():
                    remote(block, block, send.at[1], recv2.at[f, p - SIDE], second).wait_recv()

                @pl.when(p < SIDE - 1)
                def _():
                    remote(source, block, send.at[0], recv1.at[f, p], first).start()

                @pl.when(p < PUMPS - SIDE)
                def _():
                    remote(source, block, send.at[1], recv2.at[f, p], second).start()

                remote(source, block, send.at[2], pair_recv.at[0], pair).start()

        return pump

    seq = SIDE * rows
    strip = width // len(flows)

    def piece_at(j, d):
        chunk = turn(x - j) if d == 0 else turn(x + j)
        return pl.multiple_of(chunk * rows + d * HALF, HALF)

    def kv_block(stage):
        def block_of(f, oy, oz):
            return kv.at[pl.ds(req_of(oy, oz, core) * seq + piece_at(2 * stage + f // 2, f % 2), HALF)]

        return block_of

    def kv_source(stage):
        return lambda f: kvbuf.at[pl.ds(piece_at(2 * stage + f // 2, f % 2), HALF)]

    def w_block(f, oy, oz):
        return wfull.at[:, oy, oz, core, :, pl.ds(f * strip, strip)]

    pump_a = make_pump(kv_block(0), kv_send_a, kv1_recv_a, kv2_recv_a, kv_pair_recv_a)
    pump_b = make_pump(kv_block(1), kv_send_b, kv1_recv_b, kv2_recv_b, kv_pair_recv_b)
    w_pump = make_pump(w_block, w_send, w1_recv, w2_recv, w_pair_recv)

    def settle(send, pair_recv, first, second, last):
        remote(first, first, send.at[0], pair_recv.at[0], pair).wait_send()
        remote(second, second, send.at[1], pair_recv.at[0], pair).wait_send()
        remote(last, last, send.at[2], pair_recv.at[0], pair).wait_send()

    for move in moves[: 2 * SUBS + 3]:
        move.wait()

    for k in (1, 3, 2):
        out_exchange(k).wait_recv()
    w_pump(0)

    @pl.loop(0, SIDE)
    def _(j):
        @pl.when(j > 0)
        def _():
            for p in range(SUBS):
                gather_advance(hbuf, ag1_send, ag1_recv, j, p)

                @pl.when(j == 1)
                def _():
                    w_pump(1 + p)

                @pl.when(j == 2)
                def _():
                    w_pump(4 + 2 * p)
                    w_pump(5 + 2 * p)
                    if p == 1:
                        w_pump(8)

                @pl.when(j == 3)
                def _():
                    w_pump(10 + p)

        a, b = turn(x - j), turn(x + j)
        normed = rms(ring_rows(hbuf, j), gain_attn).astype(jnp.bfloat16)
        row = lax.broadcasted_iota(jnp.int32, (rows, 1), 0)
        token = jnp.where(row < HALF, a, b) * rows + row
        angle = (token - begin_of(token)).astype(jnp.float32) * freq
        cosine = jnp.cos(angle)
        sine = jnp.sin(angle) * sign

        def turned(values, gain):
            scaled = rms(values, gain)
            return (scaled * cosine + pltpu.roll(scaled, HD // 2, 1) * sine).astype(jnp.bfloat16)

        query = jnp.dot(normed, wq[...], preferred_element_type=jnp.float32)
        key = jnp.dot(normed, wk[...], preferred_element_type=jnp.float32)
        value = jnp.dot(normed, wv[...], preferred_element_type=jnp.float32).astype(jnp.bfloat16)
        for h in range(heads):
            part = turned(query[:, h * HD : (h + 1) * HD], gain_q)
            qbuf[a, 0, :, h * HD : (h + 1) * HD] = part[:HALF]
            qbuf[b, 1, :, h * HD : (h + 1) * HD] = part[HALF:]
        for h in range(kv_heads):
            part = turned(key[:, h * HD : (h + 1) * HD], gain_k)
            mine = value[:, h * HD : (h + 1) * HD]
            kbuf[a, 0, :, h * HD : (h + 1) * HD] = part[:HALF]
            kbuf[b, 1, :, h * HD : (h + 1) * HD] = part[HALF:]
            both = jnp.concatenate([part, mine], axis=1)
            kvbuf[pl.ds(a * rows, HALF), h, :] = both[:HALF]
            kvbuf[pl.ds(b * rows + HALF, HALF), h, :] = both[HALF:]
        vbuf[a, 0] = value[:HALF]
        vbuf[b, 1] = value[HALF:]

        @pl.when(j > 0)
        def _():
            w_pump(lax.select(j == 1, 3, 3 * j + 3))

        @pl.when(j == 2)
        def _():
            pump_a(0, kv_source(0))

    kv_own = pltpu.make_async_copy(kvbuf, kv.at[pl.ds(c * seq, seq)], local_sem.at[2 * SUBS + len(weights)])
    kv_own.start()

    pump_a(1)
    pump_b(0, kv_source(1))
    w_pump(13)

    def a_copy(n, src, dst, near):
        return remote(src, dst, a_send.at[n], a_recv.at[n], near)

    def head_copy(n, i=0):
        if n < 2:
            return a_copy(n, attbuf.at[i], att_in.at[2 - 2 * n], x_near[n])
        return a_copy(n, attbuf.at[i, n - 2], relay.at[n - 2], x_near[n - 2])

    relays = (
        a_copy(4, relay.at[0], att_in.at[1, 0], x_near[0]),
        a_copy(5, relay.at[1], att_in.at[1, 1], x_near[1]),
    )

    keys = kbuf[...].reshape(seq, kv_heads * HD)
    values = vbuf[...].reshape(seq, kv_heads * HD)
    for i in range(SIDE):
        extent = (i + 1) * rows
        token = lax.broadcasted_iota(jnp.int32, (rows, extent), 0) + i * rows
        other = lax.broadcasted_iota(jnp.int32, (rows, extent), 1)
        allowed = (other <= token) & (other >= begin_of(token[:, :1]))
        allowed = jnp.concatenate([allowed.astype(jnp.float32)] * group, axis=0) > 0.5
        block = qbuf[i].reshape(rows, heads * HD)
        for n in range(kv_heads):
            stacked = jnp.concatenate(
                [block[:, (n * group + h) * HD : (n * group + h + 1) * HD] for h in range(group)], axis=0
            )
            scores = lax.dot_general(
                stacked,
                keys[:extent, n * HD : (n + 1) * HD],
                (((1,), (1,)), ((), ())),
                preferred_element_type=jnp.float32,
            )
            raised = jnp.where(allowed, jnp.exp(scores * (1.0 / math.sqrt(HD))), 0.0)
            share = (raised * (1.0 / jnp.sum(raised, axis=-1, keepdims=True))).astype(jnp.bfloat16)
            mixed = jnp.dot(
                share, values[:extent, n * HD : (n + 1) * HD], preferred_element_type=jnp.float32
            ).astype(jnp.bfloat16)
            for h in range(group):
                at = (n * group + h) * HD
                attbuf[i, 0, :, at : at + HD] = mixed[h * rows : h * rows + HALF]
                attbuf[i, 1, :, at : at + HD] = mixed[h * rows + HALF : (h + 1) * rows]
        ahead = turn(i - x)

        @pl.when(ahead == 1)
        def _():
            head_copy(0, i).start()

        @pl.when(ahead == SIDE - 1)
        def _():
            head_copy(1, i).start()

        @pl.when(ahead == 2)
        def _():
            head_copy(2, i).start()
            head_copy(3, i).start()

        if i < 2:
            w_pump(14 + i)
    piece = width // SUBS

    def sum_step(send_buf, recv_buf, send, recv, j, d, n):
        return remote(send_buf.at[j, d, n], recv_buf.at[j, d, n], send.at[j, d, n], recv.at[j, d, n], x_near[d])

    def add_arrived(part, send_buf, recv_buf, send, recv, j, n):
        for d in range(2):
            sum_step(send_buf, recv_buf, send, recv, j, d, n).wait_recv()
        return part + jnp.concatenate([recv_buf[j, 0, n], recv_buf[j, 1, n]], axis=0).astype(jnp.float32)

    def send_on(part, send_buf, recv_buf, send, recv, j, n):
        rounded = part.astype(jnp.bfloat16)
        for d in range(2):
            send_buf[j, d, n] = rounded[d * HALF : (d + 1) * HALF]
            sum_step(send_buf, recv_buf, send, recv, j, d, n).start()

    ring2 = (send2, recv2, rs2_send, rs2_recv)

    def add_heads(mixed, weight, n):
        send2f[n] += jnp.dot(mixed, weight, preferred_element_type=jnp.float32)

    def add_source(k):
        mixed = att_in[k - 1].reshape(rows, att_in.shape[3])
        for n in range(SUBS):
            weight = wfull[k - 1, :, :, :, :, n * piece : (n + 1) * piece].reshape(att_in.shape[3], piece)
            add_heads(mixed, weight, n)

    moves[2 * SUBS + 3].wait()
    for n, move in enumerate(relays):
        head_copy(2 + n).wait_recv()
        move.start()
    pump_a(2)
    mixed = attbuf[x].reshape(rows, heads * HD)
    for n in range(SUBS):
        columns = slice(n * piece, (n + 1) * piece)
        before = [hbuf[x, d, :, :, columns].reshape(HALF, piece) for d in range(2)]
        send2f[n] = jnp.concatenate(before, axis=0).astype(jnp.float32)
        add_heads(mixed, wo[:, columns], n)
    pump_b(1)
    half = wfull.at[:, :, :, 0]
    remote(half, half, w_send.at[2], w_pair_recv.at[0], pair).wait_recv()
    head_copy(1).wait_recv()
    add_source(1)
    head_copy(0).wait_recv()
    add_source(3)
    for move in relays:
        move.wait_recv()
    add_source(2)
    for n in range(SUBS):
        total = send2f[n].astype(jnp.bfloat16)
        for d in range(2):
            abuf[x, d, :, :, n * piece : (n + 1) * piece] = total[d * HALF : (d + 1) * HALF].reshape(SUBS, sub, piece)
    for p in range(SUBS):
        for d in range(2):
            gather_step(abuf, ag2_send, ag2_recv, 0, d, p).start()
    for p in range(3, 7):
        pump_a(p)

    for move in moves[2 * SUBS + 4 :]:
        move.wait()

    def activation(j):
        normed = rms(ring_rows(abuf, j), gain_mlp).astype(jnp.bfloat16)
        gate = jnp.dot(normed, wg[...], preferred_element_type=jnp.float32)
        upper = jnp.dot(normed, wu[...], preferred_element_type=jnp.float32)
        return (gate * jax.nn.sigmoid(gate) * upper).astype(jnp.bfloat16)

    def down_part(act, n):
        return jnp.dot(act, wd[:, n * piece : (n + 1) * piece], preferred_element_type=jnp.float32)

    @pl.loop(0, SIDE)
    def _(j):
        @pl.when(j > 0)
        def _():
            for p in range(SUBS):
                gather_advance(abuf, ag2_send, ag2_recv, j, p)

                @pl.when(j > 1)
                def _():
                    pump_b(4 * j - 2 + p)

                if p == 0:

                    @pl.when(j == 1)
                    def _():
                        pump_a(7)

                    pump_a(4 * j + 3 + lax.select(j == 1, 1, 0))
                else:

                    @pl.when(j == 2)
                    def _():
                        pump_a(12)

        actbuf[...] = activation(j)

        @pl.when(j == 0)
        def _():
            pump_b(2)

        @pl.when(j == 1)
        def _():
            pump_b(3)
            pump_b(4)
            pump_b(5)

        @pl.when(j == 2)
        def _():
            pump_a(13)

        @pl.when(j > 1)
        def _():
            pump_b(4 * j)

        @pl.when(j > 0)
        def _():
            act = actbuf[...]
            for n in range(SUBS):
                part = down_part(act, n)
                send2f[n] = part

                @pl.when(j > 1)
                def _():
                    send2f[n] = add_arrived(send2f[n], *ring2, j - 2, n)

                send_on(send2f[n], *ring2, j - 1, n)

        @pl.when(j == 0)
        def _():
            ownbuf[...] = actbuf[...]

        @pl.when(j == 1)
        def _():
            pump_a(9)
            pump_a(10)

        @pl.when(j == 2)
        def _():
            pump_a(14)

        @pl.when(j > 1)
        def _():
            pump_b(4 * j + 1)

    act = ownbuf[...]
    for n in range(SUBS):
        send2f[n] = down_part(act, n)
    pump_b(14)
    pump_b(15)
    for n in range(SUBS):
        part = add_arrived(send2f[n], *ring2, SIDE - 2, n)
        for d in range(2):
            before = abuf[x, d, :, :, n * piece : (n + 1) * piece].reshape(HALF, piece).astype(jnp.float32)
            total = before + part[d * HALF : (d + 1) * HALF]
            out[d * HALF : (d + 1) * HALF, n * piece : (n + 1) * piece] = total.astype(jnp.bfloat16)

    @pl.loop(0, SIDE - 1)
    def _(j):
        for d in range(2):
            for p in range(SUBS):
                gather_step(hbuf, ag1_send, ag1_recv, j, d, p).wait_send()
                gather_step(abuf, ag2_send, ag2_recv, j, d, p).wait_send()
                sum_step(*ring2, j, d, p).wait_send()

    for k in range(1, SIDE):
        out_exchange(k).wait_send()
    for n in range(4):
        head_copy(n).wait_send()
    for move in relays:
        move.wait_send()
    settle(
        w_send, w_pair_recv, wfull.at[:, 0, pl.ds(0, SIDE - 1), 0], wfull.at[:, pl.ds(0, SIDE - 1), :, 0], half
    )
    kv_own.wait()
    units = HALF * len(flows)
    got = kv.at[pl.ds(0, units * PUMPS)]
    for send, pair_recv in ((kv_send_a, kv_pair_recv_a), (kv_send_b, kv_pair_recv_b)):
        settle(send, pair_recv, kv.at[pl.ds(0, units * (SIDE - 1))], kv.at[pl.ds(0, units * (PUMPS - SIDE))], got)
        remote(got, got, send.at[2], pair_recv.at[0], pair).wait_recv()


def run_layer(hidden, seg, ln_attn, w_query, w_key, w_value, q_gain, k_gain, w_out, ln_mlp, w_gate, w_up, w_down):
    rows, width = hidden.shape
    seq = rows * SIDE
    units = w_gate.shape[1]
    kvw = w_key.shape[1]
    heads_w = w_query.shape[1]
    bf16, f32 = jnp.bfloat16, jnp.float32
    sub = HALF // SUBS
    vmem = pl.BlockSpec(memory_space=pltpu.VMEM)
    hbm = pl.BlockSpec(memory_space=pl.ANY)
    ring = (SIDE - 1, 2, SUBS)
    dma = pltpu.SemaphoreType.DMA
    gather_sems = [dma((3,)), dma((4, SIDE - 1)), dma((4, PUMPS - SIDE)), dma((1,))]
    blocks = pltpu.VMEM(ring + (HALF, width // SUBS), bf16)
    return pl.pallas_call(
        layer_kernel,
        out_shape=(
            pltpu.VMEM((rows, width), bf16),
            pltpu.VMEM((seg.shape[0] * seq, kvw // HD, 2 * HD), bf16),
            pltpu.VMEM((seg.shape[0], HD), jnp.int32),
        ),
        in_specs=[hbm] * 13,
        out_specs=(vmem, vmem, vmem),
        scratch_shapes=[
            pltpu.VMEM(seg.shape, seg.dtype),
            pltpu.VMEM(ln_attn.shape, bf16),
            pltpu.VMEM(q_gain.shape, bf16),
            pltpu.VMEM(k_gain.shape, bf16),
            pltpu.VMEM(ln_mlp.shape, bf16),
            pltpu.VMEM((SIDE, 2, SUBS, sub, width), bf16),
            pltpu.VMEM((SIDE, 2, SUBS, sub, width), bf16),
            pltpu.VMEM(w_query.shape, bf16),
            pltpu.VMEM(w_key.shape, bf16),
            pltpu.VMEM(w_value.shape, bf16),
            pltpu.VMEM(w_out.shape, bf16),
            pltpu.VMEM(w_gate.shape, bf16),
            pltpu.VMEM(w_up.shape, bf16),
            pltpu.VMEM(w_down.shape, bf16),
            pltpu.VMEM((SIDE, 2, HALF, heads_w), bf16),
            pltpu.VMEM((SIDE, 2, HALF, kvw), bf16),
            pltpu.VMEM((SIDE, 2, HALF, kvw), bf16),
            pltpu.VMEM((seq, kvw // HD, 2 * HD), bf16),
            pltpu.VMEM((SIDE, 2, HALF, heads_w), bf16),
            pltpu.VMEM((rows, units), bf16),
            pltpu.VMEM((rows, units), bf16),
            pltpu.VMEM((SUBS, rows, width // SUBS), f32),
            pltpu.VMEM((SIDE - 1, SIDE, SIDE, 2, w_out.shape[0] // seg.shape[0], width), bf16),
            pltpu.VMEM((SIDE - 1, 2, HALF, heads_w), bf16),
            pltpu.VMEM((2, HALF, heads_w), bf16),
            blocks,
            blocks,
            dma((2 * SUBS + 13,)),
            dma(ring),
            dma(ring),
            dma((SIDE - 1,)),
            dma((SIDE - 1,)),
            dma((6,)),
            dma((6,)),
        ]
        + gather_sems
        + [dma(ring)] * 4
        + gather_sems * 2,
        compiler_params=pltpu.CompilerParams(
            collective_id=0, has_side_effects=True, vmem_limit_bytes=46 * 1024 * 1024
        ),
        name="layer",
    )(hidden, seg, ln_attn, w_query, w_key, w_value, q_gain, k_gain, w_out, ln_mlp, w_gate, w_up, w_down)


def body(
    hidden_in,
    segment_ids,
    request_prompt,
    page_table,
    ln_attn,
    w_query,
    w_key,
    w_value,
    q_gain,
    k_gain,
    w_out,
    ln_mlp,
    w_gate,
    w_up,
    w_down,
):
    result, everything, bounds = run_layer(
        hidden_in,
        segment_ids,
        ln_attn,
        w_query,
        w_key,
        w_value,
        q_gain,
        k_gain,
        w_out,
        ln_mlp,
        w_gate,
        w_up,
        w_down,
    )
    result, everything, bounds = (
        pltpu.with_memory_space_constraint(array, pltpu.VMEM) for array in (result, everything, bounds)
    )
    cache, result = fill_pages(page_table, request_prompt, bounds, result, everything)
    return (result, cache)


def solution(mesh):
    return jax.shard_map(
        body,
        mesh=mesh,
        in_specs=(
            P(("req", "mp"), None),
            P(),
            P("req"),
            P("req", None),
            P(),
            P(None, "mp"),
            P(None, "mp"),
            P(None, "mp"),
            P(),
            P(),
            P("mp", None),
            P(),
            P(None, "mp"),
            P(None, "mp"),
            P("mp", None),
        ),
        out_specs=(P(("req", "mp"), None), P("req", None, "mp", None)),
        check_vma=False,
    )
```
